32 devices in a mesh: row: 16 (over z, y, x), col: 2 (over core).
Axes of the slice: x: 2, y: 2, z: 4, core: 2. Of those that a mesh axis runs over, the one named last changes fastest.
Arguments:
- image_embeddings: bfloat16 [128, 64, 1024], P('row', 'col'), may hold values from -6 to 6
- lagged_blend_ratios: float32 [3, 1024], replicated, may hold values from 0.05 to 0.95
- linear_map_coefficients: bfloat16 [3, 1024, 1024], P(None, 'row'), may hold values from -0.1875 to 0.1875
- retention_exponent: float32 [16, 128, 64], P(None, 'row', 'col'), may hold values from -3 to 0, as said below
- self_credit: float32 [1024], replicated, may hold values from 1 to 8
- channel_scale_vector: float32 [1024], replicated, may hold values from 0.5 to 2
- pooling_scale_vector: float32 [4096], replicated, may hold values from 0.5 to 2
- pooling_offset_vector: float32 [4096], replicated, may hold values from -3 to 3
Outputs:
- merged: bfloat16 [64, 32, 4096], P('row', 'col')
The draws below stay inside these ranges and needn't reach their ends.
Inputs may be any that keep to these rules, and one draw needn't show every extreme that they name: `retention_exponent`: the logarithm of the share of a head's state kept at each patch.
All inputs are finite; a program needn't handle non-finite values.
Results may differ from the reference program's by a relative error of at most 0.0057.
Values may be sent and summed in bfloat16 or wider, within the bound.
A program may use at most 192 MiB of HBM per device.

```python
import math
import jax
import jax.numpy as jnp
from jax import lax

EMBEDDING_SIZE = 1024
HEAD_COUNT = 16
HEAD = 64
R_DEV = 8
STRIP_COLUMNS = 32
PATCH_ROWS = 128
PATCH_COLUMNS = 64
N_ROW = 16
N_COL = 2


def draw_retention_exponent(key, part):
    direction_flows = jax.random.split(jax.random.fold_in(key, 11), 9)
    chain_length = PATCH_ROWS * STRIP_COLUMNS
    block_length = R_DEV * STRIP_COLUMNS
    row_blocks = PATCH_ROWS // R_DEV
    column_block_count = PATCH_COLUMNS // STRIP_COLUMNS
    fast_heads = max(1, HEAD_COUNT * 3 // 16)
    middle_heads = max(1, HEAD_COUNT * 5 // 16)
    ranking = jax.random.permutation(direction_flows[0], HEAD_COUNT)
    is_fast = ranking < fast_heads
    is_middle = (ranking >= fast_heads) & (ranking < fast_heads + middle_heads)
    fast_rate = 2.3 / 40.0 * jnp.exp(jax.random.uniform(direction_flows[1], (HEAD_COUNT,), minval=-0.3, maxval=0.3))
    slow_rate = 0.35 / chain_length * jnp.exp(jax.random.uniform(direction_flows[2], (HEAD_COUNT,), minval=-0.7, maxval=0.7))
    middle_rate = 1.0 / block_length * jnp.exp(jax.random.uniform(direction_flows[8], (HEAD_COUNT,), minval=-0.5, maxval=0.5))
    base_rate = jnp.where(is_fast, fast_rate, jnp.where(is_middle, middle_rate, slow_rate))
    token_factor = jnp.exp(jax.random.uniform(direction_flows[3], (HEAD_COUNT, PATCH_ROWS, PATCH_COLUMNS), minval=-0.7, maxval=0.7))
    block_factor = jnp.exp(jax.random.uniform(direction_flows[4], (HEAD_COUNT, row_blocks, 1, column_block_count, 1), minval=-0.7, maxval=0.7))
    block_factor = jnp.broadcast_to(block_factor, (HEAD_COUNT, row_blocks, R_DEV, column_block_count, STRIP_COLUMNS)).reshape(HEAD_COUNT, PATCH_ROWS, PATCH_COLUMNS)
    decay_rates = -base_rate[:, None, None] * token_factor * block_factor
    span_rows = jax.random.randint(direction_flows[5], (3, HEAD_COUNT, 1, column_block_count, 1), 0, PATCH_ROWS)
    span_columns = jax.random.randint(direction_flows[6], (3, HEAD_COUNT, 1, column_block_count, 1), 0, STRIP_COLUMNS)
    span_length = jnp.log(jax.random.uniform(direction_flows[7], (3, HEAD_COUNT, 1, column_block_count, 1), minval=0.5, maxval=0.8))
    row_position = jnp.arange(PATCH_ROWS).reshape(1, PATCH_ROWS, 1, 1)
    column_position = jnp.arange(STRIP_COLUMNS).reshape(1, 1, 1, STRIP_COLUMNS)
    for group_span in range(3):
        matched_mask = (row_position == span_rows[group_span]) & (column_position == span_columns[group_span])
        decay_rates = decay_rates + jnp.where(matched_mask, span_length[group_span], 0.0).reshape(HEAD_COUNT, PATCH_ROWS, PATCH_COLUMNS)
    return decay_rates.astype(jnp.float32)


def block_levels(rng, shape, pieces, least, high):
    def one(dim, parts):
        heights = jax.random.uniform(jax.random.fold_in(jax.random.fold_in(rng, 6), dim), (parts,), jnp.float32, least / len(pieces), high / len(pieces))
        return jnp.repeat(jnp.exp(heights), shape[dim] // parts).reshape((-1,) + (1,) * (len(shape) - dim - 1))

    factor_of = one(*pieces[0])
    for cut in pieces[1:]:
        factor_of = factor_of * one(*cut)
    return factor_of


def bell_draw(key, dims, scale, reach, pieces=(), kind=jnp.bfloat16):
    entries = scale * jax.random.normal(key, dims, jnp.float32)
    if pieces:
        entries = entries * block_levels(key, dims, pieces, -0.22, 0.18)
    return jnp.clip(entries, -reach, reach).astype(kind)


def setup_inputs(seed: int = 0) -> dict:
    streams_of = jax.random.split(jax.random.key(seed), 9)
    return {
        "image_embeddings": bell_draw(streams_of[0], (PATCH_ROWS, PATCH_COLUMNS, EMBEDDING_SIZE), 1.0, 6.0, ((0, 16), (1, 2))),
        "lagged_blend_ratios": jnp.clip(jax.random.uniform(streams_of[1], (3, EMBEDDING_SIZE), jnp.float32, 0.05, 0.95), 0.05, 0.95),
        "linear_map_coefficients": bell_draw(streams_of[2], (3, EMBEDDING_SIZE, EMBEDDING_SIZE), EMBEDDING_SIZE ** -0.5, 0.1875, ((1, 16),)),
        "retention_exponent": draw_retention_exponent(jax.random.fold_in(streams_of[8], 71), 0),
        "self_credit": jnp.clip(jnp.exp(jax.random.uniform(streams_of[4], (EMBEDDING_SIZE,), jnp.float32, math.log(1.0), math.log(8.0))), 1.0, 8.0),
        "channel_scale_vector": jnp.clip(jnp.exp(jax.random.uniform(streams_of[5], (EMBEDDING_SIZE,), jnp.float32, math.log(0.5), math.log(2.0))), 0.5, 2.0),
        "pooling_scale_vector": jnp.clip(jnp.exp(jax.random.uniform(streams_of[6], (4 * EMBEDDING_SIZE,), jnp.float32, math.log(0.5), math.log(2.0))), 0.5, 2.0),
        "pooling_offset_vector": bell_draw(streams_of[7], (4 * EMBEDDING_SIZE,), 0.5, 3.0, (), jnp.float32),
    }


PRECISE = lax.Precision.HIGHEST

def head_mix(argument_tensors):
    query_head, key_head, value_head, running, before = argument_tensors
    count = query_head.shape[0]
    position = jnp.arange(count, dtype=jnp.int32)
    earlier_mask = position[:, None] > position[None, :]
    diagonal = position[:, None] == position[None, :]
    scores = jnp.dot(query_head, key_head.T, preferred_element_type=jnp.float32)
    exponent = jnp.where(earlier_mask, before[:, None] - running[None, :], before[None, :] - running[:, None])
    weights = jnp.where(diagonal, jnp.float32(0.0), jnp.exp(exponent))
    pair_weight = (scores * weights).astype(jnp.bfloat16)
    return jnp.dot(pair_weight, value_head, preferred_element_type=jnp.float32)

def block_states(argument_tensors):
    address_vectors, content_vectors, retention_ratio = argument_tensors
    count, width = address_vectors.shape
    attention_units = retention_ratio.shape[0]
    unit_dimension = width // attention_units
    running = jnp.cumsum(retention_ratio, axis=1)
    before = running - retention_ratio
    total = running[:, -1:]
    unitwise_addresses = address_vectors.astype(jnp.float32).reshape(count, attention_units, unit_dimension)
    unitwise_contents = content_vectors.astype(jnp.float32).reshape(count, attention_units, unit_dimension)
    forward_state = jnp.einsum('thd,the->hde', unitwise_addresses * jnp.exp(total - running).T[:, :, None], unitwise_contents, precision=PRECISE)
    backward_state = jnp.einsum('thd,the->hde', unitwise_addresses * jnp.exp(before).T[:, :, None], unitwise_contents, precision=PRECISE)
    return (jnp.exp(total[:, 0]), forward_state, backward_state)

def segment_routine(argument_tensors):
    content_vectors_full, acceptance_vectors, address_vectors, content_vectors, retention_ratio, ordered_sequence, reversed_sequence, self_credit, channel_scale_vector = argument_tensors
    count, width = acceptance_vectors.shape
    attention_units = retention_ratio.shape[0]
    unit_dimension = width // attention_units
    running = jnp.cumsum(retention_ratio, axis=1)
    before = running - retention_ratio
    total = running[:, -1:]

    def per_head(matrix):
        return matrix.reshape(count, attention_units, unit_dimension).transpose(1, 0, 2)
    local = lax.map(head_mix, (per_head(acceptance_vectors), per_head(address_vectors), per_head(content_vectors), running, before))
    unitwise_probes = acceptance_vectors.astype(jnp.float32).reshape(count, attention_units, unit_dimension)
    unitwise_addresses = address_vectors.astype(jnp.float32).reshape(count, attention_units, unit_dimension)
    unitwise_contents = content_vectors.astype(jnp.float32).reshape(count, attention_units, unit_dimension)
    carried = jnp.exp(before).T[:, :, None] * jnp.einsum('thd,hde->the', unitwise_probes, ordered_sequence, precision=PRECISE)
    carried = carried + jnp.exp(total - running).T[:, :, None] * jnp.einsum('thd,hde->the', unitwise_probes, reversed_sequence, precision=PRECISE)
    principal_summand = lax.optimization_barrier(jnp.sum(unitwise_probes * self_credit.reshape(attention_units, unit_dimension) * unitwise_addresses, axis=2, keepdims=True)) * unitwise_contents
    wkv_out = local.transpose(1, 0, 2) + carried + principal_summand
    centred = wkv_out - lax.optimization_barrier(jnp.mean(wkv_out, axis=2, keepdims=True))
    variance = lax.optimization_barrier(jnp.mean(centred * centred, axis=2, keepdims=True))
    normed = centred * lax.rsqrt(variance + 1e-05) * channel_scale_vector.reshape(attention_units, unit_dimension)
    return (content_vectors_full.reshape(count, attention_units, unit_dimension) + normed).reshape(count, width)

def merge_tiles(block_out, pooling_scale_vector, pooling_offset_vector):
    tile_rows, tile_cols, width = block_out.shape
    grouped = block_out.reshape(tile_rows // 2, 2, tile_cols // 2, 2, width).transpose(0, 2, 3, 1, 4)
    grouped = grouped.reshape(tile_rows // 2, tile_cols // 2, 4 * width)
    merge_centred = grouped - lax.optimization_barrier(jnp.mean(grouped, axis=2, keepdims=True))
    variance = lax.optimization_barrier(jnp.mean(merge_centred * merge_centred, axis=2, keepdims=True))
    return (merge_centred * lax.rsqrt(variance + 1e-05) * pooling_scale_vector + pooling_offset_vector).astype(jnp.bfloat16)

def reference(image_embeddings, lagged_blend_ratios, linear_map_coefficients, retention_exponent, self_credit, channel_scale_vector, pooling_scale_vector, pooling_offset_vector):
    quarter = EMBEDDING_SIZE // 4
    quadrant_piece = R_DEV * STRIP_COLUMNS
    padded = jnp.pad(image_embeddings, ((1, 1), (1, 1), (0, 0)))

    def one_strip(strip):
        first = (strip * STRIP_COLUMNS).astype(jnp.int32)
        window = lax.dynamic_slice_in_dim(padded, first, STRIP_COLUMNS + 2, 1)
        centre = window[1:-1, 1:-1]
        shifted = jnp.concatenate([window[1:-1, :-2, :quarter], window[1:-1, 2:, quarter:2 * quarter], window[:-2, 1:-1, 2 * quarter:3 * quarter], window[2:, 1:-1, 3 * quarter:]], axis=2)
        content_vectors_full = centre.astype(jnp.float32)
        shifted_float = shifted.astype(jnp.float32)
        mapped_embeddings = []
        for index in range(3):
            mixed = (content_vectors_full * lagged_blend_ratios[index] + shifted_float * (1.0 - lagged_blend_ratios[index])).astype(jnp.bfloat16)
            product = jnp.dot(mixed.reshape(PATCH_ROWS * STRIP_COLUMNS, EMBEDDING_SIZE), linear_map_coefficients[index], preferred_element_type=jnp.float32)
            mapped_embeddings.append(product.astype(jnp.bfloat16).reshape(N_ROW, quadrant_piece, EMBEDDING_SIZE))
        retention_ratio = lax.dynamic_slice_in_dim(retention_exponent, first, STRIP_COLUMNS, 2).reshape(HEAD_COUNT, N_ROW, quadrant_piece).transpose(1, 0, 2)
        kept, forward_state, backward_state = lax.map(block_states, (mapped_embeddings[1], mapped_embeddings[2], retention_ratio))

        def carry_step(state, item):
            return (item[0][:, None, None] * state + item[1], state)
        start_state = jnp.zeros((HEAD_COUNT, HEAD, HEAD), jnp.float32)
        ordered_sequence = lax.scan(carry_step, start_state, (kept, forward_state))[1]
        reversed_sequence = lax.scan(carry_step, start_state, (kept, backward_state), reverse=True)[1]
        self_credit_table = jnp.broadcast_to(self_credit, (N_ROW, EMBEDDING_SIZE))
        scaling_table = jnp.broadcast_to(channel_scale_vector, (N_ROW, EMBEDDING_SIZE))
        result_tensors = lax.map(segment_routine, (content_vectors_full.reshape(N_ROW, quadrant_piece, EMBEDDING_SIZE), mapped_embeddings[0], mapped_embeddings[1], mapped_embeddings[2], retention_ratio, ordered_sequence, reversed_sequence, self_credit_table, scaling_table))
        return merge_tiles(result_tensors.reshape(PATCH_ROWS, STRIP_COLUMNS, EMBEDDING_SIZE), pooling_scale_vector, pooling_offset_vector)
    merged = lax.map(one_strip, jnp.arange(N_COL, dtype=jnp.int32))
    return merged.transpose(1, 0, 2, 3).reshape(PATCH_ROWS // 2, PATCH_COLUMNS // 2, 4 * EMBEDDING_SIZE)
```

```python
import functools

import jax
import jax.numpy as jnp
from jax import lax
from jax.experimental import pallas as pl
from jax.experimental.pallas import tpu as pltpu
from jax.sharding import PartitionSpec as P

MESH = pl.DeviceIdType.MESH
F32 = jnp.float32
BF16 = jnp.bfloat16
HIGH = lax.Precision.HIGHEST
PLANE = 4
SPLIT = 2
CHUNKS = ((1, 0), (2, 0), (1, 1), (2, 1), (0, 0), (0, 1))


def iota(shape, dim):
    return lax.broadcasted_iota(jnp.int32, shape, dim)


def two_terms(value):
    first = value.astype(BF16)
    return first, (value - first.astype(F32)).astype(BF16)


def kernel(
    rows, cols, tile_rows, tile_cols, heads,
    x_ref, ratio_ref, w_ref, ret_ref, credit_ref, gain_ref, scale_ref, offset_ref,
    out_ref,
    xv, wf, mx, proj, decay, halo_side, halo_row, rows_t, spread_t, mine, totals, kept_all, states, arrived,
    scan_f, scan_b, leaving, entering, block, stats,
    x_sem, own_sem, w_send, m_send, z_recv, f_recv, s_recv, m_recv, halo_send, halo_recv,
    t_send, t_recv, a_send, a_recv, b_send, b_recv,
):
    count, width = xv.shape
    hd = width // heads
    pairs = heads // 2
    lanes = 2 * hd
    quarter = width // 4
    share = w_ref.shape[1]
    half_w = width // 2
    cw = half_w // SPLIT
    unit = states.shape[2]
    per = hd // unit
    group_pairs = pairs // SPLIT
    side_pairs = group_pairs // 2
    row, col = lax.axis_index("row"), lax.axis_index("col")
    depth = rows // PLANE
    z, q = row // PLANE, row % PLANE
    bx, by = q % 2, q // 2
    half = col % 2
    mate = col + 1 - 2 * half
    q1 = (1 - half) * (q + 1 - 2 * bx) + half * (q + 2 - 4 * by)
    q2 = half * (q + 1 - 2 * bx) + (1 - half) * (q + 2 - 4 * by)
    q12 = PLANE - 1 - q
    first_row, second_row = z * PLANE + q1, z * PLANE + q2
    right, left = (col + 1) % cols, (col + cols - 1) % cols
    down_row, up_row = (row + 1) % rows, (row + rows - 1) % rows
    has_next, has_previous = row < rows - 1, row > 0

    barrier = pltpu.get_barrier_semaphore()

    def greet(target):
        pl.semaphore_signal(barrier, inc=1, device_id=target, device_id_type=MESH)

    for o in range(1, depth):
        greet({"row": (z + o) % depth * PLANE + q})
    greet({"row": first_row})
    greet({"row": second_row})
    for other in (right, left, mate):
        greet({"col": other})
    for there, target in ((has_next, down_row), (has_previous, up_row)):
        @pl.when(there)
        def _():
            greet({"row": target})

    x_copy = pltpu.make_async_copy(x_ref, xv, x_sem)
    x_copy.start()

    ret = jnp.concatenate([ret_ref[:, r, :] for r in range(tile_rows)], axis=1)
    tri = (iota((count, count), 0) >= iota((count, count), 1)).astype(F32)
    contract_last = (((1,), (1,)), ((), ()))
    running_c = lax.dot_general(tri, ret, contract_last, precision=HIGH, preferred_element_type=F32)
    running_r = lax.dot_general(ret, tri, contract_last, precision=HIGH, preferred_element_type=F32)
    eye = (iota((count, count), 0) == iota((count, count), 1)).astype(F32)
    ret_c = lax.dot_general(eye, ret, contract_last, precision=HIGH, preferred_element_type=F32)

    pl.semaphore_wait(
        barrier, depth - 1 + 5 + has_next.astype(jnp.int32) + has_previous.astype(jnp.int32))

    halos = [
        pltpu.make_async_remote_copy(
            x_ref.at[:, 0:quarter], halo_side.at[0], halo_send.at[0], halo_recv.at[0],
            device_id={"col": right}, device_id_type=MESH),
        pltpu.make_async_remote_copy(
            x_ref.at[:, quarter:2 * quarter], halo_side.at[1], halo_send.at[1], halo_recv.at[1],
            device_id={"col": left}, device_id_type=MESH),
        pltpu.make_async_remote_copy(
            x_ref.at[count - tile_cols:count, 2 * quarter:3 * quarter], halo_row.at[0],
            halo_send.at[2], halo_recv.at[2], device_id={"row": down_row}, device_id_type=MESH),
        pltpu.make_async_remote_copy(
            x_ref.at[0:tile_cols, 3 * quarter:], halo_row.at[1],
            halo_send.at[3], halo_recv.at[3], device_id={"row": up_row}, device_id_type=MESH),
    ]

    def share_of(c):
        p, part = CHUNKS[c]
        return w_ref.at[p, :, pl.ds(pl.multiple_of(half * half_w + part * cw, cw), cw)]

    def send(c, source, zz, qq, recv, to):
        pltpu.make_async_remote_copy(
            source, wf.at[c, half, zz, qq], w_send.at[c], recv,
            device_id={"row": to}, device_id_type=MESH).start()

    def arrive(ref, recv):
        pltpu.make_async_remote_copy(
            ref, ref, m_send.at[0], recv, device_id={"col": mate}, device_id_type=MESH).wait_recv()

    def left_by(ref, sem):
        pltpu.make_async_remote_copy(
            ref, ref, sem, m_recv.at[0], device_id={"col": mate}, device_id_type=MESH).wait_send()

    def own_copy(c):
        return pltpu.make_async_copy(share_of(c), wf.at[c, half, z, q], own_sem.at[c])

    def own(c):
        for o in range(1, depth):
            send(c, share_of(c), z, q, z_recv.at[c, z], (z + o) % depth * PLANE + q)
        send(c, share_of(c), z, q, s_recv.at[c, 0], second_row)
        send(c, share_of(c), z, q, f_recv.at[c, z], first_row)
        own_copy(c).start()

    def to_mate(c, qq):
        ref = wf.at[c, half, :, qq]
        pltpu.make_async_remote_copy(
            ref, ref, m_send.at[c], m_recv.at[c], device_id={"col": mate}, device_id_type=MESH).start()

    def near(c):
        here = wf.at[c, half, z, q1]
        arrive(here, f_recv.at[c, z])
        send(c, here, z, q1, s_recv.at[c, 1], second_row)

    def planes(c):
        for o in range(1, depth):
            zz = (z + o) % depth
            here = wf.at[c, half, zz, q]
            arrive(here, z_recv.at[c, zz])
            send(c, here, zz, q, s_recv.at[c, 0], second_row)
            send(c, here, zz, q, f_recv.at[c, zz], first_row)
        own_copy(c).wait()
        to_mate(c, q)

    def firsts(c):
        for o in range(1, depth):
            zz = (z + o) % depth
            here = wf.at[c, half, zz, q1]
            arrive(here, f_recv.at[c, zz])
            send(c, here, zz, q1, s_recv.at[c, 1], second_row)
        to_mate(c, q1)

    def seconds(c):
        arrive(wf.at[c, half, :, q2], s_recv.at[c, 0])
        to_mate(c, q2)
        arrive(wf.at[c, half, :, q12], s_recv.at[c, 1])
        to_mate(c, q12)

    def from_mate(c):
        arrive(wf.at[c, 1 - half], m_recv.at[c])

    own(0)
    halos[0].start()
    halos[1].start()

    @pl.when(has_next)
    def _():
        halos[2].start()

    @pl.when(has_previous)
    def _():
        halos[3].start()

    own(1)
    own(2)

    before_c = running_c - ret_c
    before_r = running_r - ret
    total_r = running_c[count - 1:count, :]
    rows_t[0] = running_c
    rows_t[1] = before_c
    chosen = (iota((heads, width), 0) == iota((heads, width), 1) // hd).astype(F32)
    for k, table in enumerate((jnp.exp(total_r - running_c), jnp.exp(before_c))):
        spread_t[k] = jnp.dot(table, chosen, precision=HIGH, preferred_element_type=F32)
    mine[...] = jnp.broadcast_to(
        jnp.concatenate([total_r, jnp.zeros((1, 128 - heads), F32)], axis=1), (8, 128))
    totals[row] = mine[...]

    def picked(table, h):
        return jnp.sum(jnp.where(iota(table.shape, 1) == h, table, 0.0), axis=1, keepdims=True)

    def picked_row(table, h):
        return jnp.sum(jnp.where(iota(table.shape, 0) == h, table, 0.0), axis=0, keepdims=True)

    earlier = iota((count, count), 0) > iota((count, count), 1)
    diagonal = iota((count, count), 0) == iota((count, count), 1)

    def decays(h, carry):
        rc, bc = picked(rows_t[0], h), picked(rows_t[1], h)
        rr, br = picked_row(running_r, h), picked_row(before_r, h)
        exponent = jnp.where(earlier, bc - rr, br - rc)
        decay[h] = jnp.where(diagonal, 0.0, jnp.exp(exponent))
        return carry

    def some_decays(part):
        lax.fori_loop(part * heads // 4, (part + 1) * heads // 4, decays, 0)

    def mix_inputs():
        halos[0].wait()
        halos[1].wait()

        @pl.when(has_next)
        def _():
            halos[2].wait_send()
            halos[3].wait_recv()

        @pl.when(has_previous)
        def _():
            halos[3].wait_send()
            halos[2].wait_recv()

        token = iota((count, quarter), 0)
        place_in_row = token % tile_cols
        x0 = xv[:, 0:quarter].astype(F32)
        x1 = xv[:, quarter:2 * quarter].astype(F32)
        side0 = jnp.where(col > 0, halo_side[0].astype(F32), 0.0)
        side1 = jnp.where(col < cols - 1, halo_side[1].astype(F32), 0.0)
        top = jnp.where(row > 0, halo_row[0].astype(F32), 0.0)
        bottom = jnp.where(row < rows - 1, halo_row[1].astype(F32), 0.0)
        last = tile_cols - 1
        shifted = [
            jnp.where(place_in_row == 0, pltpu.roll(side0, count - last, 0), pltpu.roll(x0, 1, 0)),
            jnp.where(place_in_row == last, pltpu.roll(side1, last, 0), pltpu.roll(x1, count - 1, 0)),
            jnp.concatenate([top, xv[0:count - tile_cols, 2 * quarter:3 * quarter].astype(F32)], axis=0),
            jnp.concatenate([xv[tile_cols:count, 3 * quarter:].astype(F32), bottom], axis=0),
        ]
        for part in range(4):
            span = slice(part * quarter, (part + 1) * quarter)
            xs = xv[:, span].astype(F32)
            for p in range(3):
                c = ratio_ref[p:p + 1, span]
                mx[p, :, span] = (xs * c + shifted[part] * (1.0 - c)).astype(BF16)

    def project(c):
        p, part = CHUNKS[c]

        def one(side, carry):
            dst = pl.ds(pl.multiple_of(side * half_w + part * cw, cw), cw)
            proj[p, :, dst] = jnp.dot(
                mx[p], wf[c, side].reshape(width, cw), preferred_element_type=F32).astype(BF16)
            return carry

        lax.fori_loop(0, 2, one, 0)

    lane = iota((count, lanes), 1)
    low = lane < hd
    low_u = iota((hd, lanes), 1) < hd
    same_head = (iota((2 * lanes, lanes), 0) % lanes // hd == iota((2 * lanes, lanes), 1) // hd).astype(BF16)

    def halves(value):
        return jnp.dot(jnp.concatenate(two_terms(value), axis=1), same_head, preferred_element_type=F32)

    def pair_of(u, j):
        return j // side_pairs * (pairs // 2) + u * side_pairs + j % side_pairs

    def span_of(i):
        return pl.ds(pl.multiple_of(i * lanes, lanes), lanes)

    def local_states(u):
        def one(j, carry):
            span = span_of(pair_of(u, j))
            k = proj[1, :, span].astype(F32)
            v = proj[2, :, span]
            kd = jnp.concatenate([k * spread_t[0, :, span], k * spread_t[1, :, span]], axis=1).astype(BF16)
            m = lax.dot_general(kd, v, (((0,), (0,)), ((), ())), preferred_element_type=F32)
            a = jnp.where(low_u, m[0:hd], pltpu.roll(m[2 * hd:3 * hd], hd, 1))
            b = jnp.where(low_u, pltpu.roll(m[hd:2 * hd], hd, 1), m[3 * hd:])
            for s in range(per):
                states[u, 2 * j * per + s] = a[s * unit:(s + 1) * unit].astype(BF16)
                states[u, (2 * j + 1) * per + s] = b[s * unit:(s + 1) * unit].astype(BF16)
            return carry

        lax.fori_loop(0, group_pairs, one, 0)

    def to_all(copy):
        def one(o, carry):
            copy((row + o) % rows).start()
            return carry

        lax.fori_loop(1, rows, one, 0)

    def totals_out():
        to_all(lambda to: pltpu.make_async_remote_copy(
            mine, totals.at[row], t_send, t_recv, device_id={"row": to}, device_id_type=MESH))

    def states_out(u):
        to_all(lambda to: pltpu.make_async_remote_copy(
            states.at[u, to], arrived.at[u, row], a_send.at[u], a_recv.at[u],
            device_id={"row": to}, device_id_type=MESH))
        arrived[u, row] = states[u, row]

    def totals_in():
        arrive(totals.at[0:rows - 1], t_recv)
        everyone = totals[...]
        for u in range(SPLIT):
            local = row * unit // hd
            head = 2 * pair_of(u, local // 2) + local % 2
            here = iota(everyone.shape, 2) == head
            kept_all[u] = jnp.broadcast_to(
                jnp.exp(jnp.sum(jnp.where(here, everyone, 0.0), axis=2, keepdims=True)), everyone.shape)

    def scan(u):
        arrive(arrived.at[u, 0:rows - 1], a_recv.at[u])

        def one(j, carry):
            ahead, behind = carry
            back = rows - 1 - j
            scan_f[j] = ahead
            scan_b[back] = behind
            ahead = kept_all[u, j][0:1, :] * ahead + arrived[u, j].astype(F32)
            behind = kept_all[u, back][0:1, :] * behind + arrived[u, back].astype(F32)
            return ahead, behind

        start = jnp.zeros((unit, lanes), F32)
        lax.fori_loop(0, rows, one, (start, start), unroll=4)
        leaving[u] = jnp.where(iota(scan_f.shape, 2) < hd, scan_f[...], scan_b[...]).astype(BF16)
        to_all(lambda to: pltpu.make_async_remote_copy(
            leaving.at[u, to], entering.at[u, row], b_send.at[u], b_recv.at[u],
            device_id={"row": to}, device_id_type=MESH))
        entering[u, row] = leaving[u, row]

    def local_mix(u):
        def one(j, carry):
            i = pair_of(u, j)
            span = span_of(i)
            r, k, v = proj[0, :, span], proj[1, :, span], proj[2, :, span]
            outs = []
            for s in range(2):
                rs = jnp.where(low if s == 0 else jnp.logical_not(low), r.astype(F32), 0.0).astype(BF16)
                scores = lax.dot_general(rs, k, contract_last, preferred_element_type=F32)
                weight = (scores * decay[2 * i + s]).astype(BF16)
                outs.append(jnp.dot(weight, v, preferred_element_type=F32))
            own_term = halves(r.astype(F32) * credit_ref[:, span] * k.astype(F32)) * v.astype(F32)
            block[i] = jnp.where(low, outs[0], outs[1]) + own_term
            return carry

        lax.fori_loop(0, group_pairs, one, 0)

    def finish(u, total):
        arrive(entering.at[u, 0:rows - 1], b_recv.at[u])

        def one(j, total):
            i = pair_of(u, j)
            span = span_of(i)
            r = proj[0, :, span]
            a = jnp.concatenate([entering[u, 2 * j * per + s].astype(F32) for s in range(per)], axis=0)
            b = jnp.concatenate([entering[u, (2 * j + 1) * per + s].astype(F32) for s in range(per)], axis=0)
            fwd = jnp.concatenate(
                [jnp.where(low_u, a, 0.0), jnp.where(low_u, 0.0, pltpu.roll(b, hd, 1))], axis=0).astype(BF16)
            bwd = jnp.concatenate(
                [jnp.where(low_u, pltpu.roll(a, hd, 1), 0.0), jnp.where(low_u, 0.0, b)], axis=0).astype(BF16)
            wkv = (
                block[i]
                + spread_t[1, :, span] * jnp.dot(r, fwd, preferred_element_type=F32)
                + spread_t[0, :, span] * jnp.dot(r, bwd, preferred_element_type=F32)
            )
            centred = wkv - halves(wkv) * (1.0 / hd)
            variance = halves(centred * centred) * (1.0 / hd)
            made = xv[:, span].astype(F32) + centred * lax.rsqrt(variance + 1e-05) * gain_ref[:, span]
            block[i] = made
            return total + made

        return lax.fori_loop(0, group_pairs, one, total)

    near(0)
    planes(0)
    x_copy.wait()
    mix_inputs()
    own(3)
    near(1)
    planes(1)
    firsts(0)
    some_decays(0)
    some_decays(1)
    own(4)
    near(2)
    planes(2)
    firsts(1)
    seconds(0)
    totals_out()
    some_decays(2)
    some_decays(3)
    own(5)
    near(3)
    planes(3)
    firsts(2)
    seconds(1)
    from_mate(0)
    project(0)
    totals_in()
    near(4)
    planes(4)
    firsts(3)
    from_mate(1)
    project(1)
    local_states(0)
    states_out(0)
    seconds(2)
    near(5)
    planes(5)
    firsts(4)
    seconds(3)
    from_mate(2)
    project(2)
    scan(0)
    firsts(5)
    from_mate(3)
    project(3)
    local_states(1)
    states_out(1)
    seconds(4)
    from_mate(4)
    project(4)
    local_mix(0)
    scan(1)
    seconds(5)
    total = finish(0, jnp.zeros((count, lanes), F32))
    from_mate(5)
    project(5)
    local_mix(1)
    total = finish(1, total)

    group = (
        (iota((count, count), 0) // (2 * tile_cols) == iota((count, count), 1) // (2 * tile_cols))
        & (iota((count, count), 0) % tile_cols // 2 == iota((count, count), 1) % tile_cols // 2)
    ).astype(BF16)

    def over_group(value):
        rowsum = jnp.broadcast_to(jnp.sum(value, axis=1, keepdims=True), (count, lanes))
        both = jnp.dot(group, jnp.concatenate(two_terms(rowsum), axis=1), preferred_element_type=F32)
        return (both[:, 0:lanes] + both[:, lanes:]) * (1.0 / (4 * width))

    mean = over_group(total)

    def spread(i, acc):
        dev = block[i] - mean
        return acc + dev * dev

    variance = over_group(lax.fori_loop(0, pairs, spread, jnp.zeros((count, lanes), F32)))
    stats[0] = mean
    stats[1] = lax.rsqrt(variance + 1e-05)
    half_cols = tile_cols // 2

    def emit(i, carry):
        for part in range(4):
            span = pl.ds(pl.multiple_of(part * width + i * lanes, lanes), lanes)
            g, o = scale_ref[:, span], offset_ref[:, span]
            for a in range(tile_rows // 2):
                take = pl.ds((2 * a + part % 2) * tile_cols + part // 2, half_cols, stride=2)
                value = (block[i, take, :] - stats[0, take, :]) * stats[1, take, :]
                out_ref[a, :, span] = (value * g + o).astype(BF16)
        return carry

    lax.fori_loop(0, pairs, emit, 0)

    left_by(totals.at[0:rows - 1], t_send)
    for u in range(SPLIT):
        left_by(states.at[u, 0:rows - 1], a_send.at[u])
        left_by(leaving.at[u, 0:rows - 1], b_send.at[u])
    for c in range(len(CHUNKS)):
        left_by(wf.at[c, half], m_send.at[c])
        left_by(wf.at[c, half, 0:depth - 1], w_send.at[c])
        left_by(wf.at[c, half, 0, 0:PLANE - 1], w_send.at[c])


def body(x, ratios, w, retention, credit, gain, scale, offset):
    tile_rows, tile_cols, width = x.shape
    heads = retention.shape[0]
    count = tile_rows * tile_cols
    hd = width // heads
    rows, cols = lax.axis_size("row"), lax.axis_size("col")
    depth = rows // PLANE
    unit = heads * hd // rows // SPLIT
    pairs = heads // 2
    lanes = 2 * hd
    chunks = len(CHUNKS)
    dma = pltpu.SemaphoreType.DMA
    anywhere, vmem = pl.BlockSpec(memory_space=pl.ANY), pl.BlockSpec(memory_space=pltpu.VMEM)
    return pl.pallas_call(
        functools.partial(kernel, rows, cols, tile_rows, tile_cols, heads),
        out_shape=jax.ShapeDtypeStruct((tile_rows // 2, tile_cols // 2, 4 * width), BF16),
        in_specs=[anywhere, vmem, anywhere, vmem, vmem, vmem, vmem, vmem],
        out_specs=vmem,
        scratch_shapes=[
            pltpu.VMEM((count, width), BF16),
            pltpu.VMEM((chunks, 2, depth, PLANE, w.shape[1], width // 2 // SPLIT), BF16),
            pltpu.VMEM((3, count, width), BF16),
            pltpu.VMEM((3, count, width), BF16),
            pltpu.VMEM((heads, count, count), F32),
            pltpu.VMEM((2, count, width // 4), BF16),
            pltpu.VMEM((2, tile_cols, width // 4), BF16),
            pltpu.VMEM((2, count, heads), F32),
            pltpu.VMEM((2, count, width), F32),
            pltpu.VMEM((8, 128), F32),
            pltpu.VMEM((rows, 8, 128), F32),
            pltpu.VMEM((SPLIT, rows, 8, 128), F32),
            pltpu.VMEM((SPLIT, rows, unit, lanes), BF16),
            pltpu.VMEM((SPLIT, rows, unit, lanes), BF16),
            pltpu.VMEM((rows, unit, lanes), F32),
            pltpu.VMEM((rows, unit, lanes), F32),
            pltpu.VMEM((SPLIT, rows, unit, lanes), BF16),
            pltpu.VMEM((SPLIT, rows, unit, lanes), BF16),
            pltpu.VMEM((pairs, count, lanes), F32),
            pltpu.VMEM((2, count, lanes), F32),
            dma,
            dma((chunks,)),
            dma((chunks,)),
            dma((chunks,)),
            dma((chunks, depth)),
            dma((chunks, depth)),
            dma((chunks, 2)),
            dma((chunks,)),
            dma((4,)),
            dma((4,)),
            dma,
            dma,
            dma((SPLIT,)),
            dma((SPLIT,)),
            dma((SPLIT,)),
            dma((SPLIT,)),
        ],
        compiler_params=pltpu.CompilerParams(
            collective_id=0, has_side_effects=True, vmem_limit_bytes=60 * 1024 * 1024),
    )(
        x.reshape(count, width), ratios, w, retention,
        credit.reshape(1, width), gain.reshape(1, width),
        scale.reshape(1, 4 * width), offset.reshape(1, 4 * width),
    )


def solution(mesh):
    return jax.shard_map(
        body,
        mesh=mesh,
        in_specs=(
            P("row", "col", None),
            P(),
            P(None, "row", None),
            P(None, "row", "col"),
            P(),
            P(),
            P(),
            P(),
        ),
        out_specs=P("row", "col", None),
        check_vma=False,
    )
```

```python
import functools

import jax
import jax.numpy as jnp
from jax import lax
from jax.experimental import pallas as pl
from jax.experimental.pallas import tpu as pltpu
from jax.sharding import PartitionSpec as P

MESH = pl.DeviceIdType.MESH
F32 = jnp.float32
BF16 = jnp.bfloat16
HIGH = lax.Precision.HIGHEST
PLANE = 4
PIECES = 4
KV, R = slice(1, 3), slice(0, 1)


def iota(shape, dim):
    return lax.broadcasted_iota(jnp.int32, shape, dim)


def two_terms(value):
    first = value.astype(BF16)
    return first, (value - first.astype(F32)).astype(BF16)


def kernel(
    rows, cols, tile_rows, tile_cols, heads,
    x_ref, ratio_ref, w_ref, ret_ref, credit_ref, gain_ref, scale_ref, offset_ref,
    out_ref,
    xt, wf, mx, proj, decay, side, top_rows, bottom_rows, rets, rows_t, rows_r, spread_t, log_t, plane_log, plane_logs,
    sums, before, decays_t, plane_sum, plane_sums, entering, block, sent, landed, stats,
    x_own, x_send, x_piece, x_near, x_far, w_own, w_send, w_plane, w_z, w_mate, side_send, side_recv, edge_own,
    edge_send, edge_recv, ret_send, ret_recv, log_send, log_recv, sum_send, sum_recv, out_send, out_recv,
):
    count, width = xt.shape[1:]
    hd = width // heads
    lanes = 2 * hd
    quarter = width // 4
    gw = width // PLANE
    gp = gw // lanes
    hp = heads // PLANE
    vp_count = PLANE * gp
    hs = w_ref.shape[1] // 2
    piece = count // PIECES
    row, col = lax.axis_index("row"), lax.axis_index("col")
    depth = rows // PLANE
    z, q = row // PLANE, row % PLANE
    bx, by = q % 2, q // 2
    half = col % 2
    mate = col + 1 - 2 * half
    q1 = (1 - half) * (q + 1 - 2 * bx) + half * (q + 2 - 4 * by)
    q2 = half * (q + 1 - 2 * bx) + (1 - half) * (q + 2 - 4 * by)
    q12 = PLANE - 1 - q
    base = z * PLANE
    first_row, second_row = base + q1, base + q2
    right, left = (col + 1) % cols, (col + cols - 1) % cols
    sends_down = (q < PLANE - 1) | (z < depth - 1)
    sends_up = (q > 0) | (z > 0)
    down_plane = jnp.where(q < PLANE - 1, z, (z + 1) % depth)
    up_plane = jnp.where(q > 0, z, (z + depth - 1) % depth)
    down_slot, up_slot = (q + 1) % PLANE, (q + PLANE - 1) % PLANE

    barrier = pltpu.get_barrier_semaphore()

    def greet(target):
        pl.semaphore_signal(barrier, inc=1, device_id=target, device_id_type=MESH)

    for o in range(1, depth):
        greet({"row": (z + o) % depth * PLANE + q})
    for o in range(1, PLANE):
        greet({"row": base + (q + o) % PLANE})
    for other in (right, left, mate):
        greet({"col": other})

    @pl.when(z > 0)
    def _():
        greet({"row": (base + rows - 1) % rows})

    @pl.when(z < depth - 1)
    def _():
        greet({"row": (base + PLANE) % rows})

    def local(src, dst, sem):
        return pltpu.make_async_copy(src, dst, sem)

    def remote(src, dst, send, recv, target):
        return pltpu.make_async_remote_copy(
            src, dst, send, recv, device_id=target, device_id_type=MESH)

    def arrive(ref, recv):
        remote(ref, ref, x_send, recv, {"col": mate}).wait_recv()

    def left_by(ref, send):
        remote(ref, ref, send, x_near, {"col": mate}).wait_send()

    my_rows = pl.ds(pl.multiple_of(half * hs, hs), hs)

    def my_cols(qq):
        return pl.ds(pl.multiple_of(qq * gw, gw), gw)

    x_copy = local(x_ref, xt.at[q], x_own)
    w_copy = local(w_ref.at[:, my_rows, my_cols(q)], wf.at[:, z, q, half], w_own)
    w_copy.start()
    x_copy.start()
    top_source = x_ref.at[count - tile_cols:count, 2 * quarter:3 * quarter]
    bottom_source = x_ref.at[0:tile_cols, 3 * quarter:]
    rets[q] = jnp.concatenate([ret_ref[:, r, :] for r in range(tile_rows)], axis=1)

    expected = (
        depth + PLANE + 1
        + PLANE * ((q == PLANE - 1) & (z < depth - 1)).astype(jnp.int32)
        + PLANE * ((q == 0) & (z > 0)).astype(jnp.int32)
    )
    pl.semaphore_wait(barrier, expected)

    def weights_to_plane(which, k):
        for o in range(1, PLANE):
            qq = (q + o) % PLANE
            remote(
                w_ref.at[which, my_rows, my_cols(qq)], wf.at[which, z, q, half], w_send.at[0], w_plane.at[k],
                {"row": base + qq}).start()

    def side_copies(t, source):
        return [
            remote(source.at[:, 0:quarter], side.at[t, 0], side_send.at[t, 0], side_recv.at[t, 0], {"col": right}),
            remote(source.at[:, quarter:2 * quarter], side.at[t, 1], side_send.at[t, 1], side_recv.at[t, 1],
                   {"col": left}),
        ]

    def edges(act):
        for qq in range(PLANE):
            to = down_plane * PLANE + qq

            @pl.when(sends_down & (to != row))
            def _():
                act(remote(top_source, top_rows.at[down_slot], edge_send.at[0, qq], edge_recv.at[0, down_slot],
                           {"row": to}))

            to_up = up_plane * PLANE + qq

            @pl.when(sends_up & (to_up != row))
            def _():
                act(remote(bottom_source, bottom_rows.at[up_slot], edge_send.at[1, qq], edge_recv.at[1, up_slot],
                           {"row": to_up}))

    top_own = local(top_source, top_rows.at[down_slot], edge_own.at[0])
    bottom_own = local(bottom_source, bottom_rows.at[up_slot], edge_own.at[1])

    def own_edges(act):
        @pl.when(q < PLANE - 1)
        def _():
            act(top_own)

        @pl.when(q > 0)
        def _():
            act(bottom_own)

    weights_to_plane(KV, 0)
    for o in range(1, PLANE):
        remote(rets.at[q], rets.at[q], ret_send, ret_recv, {"row": base + (q + o) % PLANE}).start()
    edges(lambda c: c.start())
    own_edges(lambda c: c.start())
    for c in side_copies(q, x_ref):
        c.start()
    for k in range(PIECES):
        part = slice(k * piece, (k + 1) * piece)
        remote(x_ref.at[part], xt.at[q, part], x_send, x_piece.at[k], {"row": first_row}).start()
    remote(x_ref, xt.at[q], x_send, x_near, {"row": second_row}).start()
    weights_to_plane(R, 1)

    def weights_to_mate(which, k, zz):
        here = wf.at[which, zz, :, half]
        remote(here, here, w_send.at[2], w_mate.at[k], {"col": mate}).start()

    def weights_along_z(which, k):
        arrive(wf.at[which, z, 0:PLANE - 1, half], w_plane.at[k])
        here = wf.at[which, z, :, half]
        for o in range(1, depth):
            remote(here, here, w_send.at[1], w_z.at[k, z], {"row": (z + o) % depth * PLANE + q}).start()
        weights_to_mate(which, k, z)

    def weights_from_z(which, k):
        for o in range(1, depth):
            zz = (z + o) % depth
            arrive(wf.at[which, zz, :, half], w_z.at[k, zz])
            weights_to_mate(which, k, zz)

    def weights_from_mate(which, k):
        arrive(wf.at[which, :, :, 1 - half], w_mate.at[k])

    w_copy.wait()
    weights_along_z(KV, 0)

    arrive(rets.at[0:PLANE - 1], ret_recv)
    all_rets = jnp.concatenate([rets[t] for t in range(PLANE)], axis=0)
    picks = (
        iota((heads, PLANE * heads), 1)
        == iota((heads, PLANE * heads), 0) // hp * heads + q * hp + iota((heads, PLANE * heads), 0) % hp
    ).astype(F32)
    ret = jnp.dot(picks, all_rets, precision=HIGH, preferred_element_type=F32)
    tri = (iota((count, count), 0) >= iota((count, count), 1)).astype(F32)
    contract_last = (((1,), (1,)), ((), ()))
    running_c = lax.dot_general(tri, ret, contract_last, precision=HIGH, preferred_element_type=F32)
    running_r = lax.dot_general(ret, tri, contract_last, precision=HIGH, preferred_element_type=F32)
    eye = (iota((count, count), 0) == iota((count, count), 1)).astype(F32)
    ret_c = lax.dot_general(eye, ret, contract_last, precision=HIGH, preferred_element_type=F32)
    before_c = running_c - ret_c
    total_r = running_c[count - 1:count, :]
    rows_t[0] = running_c
    rows_t[1] = before_c
    rows_r[0] = running_r
    rows_r[1] = running_r - ret
    chosen = (iota((heads, width), 0) == iota((heads, width), 1) // hd).astype(F32)
    for k, table in enumerate((jnp.exp(total_r - running_c), jnp.exp(before_c))):
        spread_t[k] = jnp.dot(table, chosen, precision=HIGH, preferred_element_type=F32)
    log_t[...] = jnp.dot(jnp.broadcast_to(total_r, (8, heads)), chosen, precision=HIGH, preferred_element_type=F32)

    def log_of(vp):
        return log_t[:, vp * lanes:(vp + 1) * lanes]

    for j in range(gp):
        plane_log[j] = sum(log_of(t * gp + j) for t in range(PLANE))
    for o in range(1, depth):
        remote(plane_log, plane_logs.at[z], log_send, log_recv, {"row": (z + o) % depth * PLANE + q}).start()
    for j in range(gp):
        for t in range(PLANE):
            vp = t * gp + j
            zero = jnp.zeros((8, lanes), F32)
            decays_t[0, vp] = jnp.exp(log_of(vp))
            decays_t[1, vp] = jnp.exp(sum((log_of(s * gp + j) for s in range(t)), zero))
            decays_t[2, vp] = jnp.exp(sum((log_of(s * gp + j) for s in range(t + 1, PLANE)), zero))

    def picked(table, h):
        return jnp.sum(jnp.where(iota(table.shape, 1) == h, table, 0.0), axis=1, keepdims=True)

    def picked_row(table, h):
        return jnp.sum(jnp.where(iota(table.shape, 0) == h, table, 0.0), axis=0, keepdims=True)

    earlier = iota((count, count), 0) > iota((count, count), 1)
    diagonal = iota((count, count), 0) == iota((count, count), 1)

    def pair_decays(h, carry):
        rc, bc = picked(rows_t[0], h), picked(rows_t[1], h)
        rr, br = picked_row(rows_r[0], h), picked_row(rows_r[1], h)
        exponent = jnp.where(earlier, bc - rr, br - rc)
        decay[h] = jnp.where(diagonal, 0.0, jnp.exp(exponent))
        return carry

    def some_decays(part):
        lax.fori_loop(part * heads // 4, (part + 1) * heads // 4, pair_decays, 0)

    def forward(k):
        part = slice(k * piece, (k + 1) * piece)
        here = xt.at[q1, part]
        arrive(here, x_piece.at[k])
        remote(here, here, x_send, x_far, {"row": second_row}).start()

    def sides_out(t):
        for c in side_copies(t, xt.at[t]):
            c.start()

    def edges_in():
        own_edges(lambda c: c.wait())
        for t in range(PLANE):
            @pl.when((base + t > 0) & (q != t - 1))
            def _():
                arrive(top_rows.at[t], edge_recv.at[0, t])

            @pl.when((base + t < rows - 1) & (q != t + 1))
            def _():
                arrive(bottom_rows.at[t], edge_recv.at[1, t])

    place_in_row = iota((count, quarter), 0) % tile_cols
    last = tile_cols - 1

    def mix(t):
        for c in side_copies(t, xt.at[t]):
            c.wait_recv()
        x0 = xt[t, :, 0:quarter].astype(F32)
        x1 = xt[t, :, quarter:2 * quarter].astype(F32)
        side0 = jnp.where(col > 0, side[t, 0].astype(F32), 0.0)
        side1 = jnp.where(col < cols - 1, side[t, 1].astype(F32), 0.0)
        top = jnp.where(base + t > 0, top_rows[t].astype(F32), 0.0)
        bottom = jnp.where(base + t < rows - 1, bottom_rows[t].astype(F32), 0.0)
        shifted = [
            jnp.where(place_in_row == 0, pltpu.roll(side0, count - last, 0), pltpu.roll(x0, 1, 0)),
            jnp.where(place_in_row == last, pltpu.roll(side1, last, 0), pltpu.roll(x1, count - 1, 0)),
            jnp.concatenate([top, xt[t, 0:count - tile_cols, 2 * quarter:3 * quarter].astype(F32)], axis=0),
            jnp.concatenate([xt[t, tile_cols:count, 3 * quarter:].astype(F32), bottom], axis=0),
        ]
        for part in range(4):
            span = slice(part * quarter, (part + 1) * quarter)
            xs = xt[t, :, span].astype(F32)
            for p in range(3):
                c = ratio_ref[p:p + 1, span]
                mx[t, p, :, span] = (xs * c + shifted[part] * (1.0 - c)).astype(BF16)

    def project(p, t):
        proj[p, :, my_cols(t)] = jnp.dot(
            mx[t, p], wf[p].reshape(width, gw), preferred_element_type=F32).astype(BF16)

    low = iota((count, lanes), 1) < hd
    low_u = iota((hd, lanes), 1) < hd
    same_head = (iota((2 * lanes, lanes), 0) % lanes // hd == iota((2 * lanes, lanes), 1) // hd).astype(BF16)

    def halves(value):
        return jnp.dot(jnp.concatenate(two_terms(value), axis=1), same_head, preferred_element_type=F32)

    def span_of(i):
        return pl.ds(pl.multiple_of(i * lanes, lanes), lanes)

    def local_states(t):
        def one(j, carry):
            vp = t * gp + j
            span = span_of(vp)
            k = proj[1, :, span].astype(F32)
            v = proj[2, :, span]
            kd = jnp.concatenate([k * spread_t[0, :, span], k * spread_t[1, :, span]], axis=1).astype(BF16)
            m = lax.dot_general(kd, v, (((0,), (0,)), ((), ())), preferred_element_type=F32)
            sums[0, vp] = jnp.where(low_u, m[0:hd], m[hd:2 * hd])
            sums[1, vp] = jnp.where(low_u, m[2 * hd:3 * hd], m[3 * hd:])
            return carry

        lax.fori_loop(0, gp, one, 0)

    def keys_values(t):
        project(1, t)
        project(2, t)
        local_states(t)

    def planes_out():
        for j in range(gp):
            for d, order in ((0, range(PLANE)), (1, range(PLANE - 1, -1, -1))):
                state = jnp.zeros((hd, lanes), F32)
                for t in order:
                    vp = t * gp + j
                    before[d, vp] = state
                    state = decays_t[0, vp][0:1, :] * state + sums[d, vp]
                plane_sum[d, j] = state.astype(BF16)
        for o in range(1, depth):
            zz = (z + o) % depth
            remote(
                plane_sum.at[(zz < z).astype(jnp.int32)], plane_sums.at[z], sum_send, sum_recv,
                {"row": zz * PLANE + q}).start()

    def planes_in():
        arrive(plane_logs.at[0:depth - 1], log_recv)
        arrive(plane_sums.at[0:depth - 1], sum_recv)
        for j in range(gp):
            def one(i, carry):
                fwd, bwd = carry
                back = depth - 1 - i
                fwd = jnp.where(
                    i < z, jnp.exp(plane_logs[i, j][0:1, :]) * fwd + plane_sums[i, j].astype(F32), fwd)
                bwd = jnp.where(
                    back > z, jnp.exp(plane_logs[back, j][0:1, :]) * bwd + plane_sums[back, j].astype(F32), bwd)
                return fwd, bwd

            start = jnp.zeros((hd, lanes), F32)
            reached = lax.fori_loop(0, depth, one, (start, start), unroll=True if depth <= 4 else 1)
            for t in range(PLANE):
                vp = t * gp + j
                for d in range(2):
                    entering[d, vp] = before[d, vp] + decays_t[1 + d, vp][0:1, :] * reached[d]

    def channels(j):
        return pl.ds(pl.multiple_of(q * gw + j * lanes, lanes), lanes)

    def local_mix(t):
        def one(j, carry):
            vp = t * gp + j
            span = span_of(vp)
            r, k, v = proj[0, :, span], proj[1, :, span], proj[2, :, span]
            outs = []
            for s in range(2):
                rs = jnp.where(low if s == 0 else jnp.logical_not(low), r.astype(F32), 0.0).astype(BF16)
                scores = lax.dot_general(rs, k, contract_last, preferred_element_type=F32)
                weight = (scores * decay[2 * vp + s]).astype(BF16)
                outs.append(jnp.dot(weight, v, preferred_element_type=F32))
            own_term = halves(r.astype(F32) * credit_ref[:, channels(j)] * k.astype(F32)) * v.astype(F32)
            block[vp] = jnp.where(low, outs[0], outs[1]) + own_term
            return carry

        lax.fori_loop(0, gp, one, 0)

    def finish(t, dst):
        def one(j, carry):
            vp = t * gp + j
            span = span_of(vp)
            r = proj[0, :, span]
            fwd, bwd = [
                jnp.concatenate(
                    [jnp.where(low_u, entering[d, vp], 0.0), jnp.where(low_u, 0.0, entering[d, vp])], axis=0
                ).astype(BF16)
                for d in range(2)
            ]
            wkv = (
                block[vp]
                + spread_t[1, :, span] * jnp.dot(r, fwd, preferred_element_type=F32)
                + spread_t[0, :, span] * jnp.dot(r, bwd, preferred_element_type=F32)
            )
            centred = wkv - halves(wkv) * (1.0 / hd)
            variance = halves(centred * centred) * (1.0 / hd)
            normed = centred * lax.rsqrt(variance + 1e-05) * gain_ref[:, channels(j)]
            dst[t, :, span_of(j)] = normed.astype(BF16)
            return carry

        lax.fori_loop(0, gp, one, 0)

    def finish_and_send(t):
        finish(t, sent)
        remote(sent.at[t], landed.at[q], out_send, out_recv, {"row": base + t}).start()

    some_decays(0)
    x_copy.wait()
    edges_in()
    forward(0)
    mix(q)
    forward(1)
    some_decays(1)
    forward(2)
    some_decays(2)
    weights_from_z(KV, 0)
    forward(3)
    sides_out(q1)
    weights_along_z(R, 1)
    some_decays(3)
    arrive(xt.at[q2], x_near)
    sides_out(q2)
    weights_from_mate(KV, 0)
    keys_values(q)
    mix(q1)
    keys_values(q1)
    mix(q2)
    keys_values(q2)
    arrive(xt.at[q12], x_far)
    sides_out(q12)
    weights_from_z(R, 1)
    mix(q12)
    keys_values(q12)
    planes_out()
    weights_from_mate(R, 1)
    project(0, q1)
    local_mix(q1)
    project(0, q2)
    local_mix(q2)
    planes_in()
    finish_and_send(q1)
    finish_and_send(q2)
    project(0, q12)
    local_mix(q12)
    finish_and_send(q12)
    project(0, q)
    local_mix(q)
    finish(q, landed)
    arrive(landed.at[0:PLANE - 1], out_recv)

    group = (
        (iota((count, count), 0) // (2 * tile_cols) == iota((count, count), 1) // (2 * tile_cols))
        & (iota((count, count), 0) % tile_cols // 2 == iota((count, count), 1) % tile_cols // 2)
    ).astype(BF16)

    def over_group(value):
        rowsum = jnp.broadcast_to(jnp.sum(value, axis=1, keepdims=True), (count, lanes))
        both = jnp.dot(group, jnp.concatenate(two_terms(rowsum), axis=1), preferred_element_type=F32)
        return (both[:, 0:lanes] + both[:, lanes:]) * (1.0 / (4 * width))

    def add_up(i, total):
        made = xt[q, :, span_of(i)].astype(F32) + landed[i // gp, :, span_of(i % gp)].astype(F32)
        block[i] = made
        return total + made

    none = jnp.zeros((count, lanes), F32)
    mean = over_group(lax.fori_loop(0, vp_count, add_up, none))

    def spread(i, acc):
        dev = block[i] - mean
        return acc + dev * dev

    variance = over_group(lax.fori_loop(0, vp_count, spread, none))
    stats[0] = mean
    stats[1] = lax.rsqrt(variance + 1e-05)
    half_cols = tile_cols // 2

    def emit(i, carry):
        for part in range(4):
            span = pl.ds(pl.multiple_of(part * width + i * lanes, lanes), lanes)
            g, o = scale_ref[:, span], offset_ref[:, span]
            for a in range(tile_rows // 2):
                take = pl.ds((2 * a + part % 2) * tile_cols + part // 2, half_cols, stride=2)
                value = (block[i, take, :] - stats[0, take, :]) * stats[1, take, :]
                out_ref[a, :, span] = (value * g + o).astype(BF16)
        return carry

    lax.fori_loop(0, vp_count, emit, 0)

    left_by(xt.at[0:3], x_send)
    left_by(wf.at[:, z, 0:PLANE - 1, half], w_send.at[0])
    left_by(wf.at[:, 0:depth - 1, :, half], w_send.at[1])
    left_by(wf.at[:, :, :, half], w_send.at[2])
    left_by(rets.at[0:PLANE - 1], ret_send)
    left_by(plane_logs.at[0:depth - 1], log_send)
    left_by(plane_sums.at[0:depth - 1], sum_send)
    left_by(sent.at[0:PLANE - 1], out_send)
    edges(lambda c: c.wait_send())
    for t in range(PLANE):
        for c in side_copies(t, xt.at[t]):
            c.wait_send()


def body(x, ratios, w, retention, credit, gain, scale, offset):
    tile_rows, tile_cols, width = x.shape
    heads = retention.shape[0]
    count = tile_rows * tile_cols
    hd = width // heads
    rows, cols = lax.axis_size("row"), lax.axis_size("col")
    depth = rows // PLANE
    pairs = heads // 2
    lanes = 2 * hd
    gw = width // PLANE
    gp = gw // lanes
    dma = pltpu.SemaphoreType.DMA
    anywhere, vmem = pl.BlockSpec(memory_space=pl.ANY), pl.BlockSpec(memory_space=pltpu.VMEM)
    return pl.pallas_call(
        functools.partial(kernel, rows, cols, tile_rows, tile_cols, heads),
        out_shape=jax.ShapeDtypeStruct((tile_rows // 2, tile_cols // 2, 4 * width), BF16),
        in_specs=[anywhere, vmem, anywhere, vmem, vmem, vmem, vmem, vmem],
        out_specs=vmem,
        scratch_shapes=[
            pltpu.VMEM((PLANE, count, width), BF16),
            pltpu.VMEM((3, depth, PLANE, 2, w.shape[1] // 2, gw), BF16),
            pltpu.VMEM((PLANE, 3, count, width), BF16),
            pltpu.VMEM((3, count, width), BF16),
            pltpu.VMEM((heads, count, count), F32),
            pltpu.VMEM((PLANE, 2, count, width // 4), BF16),
            pltpu.VMEM((PLANE, tile_cols, width // 4), BF16),
            pltpu.VMEM((PLANE, tile_cols, width // 4), BF16),
            pltpu.VMEM((PLANE, heads, count), F32),
            pltpu.VMEM((2, count, heads), F32),
            pltpu.VMEM((2, heads, count), F32),
            pltpu.VMEM((2, count, width), F32),
            pltpu.VMEM((8, width), F32),
            pltpu.VMEM((gp, 8, lanes), F32),
            pltpu.VMEM((depth, gp, 8, lanes), F32),
            pltpu.VMEM((2, pairs, hd, lanes), F32),
            pltpu.VMEM((2, pairs, hd, lanes), F32),
            pltpu.VMEM((3, pairs, 8, lanes), F32),
            pltpu.VMEM((2, gp, hd, lanes), BF16),
            pltpu.VMEM((depth, gp, hd, lanes), BF16),
            pltpu.VMEM((2, pairs, hd, lanes), F32),
            pltpu.VMEM((pairs, count, lanes), F32),
            pltpu.VMEM((PLANE, count, gw), BF16),
            pltpu.VMEM((PLANE, count, gw), BF16),
            pltpu.VMEM((2, count, lanes), F32),
            dma, dma, dma((PIECES,)), dma, dma,
            dma, dma((3,)), dma((2,)), dma((2, depth)), dma((2,)),
            dma((PLANE, 2)), dma((PLANE, 2)),
            dma((2,)), dma((2, PLANE)), dma((2, PLANE)),
            dma, dma, dma, dma, dma, dma, dma, dma,
        ],
        compiler_params=pltpu.CompilerParams(
            collective_id=0, has_side_effects=True, vmem_limit_bytes=60 * 1024 * 1024),
    )(
        x.reshape(count, width), ratios, w, retention,
        credit.reshape(1, width), gain.reshape(1, width),
        scale.reshape(1, 4 * width), offset.reshape(1, 4 * width),
    )


def solution(mesh):
    return jax.shard_map(
        body,
        mesh=mesh,
        in_specs=(
            P("row", "col", None),
            P(),
            P(None, "row", None),
            P(None, "row", "col"),
            P(),
            P(),
            P(),
            P(),
        ),
        out_specs=P("row", "col", None),
        check_vma=False,
    )
```

```python
import functools

import jax
import jax.numpy as jnp
from jax import lax
from jax.experimental import pallas as pl
from jax.experimental.pallas import tpu as pltpu
from jax.sharding import PartitionSpec as P

MESH = pl.DeviceIdType.MESH
F32 = jnp.float32
BF16 = jnp.bfloat16
HIGH = lax.Precision.HIGHEST
PLANE = 4
PIECES = 4
KV, R = slice(1, 3), slice(0, 1)


def iota(shape, dim):
    return lax.broadcasted_iota(jnp.int32, shape, dim)


def two_terms(value):
    first = value.astype(BF16)
    return first, (value - first.astype(F32)).astype(BF16)


def kernel(
    rows, cols, tile_rows, tile_cols, heads,
    x_ref, ratio_hbm, w_ref, ret_hbm, credit_hbm, gain_hbm, scale_hbm, offset_hbm,
    out_hbm,
    ratio_ref, ret_ref, credit_ref, gain_ref, scale_ref, offset_ref, out_ref, shift_t,
    xt, wf, mx, proj, decay, side, top_rows, bottom_rows, ret_out, rets, rows_t, rows_r, spread_t, log_t, plane_log, plane_logs,
    sums, before, decays_t, plane_sum, plane_sums, entering, block, sent, landed, stats,
    small_in, out_left, x_own, x_send, x_piece, x_near, x_far, w_own, w_send, w_plane, w_z, w_mate, side_send, side_recv,
    edge_send, edge_recv, ret_send, ret_recv, log_send, log_recv, sum_send, sum_recv, out_send, out_recv,
):
    count, width = xt.shape[1:]
    hd = width // heads
    lanes = 2 * hd
    quarter = width // 4
    gw = width // PLANE
    gp = gw // lanes
    hp = heads // PLANE
    vp_count = PLANE * gp
    hs = w_ref.shape[1] // 2
    piece = count // PIECES
    row, col = lax.axis_index("row"), lax.axis_index("col")
    depth = rows // PLANE
    z, q = row // PLANE, row % PLANE
    bx, by = q % 2, q // 2
    half = col % 2
    mate = col + 1 - 2 * half
    q1 = (1 - half) * (q + 1 - 2 * bx) + half * (q + 2 - 4 * by)
    q2 = half * (q + 1 - 2 * bx) + (1 - half) * (q + 2 - 4 * by)
    q12 = PLANE - 1 - q
    base = z * PLANE
    first_row, second_row = base + q1, base + q2
    right, left = (col + 1) % cols, (col + cols - 1) % cols
    down_slot, up_slot = (q + 1) % PLANE, (q + PLANE - 1) % PLANE

    barrier = pltpu.get_barrier_semaphore()

    def greet(target):
        pl.semaphore_signal(barrier, inc=1, device_id=target, device_id_type=MESH)

    for o in range(1, depth):
        greet({"row": (z + o) % depth * PLANE + q})
    for o in range(1, PLANE):
        greet({"row": base + (q + o) % PLANE})
    for other in (right, left, mate):
        greet({"col": other})

    @pl.when(z > 0)
    def _():
        greet({"row": (base + rows - 1) % rows})

    @pl.when(z < depth - 1)
    def _():
        greet({"row": (base + PLANE) % rows})

    def local(src, dst, sem):
        return pltpu.make_async_copy(src, dst, sem)

    def remote(src, dst, send, recv, target):
        return pltpu.make_async_remote_copy(
            src, dst, send, recv, device_id=target, device_id_type=MESH)

    def arrive(ref, recv):
        remote(ref, ref, x_send, recv, {"col": mate}).wait_recv()

    def left_by(ref, send):
        remote(ref, ref, send, x_near, {"col": mate}).wait_send()

    my_rows = pl.ds(pl.multiple_of(half * hs, hs), hs)

    def my_cols(qq):
        return pl.ds(pl.multiple_of(qq * gw, gw), gw)

    small = [
        local(src, dst, small_in.at[k])
        for k, (src, dst) in enumerate((
            (ret_hbm, ret_ref), (ratio_hbm, ratio_ref), (credit_hbm, credit_ref), (gain_hbm, gain_ref),
            (scale_hbm, scale_ref), (offset_hbm, offset_ref)))
    ]
    for c in small:
        c.start()
    x_copy = local(x_ref, xt.at[q], x_own)
    w_copy = local(w_ref.at[:, my_rows, my_cols(q)], wf.at[:, z, q, half], w_own)
    w_copy.start()
    x_copy.start()
    top_source = x_ref.at[count - tile_cols:count, 2 * quarter:3 * quarter]
    bottom_source = x_ref.at[0:tile_cols, 3 * quarter:]
    small[0].wait()
    own_ret = jnp.concatenate([ret_ref[:, r, :] for r in range(tile_rows)], axis=1)
    for qq in range(PLANE):
        ret_out[qq, 0:hp] = own_ret[qq * hp:(qq + 1) * hp]

    expected = (
        depth + PLANE + 1
        + PLANE * ((q == PLANE - 1) & (z < depth - 1)).astype(jnp.int32)
        + PLANE * ((q == 0) & (z > 0)).astype(jnp.int32)
    )
    pl.semaphore_wait(barrier, expected)

    def weights_to_plane(which, k):
        for o in range(1, PLANE):
            qq = (q + o) % PLANE
            remote(
                w_ref.at[which, my_rows, my_cols(qq)], wf.at[which, z, q, half], w_send.at[0], w_plane.at[k],
                {"row": base + qq}).start()

    def side_copies(t, source):
        return [
            remote(source.at[:, 0:quarter], side.at[t, 0], side_send.at[t, 0], side_recv.at[t, 0], {"col": right}),
            remote(source.at[:, quarter:2 * quarter], side.at[t, 1], side_send.at[t, 1], side_recv.at[t, 1],
                   {"col": left}),
        ]

    def edges(act):
        @pl.when(q < PLANE - 1)
        def _():
            act(remote(top_source, top_rows.at[down_slot], edge_send.at[0, 0], edge_recv.at[0, down_slot],
                       {"row": base + q12}))

        @pl.when(q > 0)
        def _():
            act(remote(bottom_source, bottom_rows.at[up_slot], edge_send.at[1, 0], edge_recv.at[1, up_slot],
                       {"row": base + q12}))

        for qq in range(PLANE):
            @pl.when((q == PLANE - 1) & (z < depth - 1))
            def _():
                act(remote(top_source, top_rows.at[down_slot], edge_send.at[0, qq], edge_recv.at[0, down_slot],
                           {"row": (base + PLANE + qq) % rows}))

            @pl.when((q == 0) & (z > 0))
            def _():
                act(remote(bottom_source, bottom_rows.at[up_slot], edge_send.at[1, qq], edge_recv.at[1, up_slot],
                           {"row": (base + rows - PLANE + qq) % rows}))

    weights_to_plane(KV, 0)
    for o in range(1, PLANE):
        qq = (q + o) % PLANE
        remote(ret_out.at[qq], rets.at[q], ret_send, ret_recv, {"row": base + qq}).start()
    edges(lambda c: c.start())
    for c in side_copies(q, x_ref):
        c.start()
    for k in range(PIECES):
        part = slice(k * piece, (k + 1) * piece)
        remote(x_ref.at[part], xt.at[q, part], x_send, x_piece.at[k], {"row": first_row}).start()
    remote(x_ref, xt.at[q], x_send, x_near, {"row": second_row}).start()
    weights_to_plane(R, 1)

    def weights_to_mate(which, k, zz):
        here = wf.at[which, zz, :, half]
        remote(here, here, w_send.at[2], w_mate.at[k], {"col": mate}).start()

    def weights_along_z(which, k):
        arrive(wf.at[which, z, 0:PLANE - 1, half], w_plane.at[k])
        here = wf.at[which, z, :, half]
        for o in range(1, depth):
            remote(here, here, w_send.at[1], w_z.at[k, z], {"row": (z + o) % depth * PLANE + q}).start()
        weights_to_mate(which, k, z)

    def weights_from_z(which, k):
        for o in range(1, depth):
            zz = (z + o) % depth
            arrive(wf.at[which, zz, :, half], w_z.at[k, zz])
            weights_to_mate(which, k, zz)

    def weights_from_mate(which, k):
        arrive(wf.at[which, :, :, 1 - half], w_mate.at[k])

    w_copy.wait()
    weights_along_z(KV, 0)

    arrive(rets.at[0:PLANE - 1], ret_recv)
    rets[q] = ret_out[q]
    ret = jnp.concatenate([rets[t, 0:hp] for t in range(PLANE)], axis=0)
    tri = (iota((count, count), 0) >= iota((count, count), 1)).astype(F32)
    contract_last = (((1,), (1,)), ((), ()))
    running_c = lax.dot_general(tri, ret, contract_last, precision=HIGH, preferred_element_type=F32)
    running_r = lax.dot_general(ret, tri, contract_last, precision=HIGH, preferred_element_type=F32)
    eye = (iota((count, count), 0) == iota((count, count), 1)).astype(F32)
    ret_c = lax.dot_general(eye, ret, contract_last, precision=HIGH, preferred_element_type=F32)
    before_c = running_c - ret_c
    total_r = running_c[count - 1:count, :]
    rows_t[0] = running_c
    rows_t[1] = before_c
    rows_r[0] = running_r
    rows_r[1] = running_r - ret
    chosen = (iota((heads, width), 0) == iota((heads, width), 1) // hd).astype(F32)
    for k, table in enumerate((jnp.exp(total_r - running_c), jnp.exp(before_c))):
        spread_t[k] = jnp.dot(table, chosen, precision=HIGH, preferred_element_type=F32)
    log_t[...] = jnp.dot(jnp.broadcast_to(total_r, (8, heads)), chosen, precision=HIGH, preferred_element_type=F32)

    def log_of(vp):
        return log_t[:, vp * lanes:(vp + 1) * lanes]

    for j in range(gp):
        plane_log[j] = sum(log_of(t * gp + j) for t in range(PLANE))
    for o in range(1, depth):
        remote(plane_log, plane_logs.at[z], log_send, log_recv, {"row": (z + o) % depth * PLANE + q}).start()
    for j in range(gp):
        for t in range(PLANE):
            vp = t * gp + j
            zero = jnp.zeros((8, lanes), F32)
            decays_t[0, vp] = jnp.exp(log_of(vp))
            decays_t[1, vp] = jnp.exp(sum((log_of(s * gp + j) for s in range(t)), zero))
            decays_t[2, vp] = jnp.exp(sum((log_of(s * gp + j) for s in range(t + 1, PLANE)), zero))

    def picked(table, h):
        return jnp.sum(jnp.where(iota(table.shape, 1) == h, table, 0.0), axis=1, keepdims=True)

    def picked_row(table, h):
        return jnp.sum(jnp.where(iota(table.shape, 0) == h, table, 0.0), axis=0, keepdims=True)

    earlier = iota((count, count), 0) > iota((count, count), 1)
    diagonal = iota((count, count), 0) == iota((count, count), 1)

    def pair_decays(h, carry):
        rc, bc = picked(rows_t[0], h), picked(rows_t[1], h)
        rr, br = picked_row(rows_r[0], h), picked_row(rows_r[1], h)
        exponent = jnp.where(earlier, bc - rr, br - rc)
        decay[h] = jnp.where(diagonal, 0.0, jnp.exp(exponent))
        return carry

    def some_decays(part):
        lax.fori_loop(part * heads // 4, (part + 1) * heads // 4, pair_decays, 0)

    def forward(k):
        part = slice(k * piece, (k + 1) * piece)
        here = xt.at[q1, part]
        arrive(here, x_piece.at[k])
        remote(here, here, x_send, x_far, {"row": second_row}).start()

    def sides_out(t):
        for c in side_copies(t, xt.at[t]):
            c.start()

    def edges_in():
        @pl.when(z > 0)
        def _():
            arrive(top_rows.at[0], edge_recv.at[0, 0])

        @pl.when(z < depth - 1)
        def _():
            arrive(bottom_rows.at[PLANE - 1], edge_recv.at[1, PLANE - 1])

        @pl.when(q12 < PLANE - 1)
        def _():
            arrive(top_rows.at[0], edge_recv.at[0, (q12 + 1) % PLANE])

        @pl.when(q12 > 0)
        def _():
            arrive(bottom_rows.at[0], edge_recv.at[1, (q12 + PLANE - 1) % PLANE])

    place_in_row = iota((count, quarter), 0) % tile_cols
    last = tile_cols - 1

    def mix(t):
        for c in side_copies(t, xt.at[t]):
            c.wait_recv()
        x0 = xt[t, :, 0:quarter].astype(F32)
        x1 = xt[t, :, quarter:2 * quarter].astype(F32)
        side0 = jnp.where(col > 0, side[t, 0].astype(F32), 0.0)
        side1 = jnp.where(col < cols - 1, side[t, 1].astype(F32), 0.0)
        up_t, down_t = (t + PLANE - 1) % PLANE, (t + 1) % PLANE
        up_sent, down_sent = (t == 0) | (up_t == q12), (t == PLANE - 1) | (down_t == q12)
        up_t, down_t = jnp.where(up_sent, t, up_t), jnp.where(down_sent, t, down_t)
        above = xt[up_t, count - tile_cols:count, 2 * quarter:3 * quarter].astype(F32)
        below = xt[down_t, 0:tile_cols, 3 * quarter:].astype(F32)
        top = jnp.where(base + t > 0, jnp.where(up_sent, top_rows[t].astype(F32), above), 0.0)
        bottom = jnp.where(base + t < rows - 1, jnp.where(down_sent, bottom_rows[t].astype(F32), below), 0.0)
        shifted = [
            jnp.where(place_in_row == 0, pltpu.roll(side0, count - last, 0), pltpu.roll(x0, 1, 0)),
            jnp.where(place_in_row == last, pltpu.roll(side1, last, 0), pltpu.roll(x1, count - 1, 0)),
            jnp.concatenate([top, xt[t, 0:count - tile_cols, 2 * quarter:3 * quarter].astype(F32)], axis=0),
            jnp.concatenate([xt[t, tile_cols:count, 3 * quarter:].astype(F32), bottom], axis=0),
        ]
        for part in range(4):
            span = slice(part * quarter, (part + 1) * quarter)
            xs = xt[t, :, span].astype(F32)
            for p in range(3):
                c = ratio_ref[p:p + 1, span]
                mx[t, p, :, span] = (xs * c + shifted[part] * (1.0 - c)).astype(BF16)

    def project(p, t):
        proj[p, :, my_cols(t)] = jnp.dot(
            mx[t, p], wf[p].reshape(width, gw), preferred_element_type=F32).astype(BF16)

    low = iota((count, lanes), 1) < hd
    low_u = iota((hd, lanes), 1) < hd
    same_head = (iota((2 * lanes, lanes), 0) % lanes // hd == iota((2 * lanes, lanes), 1) // hd).astype(BF16)

    def halves(value):
        return jnp.dot(jnp.concatenate(two_terms(value), axis=1), same_head, preferred_element_type=F32)

    def span_of(i):
        return pl.ds(pl.multiple_of(i * lanes, lanes), lanes)

    def local_states(t):
        def one(j, carry):
            vp = t * gp + j
            span = span_of(vp)
            k = proj[1, :, span].astype(F32)
            v = proj[2, :, span]
            kd = jnp.concatenate([k * spread_t[0, :, span], k * spread_t[1, :, span]], axis=1).astype(BF16)
            m = lax.dot_general(kd, v, (((0,), (0,)), ((), ())), preferred_element_type=F32)
            sums[0, vp] = jnp.where(low_u, m[0:hd], m[hd:2 * hd])
            sums[1, vp] = jnp.where(low_u, m[2 * hd:3 * hd], m[3 * hd:])
            return carry

        lax.fori_loop(0, gp, one, 0)

    def keys_values(t):
        project(1, t)
        project(2, t)
        local_states(t)

    def planes_out():
        for j in range(gp):
            for d, order in ((0, range(PLANE)), (1, range(PLANE - 1, -1, -1))):
                state = jnp.zeros((hd, lanes), F32)
                for t in order:
                    vp = t * gp + j
                    before[d, vp] = state
                    state = decays_t[0, vp][0:1, :] * state + sums[d, vp]
                plane_sum[d, j] = state.astype(BF16)
        for o in range(1, depth):
            zz = (z + o) % depth
            remote(
                plane_sum.at[(zz < z).astype(jnp.int32)], plane_sums.at[z], sum_send, sum_recv,
                {"row": zz * PLANE + q}).start()

    def planes_in():
        arrive(plane_logs.at[0:depth - 1], log_recv)
        arrive(plane_sums.at[0:depth - 1], sum_recv)
        for j in range(gp):
            def one(i, carry):
                fwd, bwd = carry
                back = depth - 1 - i
                fwd = jnp.where(
                    i < z, jnp.exp(plane_logs[i, j][0:1, :]) * fwd + plane_sums[i, j].astype(F32), fwd)
                bwd = jnp.where(
                    back > z, jnp.exp(plane_logs[back, j][0:1, :]) * bwd + plane_sums[back, j].astype(F32), bwd)
                return fwd, bwd

            start = jnp.zeros((hd, lanes), F32)
            reached = lax.fori_loop(0, depth, one, (start, start), unroll=True if depth <= 4 else 1)
            for t in range(PLANE):
                vp = t * gp + j
                for d in range(2):
                    entering[d, vp] = before[d, vp] + decays_t[1 + d, vp][0:1, :] * reached[d]

    def channels(j):
        return pl.ds(pl.multiple_of(q * gw + j * lanes, lanes), lanes)

    def local_mix(t):
        def one(j, carry):
            vp = t * gp + j
            span = span_of(vp)
            r, k, v = proj[0, :, span], proj[1, :, span], proj[2, :, span]
            outs = []
            for s in range(2):
                rs = jnp.where(low if s == 0 else jnp.logical_not(low), r.astype(F32), 0.0).astype(BF16)
                scores = lax.dot_general(rs, k, contract_last, preferred_element_type=F32)
                weight = (scores * decay[2 * vp + s]).astype(BF16)
                outs.append(jnp.dot(weight, v, preferred_element_type=F32))
            own_term = halves(r.astype(F32) * credit_ref[:, channels(j)] * k.astype(F32)) * v.astype(F32)
            block[vp] = jnp.where(low, outs[0], outs[1]) + own_term
            return carry

        lax.fori_loop(0, gp, one, 0)

    def finish(t, dst, send=None):
        def one(j, carry):
            vp = t * gp + j
            span = span_of(vp)
            r = proj[0, :, span]
            fwd, bwd = [
                jnp.concatenate(
                    [jnp.where(low_u, entering[d, vp], 0.0), jnp.where(low_u, 0.0, entering[d, vp])], axis=0
                ).astype(BF16)
                for d in range(2)
            ]
            wkv = (
                block[vp]
                + spread_t[1, :, span] * jnp.dot(r, fwd, preferred_element_type=F32)
                + spread_t[0, :, span] * jnp.dot(r, bwd, preferred_element_type=F32)
            )
            centred = wkv - halves(wkv) * (1.0 / hd)
            variance = halves(centred * centred) * (1.0 / hd)
            normed = centred * lax.rsqrt(variance + 1e-05) * gain_ref[:, channels(j)]
            dst[t, j] = normed.astype(BF16)
            if send is not None:
                send(t, j)
            return carry

        lax.fori_loop(0, gp, one, 0)

    def finish_and_send(t):
        finish(t, sent, lambda t, j: remote(
            sent.at[t, j], landed.at[q, j], out_send, out_recv.at[q], {"row": base + t}).start())

    group = (
        (iota((count, count), 0) // (2 * tile_cols) == iota((count, count), 1) // (2 * tile_cols))
        & (iota((count, count), 0) % tile_cols // 2 == iota((count, count), 1) % tile_cols // 2)
    ).astype(BF16)

    def over_group(values):
        terms = []
        for value in values:
            terms.extend(two_terms(jnp.broadcast_to(jnp.sum(value, axis=1, keepdims=True), (count, lanes))))
        both = jnp.dot(group, jnp.concatenate(terms, axis=1), preferred_element_type=F32) * (1.0 / (4 * width))
        return [
            both[:, 2 * k * lanes:(2 * k + 1) * lanes] + both[:, (2 * k + 1) * lanes:(2 * k + 2) * lanes]
            for k in range(len(values))
        ]

    none = jnp.zeros((count, lanes), F32)

    def mean_of_x():
        total = none
        for i in range(vp_count):
            total = total + xt[q, :, i * lanes:(i + 1) * lanes].astype(F32)
        shift_t[...] = over_group([total])[0]

    def add_up(t, carry):
        def one(j, carry):
            first, second = carry
            i = t * gp + j
            made = xt[q, :, span_of(i)].astype(F32) - shift_t[...] + landed[t, j].astype(F32)
            block[i] = made
            return first + made, second + made * made

        return lax.fori_loop(0, gp, one, carry)

    for c in small[1:]:
        c.wait()

    some_decays(0)
    x_copy.wait()
    mean_of_x()
    edges_in()
    some_decays(1)
    forward(0)
    forward(1)
    some_decays(2)
    forward(2)
    some_decays(3)
    forward(3)
    sides_out(q1)
    arrive(xt.at[q2], x_near)
    sides_out(q2)
    weights_from_z(KV, 0)
    weights_along_z(R, 1)
    mix(q)
    mix(q1)
    mix(q2)
    weights_from_mate(KV, 0)
    keys_values(q)
    keys_values(q1)
    keys_values(q2)
    arrive(xt.at[q12], x_far)
    sides_out(q12)
    weights_from_z(R, 1)
    mix(q12)
    keys_values(q12)
    planes_out()
    weights_from_mate(R, 1)
    project(0, q1)
    local_mix(q1)
    project(0, q2)
    local_mix(q2)
    planes_in()
    finish_and_send(q1)
    finish_and_send(q2)
    project(0, q12)
    local_mix(q12)
    finish_and_send(q12)
    project(0, q)
    local_mix(q)
    finish(q, landed)
    carry = add_up(q, (none, none))
    for t in (q1, q2, q12):
        arrive(landed.at[t], out_recv.at[t])
        carry = add_up(t, carry)

    mean, square = over_group(carry)
    stats[0] = mean
    stats[1] = lax.rsqrt(jnp.maximum(square - mean * mean, 0.0) + 1e-05)
    half_cols = tile_cols // 2
    outs = []
    for a in range(tile_rows // 2):
        def emit(i, carry):
            for part in range(4):
                span = pl.ds(pl.multiple_of(part * width + i * lanes, lanes), lanes)
                take = pl.ds((2 * a + part % 2) * tile_cols + part // 2, half_cols, stride=2)
                value = (block[i, take, :] - stats[0, take, :]) * stats[1, take, :]
                out_ref[a, :, span] = (value * scale_ref[:, span] + offset_ref[:, span]).astype(BF16)
            return carry

        lax.fori_loop(0, vp_count, emit, 0)
        outs.append(local(out_ref.at[a], out_hbm.at[a], out_left.at[a]))
        outs[-1].start()

    left_by(xt.at[0:3], x_send)
    left_by(wf.at[:, z, 0:PLANE - 1, half], w_send.at[0])
    left_by(wf.at[:, 0:depth - 1, :, half], w_send.at[1])
    left_by(wf.at[:, :, :, half], w_send.at[2])
    left_by(rets.at[0:PLANE - 1], ret_send)
    left_by(plane_logs.at[0:depth - 1], log_send)
    left_by(plane_sums.at[0:depth - 1], sum_send)
    left_by(sent.at[0:PLANE - 1], out_send)
    edges(lambda c: c.wait_send())
    for t in range(PLANE):
        for c in side_copies(t, xt.at[t]):
            c.wait_send()
    for c in outs:
        c.wait()


def body(x, ratios, w, retention, credit, gain, scale, offset):
    tile_rows, tile_cols, width = x.shape
    heads = retention.shape[0]
    count = tile_rows * tile_cols
    hd = width // heads
    rows, cols = lax.axis_size("row"), lax.axis_size("col")
    depth = rows // PLANE
    pairs = heads // 2
    lanes = 2 * hd
    gw = width // PLANE
    gp = gw // lanes
    dma = pltpu.SemaphoreType.DMA
    anywhere = pl.BlockSpec(memory_space=pl.ANY)
    return pl.pallas_call(
        functools.partial(kernel, rows, cols, tile_rows, tile_cols, heads),
        out_shape=jax.ShapeDtypeStruct((tile_rows // 2, tile_cols // 2, 4 * width), BF16),
        in_specs=[anywhere] * 8,
        out_specs=anywhere,
        scratch_shapes=[
            pltpu.VMEM((3, width), F32),
            pltpu.VMEM((heads, tile_rows, tile_cols), F32),
            pltpu.VMEM((1, width), F32),
            pltpu.VMEM((1, width), F32),
            pltpu.VMEM((1, 4 * width), F32),
            pltpu.VMEM((1, 4 * width), F32),
            pltpu.VMEM((tile_rows // 2, tile_cols // 2, 4 * width), BF16),
            pltpu.VMEM((count, lanes), F32),
            pltpu.VMEM((PLANE, count, width), BF16),
            pltpu.VMEM((3, depth, PLANE, 2, w.shape[1] // 2, gw), BF16),
            pltpu.VMEM((PLANE, 3, count, width), BF16),
            pltpu.VMEM((3, count, width), BF16),
            pltpu.VMEM((heads, count, count), F32),
            pltpu.VMEM((PLANE, 2, count, width // 4), BF16),
            pltpu.VMEM((PLANE, tile_cols, width // 4), BF16),
            pltpu.VMEM((PLANE, tile_cols, width // 4), BF16),
            pltpu.VMEM((PLANE, 8, count), F32),
            pltpu.VMEM((PLANE, 8, count), F32),
            pltpu.VMEM((2, count, heads), F32),
            pltpu.VMEM((2, heads, count), F32),
            pltpu.VMEM((2, count, width), F32),
            pltpu.VMEM((8, width), F32),
            pltpu.VMEM((gp, 8, lanes), F32),
            pltpu.VMEM((depth, gp, 8, lanes), F32),
            pltpu.VMEM((2, pairs, hd, lanes), F32),
            pltpu.VMEM((2, pairs, hd, lanes), F32),
            pltpu.VMEM((3, pairs, 8, lanes), F32),
            pltpu.VMEM((2, gp, hd, lanes), BF16),
            pltpu.VMEM((depth, gp, hd, lanes), BF16),
            pltpu.VMEM((2, pairs, hd, lanes), F32),
            pltpu.VMEM((pairs, count, lanes), F32),
            pltpu.VMEM((PLANE, gp, count, lanes), BF16),
            pltpu.VMEM((PLANE, gp, count, lanes), BF16),
            pltpu.VMEM((2, count, lanes), F32),
            dma((6,)), dma((tile_rows // 2,)),
            dma, dma, dma((PIECES,)), dma, dma,
            dma, dma((3,)), dma((2,)), dma((2, depth)), dma((2,)),
            dma((PLANE, 2)), dma((PLANE, 2)),
            dma((2, PLANE)), dma((2, PLANE)),
            dma, dma, dma, dma, dma, dma, dma, dma((PLANE,)),
        ],
        compiler_params=pltpu.CompilerParams(
            collective_id=0, has_side_effects=True, vmem_limit_bytes=60 * 1024 * 1024),
    )(
        x.reshape(count, width), ratios, w, retention,
        credit.reshape(1, width), gain.reshape(1, width),
        scale.reshape(1, 4 * width), offset.reshape(1, 4 * width),
    )


def solution(mesh):
    return jax.shard_map(
        body,
        mesh=mesh,
        in_specs=(
            P("row", "col", None),
            P(),
            P(None, "row", None),
            P(None, "row", "col"),
            P(),
            P(),
            P(),
            P(),
        ),
        out_specs=P("row", "col", None),
        check_vma=False,
    )
```

```python
import functools

import jax
import jax.numpy as jnp
from jax import lax
from jax.experimental import pallas as pl
from jax.experimental.pallas import tpu as pltpu
from jax.sharding import PartitionSpec as P

MESH = pl.DeviceIdType.MESH
F32 = jnp.float32
BF16 = jnp.bfloat16
HIGH = lax.Precision.HIGHEST
PLANE = 4
PIECES = 4
KV, R = slice(1, 3), slice(0, 1)


def iota(shape, dim):
    return lax.broadcasted_iota(jnp.int32, shape, dim)


def two_terms(value):
    first = value.astype(BF16)
    return first, (value - first.astype(F32)).astype(BF16)


def kernel(
    rows, cols, tile_rows, tile_cols, heads,
    x_ref, ratio_hbm, w_ref, ret_hbm, credit_hbm, gain_hbm, scale_hbm, offset_hbm,
    out_hbm,
    ratio_ref, ret_ref, credit_ref, gain_ref, scale_ref, offset_ref, out_ref, shift_t,
    xt, wf, mx, proj, decay, side, side_out, side_far, top_rows, bottom_rows, ret_out, rets, rows_t, rows_r, spread_t, log_t, plane_log, plane_logs,
    sums, before, decays_t, plane_sum, plane_sums, entering, block, sent, landed, stats,
    small_in, out_left, x_own, x_send, x_piece, x_near, x_far, w_own, w_send, w_plane, w_z, w_mate, side_send, side_recv, far_send, far_recv,
    edge_send, edge_recv, ret_send, ret_recv, log_send, log_recv, sum_send, sum_recv, out_send, out_recv,
):
    count, width = xt.shape[1:]
    hd = width // heads
    lanes = 2 * hd
    quarter = width // 4
    gw = width // PLANE
    gp = gw // lanes
    hp = heads // PLANE
    vp_count = PLANE * gp
    hs = w_ref.shape[1] // 2
    piece = count // PIECES
    row, col = lax.axis_index("row"), lax.axis_index("col")
    depth = rows // PLANE
    z, q = row // PLANE, row % PLANE
    bx, by = q % 2, q // 2
    half = col % 2
    mate = col + 1 - 2 * half
    q1 = (1 - half) * (q + 1 - 2 * bx) + half * (q + 2 - 4 * by)
    q2 = half * (q + 1 - 2 * bx) + (1 - half) * (q + 2 - 4 * by)
    q12 = PLANE - 1 - q
    base = z * PLANE
    first_row, second_row = base + q1, base + q2
    right, left = (col + 1) % cols, (col + cols - 1) % cols
    down_slot, up_slot = (q + 1) % PLANE, (q + PLANE - 1) % PLANE

    barrier = pltpu.get_barrier_semaphore()

    def greet(target):
        pl.semaphore_signal(barrier, inc=1, device_id=target, device_id_type=MESH)

    for o in range(1, depth):
        greet({"row": (z + o) % depth * PLANE + q})
    for o in range(1, PLANE):
        greet({"row": base + (q + o) % PLANE})
    for other in (right, left, mate):
        greet({"col": other})

    @pl.when(z > 0)
    def _():
        greet({"row": (base + rows - 1) % rows})

    @pl.when(z < depth - 1)
    def _():
        greet({"row": (base + PLANE) % rows})

    def local(src, dst, sem):
        return pltpu.make_async_copy(src, dst, sem)

    def remote(src, dst, send, recv, target):
        return pltpu.make_async_remote_copy(
            src, dst, send, recv, device_id=target, device_id_type=MESH)

    def arrive(ref, recv):
        remote(ref, ref, x_send, recv, {"col": mate}).wait_recv()

    def left_by(ref, send):
        remote(ref, ref, send, x_near, {"col": mate}).wait_send()

    my_rows = pl.ds(pl.multiple_of(half * hs, hs), hs)

    def my_cols(qq):
        return pl.ds(pl.multiple_of(qq * gw, gw), gw)

    small = [
        local(src, dst, small_in.at[k])
        for k, (src, dst) in enumerate((
            (ret_hbm, ret_ref), (ratio_hbm, ratio_ref), (credit_hbm, credit_ref), (gain_hbm, gain_ref),
            (scale_hbm, scale_ref), (offset_hbm, offset_ref)))
    ]
    for c in small:
        c.start()
    x_copy = local(x_ref, xt.at[q], x_own)
    w_copy = local(w_ref.at[:, my_rows, my_cols(q)], wf.at[:, z, q, half], w_own)
    w_copy.start()
    x_copy.start()
    top_source = x_ref.at[count - tile_cols:count, 2 * quarter:3 * quarter]
    bottom_source = x_ref.at[0:tile_cols, 3 * quarter:]
    small[0].wait()
    own_ret = jnp.concatenate([ret_ref[:, r, :] for r in range(tile_rows)], axis=1)
    for qq in range(PLANE):
        ret_out[qq, 0:hp] = own_ret[qq * hp:(qq + 1) * hp]

    expected = (
        depth + PLANE + 1
        + PLANE * ((q == PLANE - 1) & (z < depth - 1)).astype(jnp.int32)
        + PLANE * ((q == 0) & (z > 0)).astype(jnp.int32)
    )
    pl.semaphore_wait(barrier, expected)

    def weights_to_plane(which, k):
        for o in range(1, PLANE):
            qq = (q + o) % PLANE
            remote(
                w_ref.at[which, my_rows, my_cols(qq)], wf.at[which, z, q, half], w_send.at[0], w_plane.at[k],
                {"row": base + qq}).start()

    def side_copies(t, source):
        return [
            remote(source.at[:, 0:quarter], side.at[t, 0], side_send.at[t, 0], side_recv.at[t, 0], {"col": right}),
            remote(source.at[:, quarter:2 * quarter], side.at[t, 1], side_send.at[t, 1], side_recv.at[t, 1],
                   {"col": left}),
        ]

    def edges(act):
        @pl.when(q < PLANE - 1)
        def _():
            act(remote(top_source, top_rows.at[down_slot], edge_send.at[0, 0], edge_recv.at[0, down_slot],
                       {"row": base + q12}))

        @pl.when(q > 0)
        def _():
            act(remote(bottom_source, bottom_rows.at[up_slot], edge_send.at[1, 0], edge_recv.at[1, up_slot],
                       {"row": base + q12}))

        for qq in range(PLANE):
            @pl.when((q == PLANE - 1) & (z < depth - 1))
            def _():
                act(remote(top_source, top_rows.at[down_slot], edge_send.at[0, qq], edge_recv.at[0, down_slot],
                           {"row": (base + PLANE + qq) % rows}))

            @pl.when((q == 0) & (z > 0))
            def _():
                act(remote(bottom_source, bottom_rows.at[up_slot], edge_send.at[1, qq], edge_recv.at[1, up_slot],
                           {"row": (base + rows - PLANE + qq) % rows}))

    weights_to_plane(KV, 0)
    for o in range(1, PLANE):
        qq = (q + o) % PLANE
        remote(ret_out.at[qq], rets.at[q], ret_send, ret_recv, {"row": base + qq}).start()
    edges(lambda c: c.start())
    for c in side_copies(q, x_ref):
        c.start()
    for k in range(PIECES):
        part = slice(k * piece, (k + 1) * piece)
        remote(x_ref.at[part], xt.at[q, part], x_send, x_piece.at[k], {"row": first_row}).start()
    remote(x_ref, xt.at[q], x_send, x_near, {"row": second_row}).start()
    weights_to_plane(R, 1)

    def weights_to_mate(which, k, zz):
        here = wf.at[which, zz, :, half]
        remote(here, here, w_send.at[2], w_mate.at[k], {"col": mate}).start()

    def weights_along_z(which, k):
        arrive(wf.at[which, z, 0:PLANE - 1, half], w_plane.at[k])
        here = wf.at[which, z, :, half]
        for o in range(1, depth):
            remote(here, here, w_send.at[1], w_z.at[k, z], {"row": (z + o) % depth * PLANE + q}).start()
        weights_to_mate(which, k, z)

    def weights_from_z(which, k):
        for o in range(1, depth):
            zz = (z + o) % depth
            arrive(wf.at[which, zz, :, half], w_z.at[k, zz])
            weights_to_mate(which, k, zz)

    def weights_from_mate(which, k):
        arrive(wf.at[which, :, :, 1 - half], w_mate.at[k])

    w_copy.wait()
    weights_along_z(KV, 0)

    arrive(rets.at[0:PLANE - 1], ret_recv)
    rets[q] = ret_out[q]
    ret = jnp.concatenate([rets[t, 0:hp] for t in range(PLANE)], axis=0)
    tri = (iota((count, count), 0) >= iota((count, count), 1)).astype(F32)
    contract_last = (((1,), (1,)), ((), ()))
    running_c = lax.dot_general(tri, ret, contract_last, precision=HIGH, preferred_element_type=F32)
    running_r = lax.dot_general(ret, tri, contract_last, precision=HIGH, preferred_element_type=F32)
    eye = (iota((count, count), 0) == iota((count, count), 1)).astype(F32)
    ret_c = lax.dot_general(eye, ret, contract_last, precision=HIGH, preferred_element_type=F32)
    before_c = running_c - ret_c
    total_r = running_c[count - 1:count, :]
    rows_t[0] = running_c
    rows_t[1] = before_c
    rows_r[0] = running_r
    rows_r[1] = running_r - ret
    chosen = (iota((heads, width), 0) == iota((heads, width), 1) // hd).astype(F32)
    for k, table in enumerate((jnp.exp(total_r - running_c), jnp.exp(before_c))):
        spread_t[k] = jnp.dot(table, chosen, precision=HIGH, preferred_element_type=F32)
    log_t[...] = jnp.dot(jnp.broadcast_to(total_r, (8, heads)), chosen, precision=HIGH, preferred_element_type=F32)

    def log_of(vp):
        return log_t[:, vp * lanes:(vp + 1) * lanes]

    for j in range(gp):
        plane_log[j] = sum(log_of(t * gp + j) for t in range(PLANE))
    for o in range(1, depth):
        remote(plane_log, plane_logs.at[z], log_send, log_recv, {"row": (z + o) % depth * PLANE + q}).start()
    for j in range(gp):
        for t in range(PLANE):
            vp = t * gp + j
            zero = jnp.zeros((8, lanes), F32)
            decays_t[0, vp] = jnp.exp(log_of(vp))
            decays_t[1, vp] = jnp.exp(sum((log_of(s * gp + j) for s in range(t)), zero))
            decays_t[2, vp] = jnp.exp(sum((log_of(s * gp + j) for s in range(t + 1, PLANE)), zero))

    def picked(table, h):
        return jnp.sum(jnp.where(iota(table.shape, 1) == h, table, 0.0), axis=1, keepdims=True)

    def picked_row(table, h):
        return jnp.sum(jnp.where(iota(table.shape, 0) == h, table, 0.0), axis=0, keepdims=True)

    earlier = iota((count, count), 0) > iota((count, count), 1)
    diagonal = iota((count, count), 0) == iota((count, count), 1)

    def pair_decays(h, carry):
        rc, bc = picked(rows_t[0], h), picked(rows_t[1], h)
        rr, br = picked_row(rows_r[0], h), picked_row(rows_r[1], h)
        exponent = jnp.where(earlier, bc - rr, br - rc)
        decay[h] = jnp.where(diagonal, 0.0, jnp.exp(exponent))
        return carry

    def some_decays(part):
        lax.fori_loop(part * heads // 4, (part + 1) * heads // 4, pair_decays, 0)

    def forward(k):
        part = slice(k * piece, (k + 1) * piece)
        here = xt.at[q1, part]
        arrive(here, x_piece.at[k])
        remote(here, here, x_send, x_far, {"row": second_row}).start()

    def sides_out(t):
        for c in side_copies(t, xt.at[t]):
            c.start()

    def edges_in():
        @pl.when(z > 0)
        def _():
            arrive(top_rows.at[0], edge_recv.at[0, 0])

        @pl.when(z < depth - 1)
        def _():
            arrive(bottom_rows.at[PLANE - 1], edge_recv.at[1, PLANE - 1])

        @pl.when(q12 < PLANE - 1)
        def _():
            arrive(top_rows.at[0], edge_recv.at[0, (q12 + 1) % PLANE])

        @pl.when(q12 > 0)
        def _():
            arrive(bottom_rows.at[0], edge_recv.at[1, (q12 + PLANE - 1) % PLANE])

    place_in_row = iota((count, quarter), 0) % tile_cols
    last = tile_cols - 1

    def far_sides_out():
        for c in side_copies(q, x_ref):
            c.wait_recv()
        token, line = iota((tile_rows, count), 1), iota((tile_rows, count), 0) * tile_cols
        for k in range(2):
            pick = (token == line + (last if k == 0 else 0)).astype(BF16)
            side_out[k] = jnp.dot(pick, side[q, k], preferred_element_type=F32).astype(BF16)
        remote(side_out, side_far, far_send, far_recv, {"row": base + q12}).start()

    def mix(t, kind):
        x0 = xt[t, :, 0:quarter].astype(F32)
        x1 = xt[t, :, quarter:2 * quarter].astype(F32)
        if kind == "far":
            arrive(side_far, far_recv)
            token, line = iota((count, tile_rows), 0), iota((count, tile_rows), 1) * tile_cols
            side0, side1 = [
                jnp.dot((token == line + (0 if k == 0 else last)).astype(BF16), side_far[k],
                        preferred_element_type=F32)
                for k in range(2)
            ]
        else:
            if kind == "near":
                for c in side_copies(t, xt.at[t]):
                    c.wait_recv()
            side0 = pltpu.roll(side[t, 0].astype(F32), count - last, 0)
            side1 = pltpu.roll(side[t, 1].astype(F32), last, 0)
        side0 = jnp.where(col > 0, side0, 0.0)
        side1 = jnp.where(col < cols - 1, side1, 0.0)
        up_t, down_t = (t + PLANE - 1) % PLANE, (t + 1) % PLANE
        up_sent, down_sent = (t == 0) | (up_t == q12), (t == PLANE - 1) | (down_t == q12)
        up_t, down_t = jnp.where(up_sent, t, up_t), jnp.where(down_sent, t, down_t)
        above = xt[up_t, count - tile_cols:count, 2 * quarter:3 * quarter].astype(F32)
        below = xt[down_t, 0:tile_cols, 3 * quarter:].astype(F32)
        top = jnp.where(base + t > 0, jnp.where(up_sent, top_rows[t].astype(F32), above), 0.0)
        bottom = jnp.where(base + t < rows - 1, jnp.where(down_sent, bottom_rows[t].astype(F32), below), 0.0)
        shifted = [
            jnp.where(place_in_row == 0, side0, pltpu.roll(x0, 1, 0)),
            jnp.where(place_in_row == last, side1, pltpu.roll(x1, count - 1, 0)),
            jnp.concatenate([top, xt[t, 0:count - tile_cols, 2 * quarter:3 * quarter].astype(F32)], axis=0),
            jnp.concatenate([xt[t, tile_cols:count, 3 * quarter:].astype(F32), bottom], axis=0),
        ]
        for part in range(4):
            span = slice(part * quarter, (part + 1) * quarter)
            xs = xt[t, :, span].astype(F32)
            for p in range(3):
                c = ratio_ref[p:p + 1, span]
                mx[t, p, :, span] = (xs * c + shifted[part] * (1.0 - c)).astype(BF16)

    def project(p, t):
        proj[p, :, my_cols(t)] = jnp.dot(
            mx[t, p], wf[p].reshape(width, gw), preferred_element_type=F32).astype(BF16)

    low = iota((count, lanes), 1) < hd
    low_u = iota((hd, lanes), 1) < hd
    same_head = (iota((2 * lanes, lanes), 0) % lanes // hd == iota((2 * lanes, lanes), 1) // hd).astype(BF16)

    def halves(value):
        return jnp.dot(jnp.concatenate(two_terms(value), axis=1), same_head, preferred_element_type=F32)

    def span_of(i):
        return pl.ds(pl.multiple_of(i * lanes, lanes), lanes)

    def local_states(t):
        def one(j, carry):
            vp = t * gp + j
            span = span_of(vp)
            k = proj[1, :, span].astype(F32)
            v = proj[2, :, span]
            kd = jnp.concatenate([k * spread_t[0, :, span], k * spread_t[1, :, span]], axis=1).astype(BF16)
            m = lax.dot_general(kd, v, (((0,), (0,)), ((), ())), preferred_element_type=F32)
            sums[0, vp] = jnp.where(low_u, m[0:hd], m[hd:2 * hd])
            sums[1, vp] = jnp.where(low_u, m[2 * hd:3 * hd], m[3 * hd:])
            return carry

        lax.fori_loop(0, gp, one, 0)

    def keys_values(t):
        project(1, t)
        project(2, t)
        local_states(t)

    def planes_out():
        for j in range(gp):
            for d, order in ((0, range(PLANE)), (1, range(PLANE - 1, -1, -1))):
                state = jnp.zeros((hd, lanes), F32)
                for t in order:
                    vp = t * gp + j
                    before[d, vp] = state
                    state = decays_t[0, vp][0:1, :] * state + sums[d, vp]
                plane_sum[d, j] = state.astype(BF16)
        for o in range(1, depth):
            zz = (z + o) % depth
            remote(
                plane_sum.at[(zz < z).astype(jnp.int32)], plane_sums.at[z], sum_send, sum_recv,
                {"row": zz * PLANE + q}).start()

    def planes_in():
        arrive(plane_logs.at[0:depth - 1], log_recv)
        arrive(plane_sums.at[0:depth - 1], sum_recv)
        for j in range(gp):
            def one(i, carry):
                fwd, bwd = carry
                back = depth - 1 - i
                fwd = jnp.where(
                    i < z, jnp.exp(plane_logs[i, j][0:1, :]) * fwd + plane_sums[i, j].astype(F32), fwd)
                bwd = jnp.where(
                    back > z, jnp.exp(plane_logs[back, j][0:1, :]) * bwd + plane_sums[back, j].astype(F32), bwd)
                return fwd, bwd

            start = jnp.zeros((hd, lanes), F32)
            reached = lax.fori_loop(0, depth, one, (start, start), unroll=True if depth <= 4 else 1)
            for t in range(PLANE):
                vp = t * gp + j
                for d in range(2):
                    entering[d, vp] = before[d, vp] + decays_t[1 + d, vp][0:1, :] * reached[d]

    def channels(j):
        return pl.ds(pl.multiple_of(q * gw + j * lanes, lanes), lanes)

    def local_mix(t):
        def one(j, carry):
            vp = t * gp + j
            span = span_of(vp)
            r, k, v = proj[0, :, span], proj[1, :, span], proj[2, :, span]
            outs = []
            for s in range(2):
                rs = jnp.where(low if s == 0 else jnp.logical_not(low), r.astype(F32), 0.0).astype(BF16)
                scores = lax.dot_general(rs, k, contract_last, preferred_element_type=F32)
                weight = (scores * decay[2 * vp + s]).astype(BF16)
                outs.append(jnp.dot(weight, v, preferred_element_type=F32))
            own_term = halves(r.astype(F32) * credit_ref[:, channels(j)] * k.astype(F32)) * v.astype(F32)
            block[vp] = jnp.where(low, outs[0], outs[1]) + own_term
            return carry

        lax.fori_loop(0, gp, one, 0)

    def finish(t, dst, send=None):
        def one(j, carry):
            vp = t * gp + j
            span = span_of(vp)
            r = proj[0, :, span]
            fwd, bwd = [
                jnp.concatenate(
                    [jnp.where(low_u, entering[d, vp], 0.0), jnp.where(low_u, 0.0, entering[d, vp])], axis=0
                ).astype(BF16)
                for d in range(2)
            ]
            wkv = (
                block[vp]
                + spread_t[1, :, span] * jnp.dot(r, fwd, preferred_element_type=F32)
                + spread_t[0, :, span] * jnp.dot(r, bwd, preferred_element_type=F32)
            )
            centred = wkv - halves(wkv) * (1.0 / hd)
            variance = halves(centred * centred) * (1.0 / hd)
            normed = centred * lax.rsqrt(variance + 1e-05) * gain_ref[:, channels(j)]
            dst[t, j] = normed.astype(BF16)
            if send is not None:
                send(t, j)
            return carry

        lax.fori_loop(0, gp, one, 0)

    def finish_and_send(t):
        finish(t, sent, lambda t, j: remote(
            sent.at[t, j], landed.at[q, j], out_send, out_recv.at[q], {"row": base + t}).start())

    group = (
        (iota((count, count), 0) // (2 * tile_cols) == iota((count, count), 1) // (2 * tile_cols))
        & (iota((count, count), 0) % tile_cols // 2 == iota((count, count), 1) % tile_cols // 2)
    ).astype(BF16)

    def over_group(values):
        terms = []
        for value in values:
            terms.extend(two_terms(jnp.broadcast_to(jnp.sum(value, axis=1, keepdims=True), (count, lanes))))
        both = jnp.dot(group, jnp.concatenate(terms, axis=1), preferred_element_type=F32) * (1.0 / (4 * width))
        return [
            both[:, 2 * k * lanes:(2 * k + 1) * lanes] + both[:, (2 * k + 1) * lanes:(2 * k + 2) * lanes]
            for k in range(len(values))
        ]

    none = jnp.zeros((count, lanes), F32)

    def mean_of_x():
        total = none
        for i in range(vp_count):
            total = total + xt[q, :, i * lanes:(i + 1) * lanes].astype(F32)
        shift_t[...] = over_group([total])[0]

    def add_up(t, carry):
        def one(j, carry):
            first, second = carry
            i = t * gp + j
            made = xt[q, :, span_of(i)].astype(F32) - shift_t[...] + landed[t, j].astype(F32)
            block[i] = made
            return first + made, second + made * made

        return lax.fori_loop(0, gp, one, carry)

    for c in small[1:]:
        c.wait()

    far_sides_out()
    some_decays(0)
    x_copy.wait()
    mean_of_x()
    edges_in()
    some_decays(1)
    forward(0)
    forward(1)
    some_decays(2)
    forward(2)
    some_decays(3)
    forward(3)
    sides_out(q1)
    arrive(xt.at[q2], x_near)
    sides_out(q2)
    weights_from_z(KV, 0)
    weights_along_z(R, 1)
    mix(q, "own")
    mix(q1, "near")
    mix(q2, "near")
    weights_from_mate(KV, 0)
    keys_values(q)
    keys_values(q1)
    keys_values(q2)
    arrive(xt.at[q12], x_far)
    mix(q12, "far")
    keys_values(q12)
    planes_out()
    weights_from_z(R, 1)
    weights_from_mate(R, 1)
    project(0, q1)
    local_mix(q1)
    project(0, q2)
    local_mix(q2)
    planes_in()
    finish_and_send(q1)
    finish_and_send(q2)
    project(0, q12)
    local_mix(q12)
    finish_and_send(q12)
    project(0, q)
    local_mix(q)
    finish(q, landed)
    carry = add_up(q, (none, none))
    for t in (q1, q2, q12):
        arrive(landed.at[t], out_recv.at[t])
        carry = add_up(t, carry)

    mean, square = over_group(carry)
    stats[0] = mean
    stats[1] = lax.rsqrt(jnp.maximum(square - mean * mean, 0.0) + 1e-05)
    half_cols = tile_cols // 2
    outs = []
    for a in range(tile_rows // 2):
        def emit(i, carry):
            for part in range(4):
                span = pl.ds(pl.multiple_of(part * width + i * lanes, lanes), lanes)
                take = pl.ds((2 * a + part % 2) * tile_cols + part // 2, half_cols, stride=2)
                value = (block[i, take, :] - stats[0, take, :]) * stats[1, take, :]
                out_ref[a, :, span] = (value * scale_ref[:, span] + offset_ref[:, span]).astype(BF16)
            return carry

        lax.fori_loop(0, vp_count, emit, 0)
        outs.append(local(out_ref.at[a], out_hbm.at[a], out_left.at[a]))
        outs[-1].start()

    left_by(xt.at[0:3], x_send)
    left_by(wf.at[:, z, 0:PLANE - 1, half], w_send.at[0])
    left_by(wf.at[:, 0:depth - 1, :, half], w_send.at[1])
    left_by(wf.at[:, :, :, half], w_send.at[2])
    left_by(rets.at[0:PLANE - 1], ret_send)
    left_by(plane_logs.at[0:depth - 1], log_send)
    left_by(plane_sums.at[0:depth - 1], sum_send)
    left_by(sent.at[0:PLANE - 1], out_send)
    edges(lambda c: c.wait_send())
    for t in (q, q1, q2):
        for c in side_copies(t, xt.at[t]):
            c.wait_send()
    left_by(side_out, far_send)
    for c in outs:
        c.wait()


def body(x, ratios, w, retention, credit, gain, scale, offset):
    tile_rows, tile_cols, width = x.shape
    heads = retention.shape[0]
    count = tile_rows * tile_cols
    hd = width // heads
    rows, cols = lax.axis_size("row"), lax.axis_size("col")
    depth = rows // PLANE
    pairs = heads // 2
    lanes = 2 * hd
    gw = width // PLANE
    gp = gw // lanes
    dma = pltpu.SemaphoreType.DMA
    anywhere = pl.BlockSpec(memory_space=pl.ANY)
    return pl.pallas_call(
        functools.partial(kernel, rows, cols, tile_rows, tile_cols, heads),
        out_shape=jax.ShapeDtypeStruct((tile_rows // 2, tile_cols // 2, 4 * width), BF16),
        in_specs=[anywhere] * 8,
        out_specs=anywhere,
        scratch_shapes=[
            pltpu.VMEM((3, width), F32),
            pltpu.VMEM((heads, tile_rows, tile_cols), F32),
            pltpu.VMEM((1, width), F32),
            pltpu.VMEM((1, width), F32),
            pltpu.VMEM((1, 4 * width), F32),
            pltpu.VMEM((1, 4 * width), F32),
            pltpu.VMEM((tile_rows // 2, tile_cols // 2, 4 * width), BF16),
            pltpu.VMEM((count, lanes), F32),
            pltpu.VMEM((PLANE, count, width), BF16),
            pltpu.VMEM((3, depth, PLANE, 2, w.shape[1] // 2, gw), BF16),
            pltpu.VMEM((PLANE, 3, count, width), BF16),
            pltpu.VMEM((3, count, width), BF16),
            pltpu.VMEM((heads, count, count), F32),
            pltpu.VMEM((PLANE, 2, count, width // 4), BF16),
            pltpu.VMEM((2, tile_rows, width // 4), BF16),
            pltpu.VMEM((2, tile_rows, width // 4), BF16),
            pltpu.VMEM((PLANE, tile_cols, width // 4), BF16),
            pltpu.VMEM((PLANE, tile_cols, width // 4), BF16),
            pltpu.VMEM((PLANE, 8, count), F32),
            pltpu.VMEM((PLANE, 8, count), F32),
            pltpu.VMEM((2, count, heads), F32),
            pltpu.VMEM((2, heads, count), F32),
            pltpu.VMEM((2, count, width), F32),
            pltpu.VMEM((8, width), F32),
            pltpu.VMEM((gp, 8, lanes), F32),
            pltpu.VMEM((depth, gp, 8, lanes), F32),
            pltpu.VMEM((2, pairs, hd, lanes), F32),
            pltpu.VMEM((2, pairs, hd, lanes), F32),
            pltpu.VMEM((3, pairs, 8, lanes), F32),
            pltpu.VMEM((2, gp, hd, lanes), BF16),
            pltpu.VMEM((depth, gp, hd, lanes), BF16),
            pltpu.VMEM((2, pairs, hd, lanes), F32),
            pltpu.VMEM((pairs, count, lanes), F32),
            pltpu.VMEM((PLANE, gp, count, lanes), BF16),
            pltpu.VMEM((PLANE, gp, count, lanes), BF16),
            pltpu.VMEM((2, count, lanes), F32),
            dma((6,)), dma((tile_rows // 2,)),
            dma, dma, dma((PIECES,)), dma, dma,
            dma, dma((3,)), dma((2,)), dma((2, depth)), dma((2,)),
            dma((PLANE, 2)), dma((PLANE, 2)), dma, dma,
            dma((2, PLANE)), dma((2, PLANE)),
            dma, dma, dma, dma, dma, dma, dma, dma((PLANE,)),
        ],
        compiler_params=pltpu.CompilerParams(
            collective_id=0, has_side_effects=True, vmem_limit_bytes=40 * 1024 * 1024),
    )(*[
        pltpu.with_memory_space_constraint(value, pltpu.MemorySpace.HBM)
        for value in (
            x.reshape(count, width), ratios, w, retention,
            credit.reshape(1, width), gain.reshape(1, width),
            scale.reshape(1, 4 * width), offset.reshape(1, 4 * width))
    ])


def solution(mesh):
    return jax.shard_map(
        body,
        mesh=mesh,
        in_specs=(
            P("row", "col", None),
            P(),
            P(None, "row", None),
            P(None, "row", "col"),
            P(),
            P(),
            P(),
            P(),
        ),
        out_specs=P("row", "col", None),
        check_vma=False,
    )
```

```python
import functools

import jax
import jax.numpy as jnp
from jax import lax
from jax.experimental import pallas as pl
from jax.experimental.pallas import tpu as pltpu
from jax.sharding import PartitionSpec as P

MESH = pl.DeviceIdType.MESH
F32 = jnp.float32
BF16 = jnp.bfloat16
HIGH = lax.Precision.HIGHEST
PLANE = 4
PIECES = 4
KV, R = slice(1, 3), slice(0, 1)


def iota(shape, dim):
    return lax.broadcasted_iota(jnp.int32, shape, dim)


def two_terms(value):
    first = value.astype(BF16)
    return first, (value - first.astype(F32)).astype(BF16)


def kernel(
    rows, cols, tile_rows, tile_cols, heads,
    x_ref, ratio_hbm, w_ref, ret_hbm, credit_hbm, gain_hbm, scale_hbm, offset_hbm,
    out_hbm,
    ratio_ref, ret_ref, credit_ref, gain_ref, scale_ref, offset_ref, out_ref, shift_t,
    xt, wf, mx, proj, decay, side, side_out, side_far, top_rows, bottom_rows, ret_out, rets, rows_t, rows_r, spread_t, log_t, plane_log, plane_logs,
    sums, before, decays_t, plane_sum, plane_sums, entering, block, sent, landed, stats,
    small_in, out_left, x_own, x_send, x_piece, x_near, x_far, w_own, w_send, w_plane, w_z, w_mate, side_send, side_recv, far_send, far_recv,
    edge_send, edge_recv, ret_send, ret_recv, log_send, log_recv, sum_send, sum_recv, out_send, out_recv,
):
    count, width = xt.shape[1:]
    hd = width // heads
    lanes = 2 * hd
    quarter = width // 4
    gw = width // PLANE
    gp = gw // lanes
    hp = heads // PLANE
    vp_count = PLANE * gp
    hs = w_ref.shape[1] // 2
    piece = count // PIECES
    row, col = lax.axis_index("row"), lax.axis_index("col")
    depth = rows // PLANE
    z, q = row // PLANE, row % PLANE
    bx, by = q % 2, q // 2
    half = col % 2
    mate = col + 1 - 2 * half
    q1 = (1 - half) * (q + 1 - 2 * bx) + half * (q + 2 - 4 * by)
    q2 = half * (q + 1 - 2 * bx) + (1 - half) * (q + 2 - 4 * by)
    q12 = PLANE - 1 - q
    base = z * PLANE
    first_row, second_row = base + q1, base + q2
    right, left = (col + 1) % cols, (col + cols - 1) % cols
    down_slot, up_slot = (q + 1) % PLANE, (q + PLANE - 1) % PLANE

    barrier = pltpu.get_barrier_semaphore()

    def greet(target):
        pl.semaphore_signal(barrier, inc=1, device_id=target, device_id_type=MESH)

    for o in range(1, depth):
        greet({"row": (z + o) % depth * PLANE + q})
    for o in range(1, PLANE):
        greet({"row": base + (q + o) % PLANE})
    for other in (right, left, mate):
        greet({"col": other})

    @pl.when(z > 0)
    def _():
        greet({"row": (base + rows - 1) % rows})

    @pl.when(z < depth - 1)
    def _():
        greet({"row": (base + PLANE) % rows})

    def local(src, dst, sem):
        return pltpu.make_async_copy(src, dst, sem)

    def remote(src, dst, send, recv, target):
        return pltpu.make_async_remote_copy(
            src, dst, send, recv, device_id=target, device_id_type=MESH)

    def arrive(ref, recv):
        remote(ref, ref, x_send, recv, {"col": mate}).wait_recv()

    def left_by(ref, send):
        remote(ref, ref, send, x_near, {"col": mate}).wait_send()

    my_rows = pl.ds(pl.multiple_of(half * hs, hs), hs)

    def my_cols(qq):
        return pl.ds(pl.multiple_of(qq * gw, gw), gw)

    small = [
        local(src, dst, small_in.at[k])
        for k, (src, dst) in enumerate((
            (ret_hbm, ret_ref), (ratio_hbm, ratio_ref), (credit_hbm, credit_ref), (gain_hbm, gain_ref),
            (scale_hbm, scale_ref), (offset_hbm, offset_ref)))
    ]
    for c in small:
        c.start()
    x_copy = local(x_ref, xt.at[q], x_own)
    w_copy = local(w_ref.at[:, my_rows, my_cols(q)], wf.at[:, z, q, half], w_own)
    w_copy.start()
    x_copy.start()
    top_source = x_ref.at[count - tile_cols:count, 2 * quarter:3 * quarter]
    bottom_source = x_ref.at[0:tile_cols, 3 * quarter:]
    small[0].wait()
    own_ret = jnp.concatenate([ret_ref[:, r, :] for r in range(tile_rows)], axis=1)
    for qq in range(PLANE):
        ret_out[qq, 0:hp] = own_ret[qq * hp:(qq + 1) * hp]

    expected = (
        depth + PLANE + 1
        + PLANE * ((q == PLANE - 1) & (z < depth - 1)).astype(jnp.int32)
        + PLANE * ((q == 0) & (z > 0)).astype(jnp.int32)
    )
    pl.semaphore_wait(barrier, expected)

    def weights_to_plane(which, k):
        for o in range(1, PLANE):
            qq = (q + o) % PLANE
            remote(
                w_ref.at[which, my_rows, my_cols(qq)], wf.at[which, z, q, half], w_send.at[0], w_plane.at[k],
                {"row": base + qq}).start()

    def side_copies(t, source):
        return [
            remote(source.at[:, 0:quarter], side.at[t, 0], side_send.at[t, 0], side_recv.at[t, 0], {"col": right}),
            remote(source.at[:, quarter:2 * quarter], side.at[t, 1], side_send.at[t, 1], side_recv.at[t, 1],
                   {"col": left}),
        ]

    def edges(act):
        @pl.when(q < PLANE - 1)
        def _():
            act(remote(top_source, top_rows.at[down_slot], edge_send.at[0, 0], edge_recv.at[0, down_slot],
                       {"row": base + q12}))

        @pl.when(q > 0)
        def _():
            act(remote(bottom_source, bottom_rows.at[up_slot], edge_send.at[1, 0], edge_recv.at[1, up_slot],
                       {"row": base + q12}))

        for qq in range(PLANE):
            @pl.when((q == PLANE - 1) & (z < depth - 1))
            def _():
                act(remote(top_source, top_rows.at[down_slot], edge_send.at[0, qq], edge_recv.at[0, down_slot],
                           {"row": (base + PLANE + qq) % rows}))

            @pl.when((q == 0) & (z > 0))
            def _():
                act(remote(bottom_source, bottom_rows.at[up_slot], edge_send.at[1, qq], edge_recv.at[1, up_slot],
                           {"row": (base + rows - PLANE + qq) % rows}))

    weights_to_plane(KV, 0)
    for o in range(1, PLANE):
        qq = (q + o) % PLANE
        remote(ret_out.at[qq], rets.at[q], ret_send, ret_recv, {"row": base + qq}).start()
    edges(lambda c: c.start())
    for c in side_copies(q, x_ref):
        c.start()
    for k in range(PIECES):
        part = slice(k * piece, (k + 1) * piece)
        remote(x_ref.at[part], xt.at[q, part], x_send, x_piece.at[k], {"row": first_row}).start()
    weights_to_plane(R, 1)

    def weights_to_mate(which, k, zz):
        here = wf.at[which, zz, :, half]
        remote(here, here, w_send.at[2], w_mate.at[k], {"col": mate}).start()

    def weights_along_z(which, k):
        arrive(wf.at[which, z, 0:PLANE - 1, half], w_plane.at[k])
        here = wf.at[which, z, :, half]
        for o in range(1, depth):
            remote(here, here, w_send.at[1], w_z.at[k, z], {"row": (z + o) % depth * PLANE + q}).start()
        weights_to_mate(which, k, z)

    def weights_from_z(which, k):
        for o in range(1, depth):
            zz = (z + o) % depth
            arrive(wf.at[which, zz, :, half], w_z.at[k, zz])
            weights_to_mate(which, k, zz)

    def weights_from_mate(which, k):
        arrive(wf.at[which, :, :, 1 - half], w_mate.at[k])

    w_copy.wait()
    weights_along_z(KV, 0)

    arrive(rets.at[0:PLANE - 1], ret_recv)
    remote(x_ref, xt.at[q], x_send, x_near, {"row": second_row}).start()
    rets[q] = ret_out[q]
    ret = jnp.concatenate([rets[t, 0:hp] for t in range(PLANE)], axis=0)
    tri = (iota((count, count), 0) >= iota((count, count), 1)).astype(F32)
    contract_last = (((1,), (1,)), ((), ()))
    running_c = lax.dot_general(tri, ret, contract_last, precision=HIGH, preferred_element_type=F32)
    running_r = lax.dot_general(ret, tri, contract_last, precision=HIGH, preferred_element_type=F32)
    eye = (iota((count, count), 0) == iota((count, count), 1)).astype(F32)
    ret_c = lax.dot_general(eye, ret, contract_last, precision=HIGH, preferred_element_type=F32)
    before_c = running_c - ret_c
    total_r = running_c[count - 1:count, :]
    rows_t[0] = running_c
    rows_t[1] = before_c
    rows_r[0] = running_r
    rows_r[1] = running_r - ret
    chosen = (iota((heads, width), 0) == iota((heads, width), 1) // hd).astype(F32)
    for k, table in enumerate((jnp.exp(total_r - running_c), jnp.exp(before_c))):
        spread_t[k] = jnp.dot(table, chosen, precision=HIGH, preferred_element_type=F32)
    log_t[...] = jnp.dot(jnp.broadcast_to(total_r, (8, heads)), chosen, precision=HIGH, preferred_element_type=F32)

    def log_of(vp):
        return log_t[:, vp * lanes:(vp + 1) * lanes]

    for j in range(gp):
        plane_log[j] = sum(log_of(t * gp + j) for t in range(PLANE))
    for o in range(1, depth):
        remote(plane_log, plane_logs.at[z], log_send, log_recv, {"row": (z + o) % depth * PLANE + q}).start()
    for j in range(gp):
        for t in range(PLANE):
            vp = t * gp + j
            zero = jnp.zeros((8, lanes), F32)
            decays_t[0, vp] = jnp.exp(log_of(vp))
            decays_t[1, vp] = jnp.exp(sum((log_of(s * gp + j) for s in range(t)), zero))
            decays_t[2, vp] = jnp.exp(sum((log_of(s * gp + j) for s in range(t + 1, PLANE)), zero))

    def picked(table, h):
        return jnp.sum(jnp.where(iota(table.shape, 1) == h, table, 0.0), axis=1, keepdims=True)

    def picked_row(table, h):
        return jnp.sum(jnp.where(iota(table.shape, 0) == h, table, 0.0), axis=0, keepdims=True)

    earlier = iota((count, count), 0) > iota((count, count), 1)
    diagonal = iota((count, count), 0) == iota((count, count), 1)

    def pair_decays(h, carry):
        rc, bc = picked(rows_t[0], h), picked(rows_t[1], h)
        rr, br = picked_row(rows_r[0], h), picked_row(rows_r[1], h)
        exponent = jnp.where(earlier, bc - rr, br - rc)
        decay[h] = jnp.where(diagonal, 0.0, jnp.exp(exponent))
        return carry

    def some_decays(part):
        lax.fori_loop(part * heads // 4, (part + 1) * heads // 4, pair_decays, 0)

    def forward(k):
        part = slice(k * piece, (k + 1) * piece)
        here = xt.at[q1, part]
        arrive(here, x_piece.at[k])
        remote(here, here, x_send, x_far, {"row": second_row}).start()

    def sides_out(t):
        for c in side_copies(t, xt.at[t]):
            c.start()

    def edges_in():
        @pl.when(z > 0)
        def _():
            arrive(top_rows.at[0], edge_recv.at[0, 0])

        @pl.when(z < depth - 1)
        def _():
            arrive(bottom_rows.at[PLANE - 1], edge_recv.at[1, PLANE - 1])

        @pl.when(q12 < PLANE - 1)
        def _():
            arrive(top_rows.at[0], edge_recv.at[0, (q12 + 1) % PLANE])

        @pl.when(q12 > 0)
        def _():
            arrive(bottom_rows.at[0], edge_recv.at[1, (q12 + PLANE - 1) % PLANE])

    place_in_row = iota((count, quarter), 0) % tile_cols
    last = tile_cols - 1

    def far_sides_out():
        for c in side_copies(q, x_ref):
            c.wait_recv()
        token, line = iota((tile_rows, count), 1), iota((tile_rows, count), 0) * tile_cols
        for k in range(2):
            pick = (token == line + (last if k == 0 else 0)).astype(BF16)
            side_out[k] = jnp.dot(pick, side[q, k], preferred_element_type=F32).astype(BF16)
        remote(side_out, side_far, far_send, far_recv, {"row": base + q12}).start()

    def mix(t, kind):
        x0 = xt[t, :, 0:quarter].astype(F32)
        x1 = xt[t, :, quarter:2 * quarter].astype(F32)
        if kind == "far":
            arrive(side_far, far_recv)
            token, line = iota((count, tile_rows), 0), iota((count, tile_rows), 1) * tile_cols
            side0, side1 = [
                jnp.dot((token == line + (0 if k == 0 else last)).astype(BF16), side_far[k],
                        preferred_element_type=F32)
                for k in range(2)
            ]
        else:
            if kind == "near":
                for c in side_copies(t, xt.at[t]):
                    c.wait_recv()
            side0 = pltpu.roll(side[t, 0].astype(F32), count - last, 0)
            side1 = pltpu.roll(side[t, 1].astype(F32), last, 0)
        side0 = jnp.where(col > 0, side0, 0.0)
        side1 = jnp.where(col < cols - 1, side1, 0.0)
        up_t, down_t = (t + PLANE - 1) % PLANE, (t + 1) % PLANE
        up_sent, down_sent = (t == 0) | (up_t == q12), (t == PLANE - 1) | (down_t == q12)
        up_t, down_t = jnp.where(up_sent, t, up_t), jnp.where(down_sent, t, down_t)
        above = xt[up_t, count - tile_cols:count, 2 * quarter:3 * quarter].astype(F32)
        below = xt[down_t, 0:tile_cols, 3 * quarter:].astype(F32)
        top = jnp.where(base + t > 0, jnp.where(up_sent, top_rows[t].astype(F32), above), 0.0)
        bottom = jnp.where(base + t < rows - 1, jnp.where(down_sent, bottom_rows[t].astype(F32), below), 0.0)
        shifted = [
            jnp.where(place_in_row == 0, side0, pltpu.roll(x0, 1, 0)),
            jnp.where(place_in_row == last, side1, pltpu.roll(x1, count - 1, 0)),
            jnp.concatenate([top, xt[t, 0:count - tile_cols, 2 * quarter:3 * quarter].astype(F32)], axis=0),
            jnp.concatenate([xt[t, tile_cols:count, 3 * quarter:].astype(F32), bottom], axis=0),
        ]
        for part in range(4):
            span = slice(part * quarter, (part + 1) * quarter)
            xs = xt[t, :, span].astype(F32)
            for p in range(3):
                c = ratio_ref[p:p + 1, span]
                mx[t, p, :, span] = (xs * c + shifted[part] * (1.0 - c)).astype(BF16)

    def project(p, t):
        proj[p, :, my_cols(t)] = jnp.dot(
            mx[t, p], wf[p].reshape(width, gw), preferred_element_type=F32).astype(BF16)

    low = iota((count, lanes), 1) < hd
    low_u = iota((hd, lanes), 1) < hd
    same_head = (iota((2 * lanes, lanes), 0) % lanes // hd == iota((2 * lanes, lanes), 1) // hd).astype(BF16)

    def halves(value):
        return jnp.dot(jnp.concatenate(two_terms(value), axis=1), same_head, preferred_element_type=F32)

    def span_of(i):
        return pl.ds(pl.multiple_of(i * lanes, lanes), lanes)

    def local_states(t):
        def one(j, carry):
            vp = t * gp + j
            span = span_of(vp)
            k = proj[1, :, span].astype(F32)
            v = proj[2, :, span]
            kd = jnp.concatenate([k * spread_t[0, :, span], k * spread_t[1, :, span]], axis=1).astype(BF16)
            m = lax.dot_general(kd, v, (((0,), (0,)), ((), ())), preferred_element_type=F32)
            sums[0, vp] = jnp.where(low_u, m[0:hd], m[hd:2 * hd])
            sums[1, vp] = jnp.where(low_u, m[2 * hd:3 * hd], m[3 * hd:])
            return carry

        lax.fori_loop(0, gp, one, 0, unroll=True)

    def keys_values(t):
        project(1, t)
        project(2, t)
        local_states(t)

    def planes_out():
        for j in range(gp):
            for d, order in ((0, range(PLANE)), (1, range(PLANE - 1, -1, -1))):
                state = jnp.zeros((hd, lanes), F32)
                for t in order:
                    vp = t * gp + j
                    before[d, vp] = state
                    state = decays_t[0, vp][0:1, :] * state + sums[d, vp]
                plane_sum[d, j] = state.astype(BF16)
        for o in range(1, depth):
            zz = (z + o) % depth
            remote(
                plane_sum.at[(zz < z).astype(jnp.int32)], plane_sums.at[z], sum_send, sum_recv,
                {"row": zz * PLANE + q}).start()

    def planes_in():
        arrive(plane_logs.at[0:depth - 1], log_recv)
        arrive(plane_sums.at[0:depth - 1], sum_recv)
        for j in range(gp):
            def one(i, carry):
                fwd, bwd = carry
                back = depth - 1 - i
                fwd = jnp.where(
                    i < z, jnp.exp(plane_logs[i, j][0:1, :]) * fwd + plane_sums[i, j].astype(F32), fwd)
                bwd = jnp.where(
                    back > z, jnp.exp(plane_logs[back, j][0:1, :]) * bwd + plane_sums[back, j].astype(F32), bwd)
                return fwd, bwd

            start = jnp.zeros((hd, lanes), F32)
            reached = lax.fori_loop(0, depth, one, (start, start), unroll=True if depth <= 4 else 1)
            for t in range(PLANE):
                vp = t * gp + j
                for d in range(2):
                    entering[d, vp] = before[d, vp] + decays_t[1 + d, vp][0:1, :] * reached[d]

    def channels(j):
        return pl.ds(pl.multiple_of(q * gw + j * lanes, lanes), lanes)

    def local_mix(t):
        def one(j, carry):
            vp = t * gp + j
            span = span_of(vp)
            r, k, v = proj[0, :, span], proj[1, :, span], proj[2, :, span]
            outs = []
            for s in range(2):
                rs = jnp.where(low if s == 0 else jnp.logical_not(low), r.astype(F32), 0.0).astype(BF16)
                scores = lax.dot_general(rs, k, contract_last, preferred_element_type=F32)
                weight = (scores * decay[2 * vp + s]).astype(BF16)
                outs.append(jnp.dot(weight, v, preferred_element_type=F32))
            own_term = halves(r.astype(F32) * credit_ref[:, channels(j)] * k.astype(F32)) * v.astype(F32)
            block[vp] = jnp.where(low, outs[0], outs[1]) + own_term
            return carry

        lax.fori_loop(0, gp, one, 0)

    def finish(t, dst, send=None):
        def one(j, carry):
            vp = t * gp + j
            span = span_of(vp)
            r = proj[0, :, span]
            fwd, bwd = [
                jnp.concatenate(
                    [jnp.where(low_u, entering[d, vp], 0.0), jnp.where(low_u, 0.0, entering[d, vp])], axis=0
                ).astype(BF16)
                for d in range(2)
            ]
            wkv = (
                block[vp]
                + spread_t[1, :, span] * jnp.dot(r, fwd, preferred_element_type=F32)
                + spread_t[0, :, span] * jnp.dot(r, bwd, preferred_element_type=F32)
            )
            centred = wkv - halves(wkv) * (1.0 / hd)
            variance = halves(centred * centred) * (1.0 / hd)
            normed = centred * lax.rsqrt(variance + 1e-05) * gain_ref[:, channels(j)]
            dst[t, j] = normed.astype(BF16)
            if send is not None:
                send(t, j)
            return carry

        lax.fori_loop(0, gp, one, 0, unroll=True)

    def finish_and_send(t):
        finish(t, sent, lambda t, j: remote(
            sent.at[t, j], landed.at[q, j], out_send, out_recv.at[q], {"row": base + t}).start())

    group = (
        (iota((count, count), 0) // (2 * tile_cols) == iota((count, count), 1) // (2 * tile_cols))
        & (iota((count, count), 0) % tile_cols // 2 == iota((count, count), 1) % tile_cols // 2)
    ).astype(BF16)

    def over_group(values):
        terms = []
        for value in values:
            terms.extend(two_terms(jnp.broadcast_to(jnp.sum(value, axis=1, keepdims=True), (count, lanes))))
        both = jnp.dot(group, jnp.concatenate(terms, axis=1), preferred_element_type=F32) * (1.0 / (4 * width))
        return [
            both[:, 2 * k * lanes:(2 * k + 1) * lanes] + both[:, (2 * k + 1) * lanes:(2 * k + 2) * lanes]
            for k in range(len(values))
        ]

    none = jnp.zeros((count, lanes), F32)

    def mean_of_x():
        total = none
        for i in range(vp_count):
            total = total + xt[q, :, i * lanes:(i + 1) * lanes].astype(F32)
        shift_t[...] = over_group([total])[0]

    def add_up(t, carry):
        def one(j, carry):
            first, second = carry
            i = t * gp + j
            made = xt[q, :, span_of(i)].astype(F32) - shift_t[...] + landed[t, j].astype(F32)
            block[i] = made
            return first + made, second + made * made

        return lax.fori_loop(0, gp, one, carry, unroll=True)

    for c in small[1:]:
        c.wait()

    far_sides_out()
    some_decays(0)
    x_copy.wait()
    mean_of_x()
    edges_in()
    some_decays(1)
    forward(0)
    forward(1)
    some_decays(2)
    forward(2)
    some_decays(3)
    forward(3)
    sides_out(q1)
    arrive(xt.at[q2], x_near)
    sides_out(q2)
    weights_from_z(KV, 0)
    weights_along_z(R, 1)
    mix(q, "own")
    mix(q1, "near")
    mix(q2, "near")
    weights_from_mate(KV, 0)
    keys_values(q)
    keys_values(q1)
    keys_values(q2)
    arrive(xt.at[q12], x_far)
    mix(q12, "far")
    keys_values(q12)
    planes_out()
    weights_from_z(R, 1)
    weights_from_mate(R, 1)
    project(0, q1)
    local_mix(q1)
    project(0, q2)
    local_mix(q2)
    planes_in()
    finish_and_send(q1)
    finish_and_send(q2)
    project(0, q12)
    local_mix(q12)
    finish_and_send(q12)
    project(0, q)
    local_mix(q)
    finish(q, landed)
    carry = add_up(q, (none, none))
    for t in (q1, q2, q12):
        arrive(landed.at[t], out_recv.at[t])
        carry = add_up(t, carry)

    mean, square = over_group(carry)
    stats[0] = mean
    stats[1] = lax.rsqrt(jnp.maximum(square - mean * mean, 0.0) + 1e-05)
    half_cols = tile_cols // 2
    outs = []
    for a in range(tile_rows // 2):
        def emit(i, carry):
            for part in range(4):
                span = pl.ds(pl.multiple_of(part * width + i * lanes, lanes), lanes)
                take = pl.ds((2 * a + part % 2) * tile_cols + part // 2, half_cols, stride=2)
                value = (block[i, take, :] - stats[0, take, :]) * stats[1, take, :]
                out_ref[a, :, span] = (value * scale_ref[:, span] + offset_ref[:, span]).astype(BF16)
            return carry

        lax.fori_loop(0, vp_count, emit, 0, unroll=4)
        outs.append(local(out_ref.at[a], out_hbm.at[a], out_left.at[a]))
        outs[-1].start()

    left_by(xt.at[0:3], x_send)
    left_by(wf.at[:, z, 0:PLANE - 1, half], w_send.at[0])
    left_by(wf.at[:, 0:depth - 1, :, half], w_send.at[1])
    left_by(wf.at[:, :, :, half], w_send.at[2])
    left_by(rets.at[0:PLANE - 1], ret_send)
    left_by(plane_logs.at[0:depth - 1], log_send)
    left_by(plane_sums.at[0:depth - 1], sum_send)
    left_by(sent.at[0:PLANE - 1], out_send)
    edges(lambda c: c.wait_send())
    for t in (q, q1, q2):
        for c in side_copies(t, xt.at[t]):
            c.wait_send()
    left_by(side_out, far_send)
    for c in outs:
        c.wait()


def body(x, ratios, w, retention, credit, gain, scale, offset):
    tile_rows, tile_cols, width = x.shape
    heads = retention.shape[0]
    count = tile_rows * tile_cols
    hd = width // heads
    rows, cols = lax.axis_size("row"), lax.axis_size("col")
    depth = rows // PLANE
    pairs = heads // 2
    lanes = 2 * hd
    gw = width // PLANE
    gp = gw // lanes
    dma = pltpu.SemaphoreType.DMA
    anywhere = pl.BlockSpec(memory_space=pl.ANY)
    return pl.pallas_call(
        functools.partial(kernel, rows, cols, tile_rows, tile_cols, heads),
        out_shape=jax.ShapeDtypeStruct((tile_rows // 2, tile_cols // 2, 4 * width), BF16),
        in_specs=[anywhere] * 8,
        out_specs=anywhere,
        scratch_shapes=[
            pltpu.VMEM((3, width), F32),
            pltpu.VMEM((heads, tile_rows, tile_cols), F32),
            pltpu.VMEM((1, width), F32),
            pltpu.VMEM((1, width), F32),
            pltpu.VMEM((1, 4 * width), F32),
            pltpu.VMEM((1, 4 * width), F32),
            pltpu.VMEM((tile_rows // 2, tile_cols // 2, 4 * width), BF16),
            pltpu.VMEM((count, lanes), F32),
            pltpu.VMEM((PLANE, count, width), BF16),
            pltpu.VMEM((3, depth, PLANE, 2, w.shape[1] // 2, gw), BF16),
            pltpu.VMEM((PLANE, 3, count, width), BF16),
            pltpu.VMEM((3, count, width), BF16),
            pltpu.VMEM((heads, count, count), F32),
            pltpu.VMEM((PLANE, 2, count, width // 4), BF16),
            pltpu.VMEM((2, tile_rows, width // 4), BF16),
            pltpu.VMEM((2, tile_rows, width // 4), BF16),
            pltpu.VMEM((PLANE, tile_cols, width // 4), BF16),
            pltpu.VMEM((PLANE, tile_cols, width // 4), BF16),
            pltpu.VMEM((PLANE, 8, count), F32),
            pltpu.VMEM((PLANE, 8, count), F32),
            pltpu.VMEM((2, count, heads), F32),
            pltpu.VMEM((2, heads, count), F32),
            pltpu.VMEM((2, count, width), F32),
            pltpu.VMEM((8, width), F32),
            pltpu.VMEM((gp, 8, lanes), F32),
            pltpu.VMEM((depth, gp, 8, lanes), F32),
            pltpu.VMEM((2, pairs, hd, lanes), F32),
            pltpu.VMEM((2, pairs, hd, lanes), F32),
            pltpu.VMEM((3, pairs, 8, lanes), F32),
            pltpu.VMEM((2, gp, hd, lanes), BF16),
            pltpu.VMEM((depth, gp, hd, lanes), BF16),
            pltpu.VMEM((2, pairs, hd, lanes), F32),
            pltpu.VMEM((pairs, count, lanes), F32),
            pltpu.VMEM((PLANE, gp, count, lanes), BF16),
            pltpu.VMEM((PLANE, gp, count, lanes), BF16),
            pltpu.VMEM((2, count, lanes), F32),
            dma((6,)), dma((tile_rows // 2,)),
            dma, dma, dma((PIECES,)), dma, dma,
            dma, dma((3,)), dma((2,)), dma((2, depth)), dma((2,)),
            dma((PLANE, 2)), dma((PLANE, 2)), dma, dma,
            dma((2, PLANE)), dma((2, PLANE)),
            dma, dma, dma, dma, dma, dma, dma, dma((PLANE,)),
        ],
        compiler_params=pltpu.CompilerParams(
            collective_id=0, has_side_effects=True, vmem_limit_bytes=40 * 1024 * 1024),
    )(*[
        pltpu.with_memory_space_constraint(value, pltpu.MemorySpace.HBM)
        for value in (
            x.reshape(count, width), ratios, w, retention,
            credit.reshape(1, width), gain.reshape(1, width),
            scale.reshape(1, 4 * width), offset.reshape(1, 4 * width))
    ])


def solution(mesh):
    return jax.shard_map(
        body,
        mesh=mesh,
        in_specs=(
            P("row", "col", None),
            P(),
            P(None, "row", None),
            P(None, "row", "col"),
            P(),
            P(),
            P(),
            P(),
        ),
        out_specs=P("row", "col", None),
        check_vma=False,
    )
```

```python
import functools

import jax
import jax.numpy as jnp
from jax import lax
from jax.experimental import pallas as pl
from jax.experimental.pallas import tpu as pltpu
from jax.sharding import PartitionSpec as P

MESH = pl.DeviceIdType.MESH
F32 = jnp.float32
BF16 = jnp.bfloat16
HIGH = lax.Precision.HIGHEST
PLANE = 4
PIECES = 4
KV, R = slice(1, 3), slice(0, 1)


def iota(shape, dim):
    return lax.broadcasted_iota(jnp.int32, shape, dim)


def two_terms(value):
    first = value.astype(BF16)
    return first, (value - first.astype(F32)).astype(BF16)


def kernel(
    rows, cols, tile_rows, tile_cols, heads,
    x_ref, ratio_hbm, w_ref, ret_hbm, credit_hbm, gain_hbm, scale_hbm, offset_hbm,
    out_ref,
    ratio_ref, ret_ref, credit_ref, gain_ref, scale_ref, offset_ref, shift_t,
    xt, wf, mx, proj, decay, side, side_out, side_far, top_rows, bottom_rows, ret_out, rets, rows_t, rows_r, spread_t, log_t, plane_log, plane_logs,
    sums, before, decays_t, plane_sum, plane_sums, entering, block, sent, landed, stats,
    small_in, x_own, x_send, x_piece, x_near, x_far, w_own, w_send, w_plane, w_z, w_mate, side_send, side_recv, far_send, far_recv,
    edge_send, edge_recv, ret_send, ret_recv, log_send, log_recv, sum_send, sum_recv, out_send, out_recv,
):
    count, width = xt.shape[1:]
    hd = width // heads
    lanes = 2 * hd
    quarter = width // 4
    gw = width // PLANE
    gp = gw // lanes
    hp = heads // PLANE
    vp_count = PLANE * gp
    hs = w_ref.shape[1] // 2
    piece = count // PIECES
    row, col = lax.axis_index("row"), lax.axis_index("col")
    depth = rows // PLANE
    z, q = row // PLANE, row % PLANE
    bx, by = q % 2, q // 2
    half = col % 2
    mate = col + 1 - 2 * half
    q1 = (1 - half) * (q + 1 - 2 * bx) + half * (q + 2 - 4 * by)
    q2 = half * (q + 1 - 2 * bx) + (1 - half) * (q + 2 - 4 * by)
    q12 = PLANE - 1 - q
    base = z * PLANE
    first_row, second_row = base + q1, base + q2
    right, left = (col + 1) % cols, (col + cols - 1) % cols
    down_slot, up_slot = (q + 1) % PLANE, (q + PLANE - 1) % PLANE

    barrier = pltpu.get_barrier_semaphore()

    def greet(target):
        pl.semaphore_signal(barrier, inc=1, device_id=target, device_id_type=MESH)

    for o in range(1, depth):
        greet({"row": (z + o) % depth * PLANE + q})
    for o in range(1, PLANE):
        greet({"row": base + (q + o) % PLANE})
    for other in (right, left, mate):
        greet({"col": other})

    @pl.when(z > 0)
    def _():
        greet({"row": (base + rows - 1) % rows})

    @pl.when(z < depth - 1)
    def _():
        greet({"row": (base + PLANE) % rows})

    def local(src, dst, sem):
        return pltpu.make_async_copy(src, dst, sem)

    def remote(src, dst, send, recv, target):
        return pltpu.make_async_remote_copy(
            src, dst, send, recv, device_id=target, device_id_type=MESH)

    def arrive(ref, recv):
        remote(ref, ref, x_send, recv, {"col": mate}).wait_recv()

    def left_by(ref, send):
        remote(ref, ref, send, x_near, {"col": mate}).wait_send()

    my_rows = pl.ds(pl.multiple_of(half * hs, hs), hs)

    def my_cols(qq):
        return pl.ds(pl.multiple_of(qq * gw, gw), gw)

    small = [
        local(src, dst, small_in.at[k])
        for k, (src, dst) in enumerate((
            (ret_hbm, ret_ref), (ratio_hbm, ratio_ref), (credit_hbm, credit_ref), (gain_hbm, gain_ref),
            (scale_hbm, scale_ref), (offset_hbm, offset_ref)))
    ]
    for c in small:
        c.start()
    x_copy = local(x_ref, xt.at[q], x_own)
    w_copy = local(w_ref.at[:, my_rows, my_cols(q)], wf.at[:, z, q, half], w_own)
    w_copy.start()
    x_copy.start()
    top_source = x_ref.at[count - tile_cols:count, 2 * quarter:3 * quarter]
    bottom_source = x_ref.at[0:tile_cols, 3 * quarter:]
    small[0].wait()
    own_ret = jnp.concatenate([ret_ref[:, r, :] for r in range(tile_rows)], axis=1)
    for qq in range(PLANE):
        ret_out[qq, 0:hp] = own_ret[qq * hp:(qq + 1) * hp]

    expected = (
        depth + PLANE + 1
        + PLANE * ((q == PLANE - 1) & (z < depth - 1)).astype(jnp.int32)
        + PLANE * ((q == 0) & (z > 0)).astype(jnp.int32)
    )
    pl.semaphore_wait(barrier, expected)

    def weights_to_plane(which, k):
        for o in range(1, PLANE):
            qq = (q + o) % PLANE
            remote(
                w_ref.at[which, my_rows, my_cols(qq)], wf.at[which, z, q, half], w_send.at[0], w_plane.at[k],
                {"row": base + qq}).start()

    def side_copies(t, source):
        return [
            remote(source.at[:, 0:quarter], side.at[t, 0], side_send.at[t, 0], side_recv.at[t, 0], {"col": right}),
            remote(source.at[:, quarter:2 * quarter], side.at[t, 1], side_send.at[t, 1], side_recv.at[t, 1],
                   {"col": left}),
        ]

    def edges(act):
        @pl.when(q < PLANE - 1)
        def _():
            act(remote(top_source, top_rows.at[down_slot], edge_send.at[0, 0], edge_recv.at[0, down_slot],
                       {"row": base + q12}))

        @pl.when(q > 0)
        def _():
            act(remote(bottom_source, bottom_rows.at[up_slot], edge_send.at[1, 0], edge_recv.at[1, up_slot],
                       {"row": base + q12}))

        for qq in range(PLANE):
            @pl.when((q == PLANE - 1) & (z < depth - 1))
            def _():
                act(remote(top_source, top_rows.at[down_slot], edge_send.at[0, qq], edge_recv.at[0, down_slot],
                           {"row": (base + PLANE + qq) % rows}))

            @pl.when((q == 0) & (z > 0))
            def _():
                act(remote(bottom_source, bottom_rows.at[up_slot], edge_send.at[1, qq], edge_recv.at[1, up_slot],
                           {"row": (base + rows - PLANE + qq) % rows}))

    weights_to_plane(KV, 0)
    for o in range(1, PLANE):
        qq = (q + o) % PLANE
        remote(ret_out.at[qq], rets.at[q], ret_send, ret_recv, {"row": base + qq}).start()
    edges(lambda c: c.start())
    for c in side_copies(q, x_ref):
        c.start()
    for k in range(PIECES):
        part = slice(k * piece, (k + 1) * piece)
        remote(x_ref.at[part], xt.at[q, part], x_send, x_piece.at[k], {"row": first_row}).start()
    weights_to_plane(R, 1)

    def weights_to_mate(which, k, zz):
        here = wf.at[which, zz, :, half]
        remote(here, here, w_send.at[2], w_mate.at[k], {"col": mate}).start()

    def weights_along_z(which, k):
        arrive(wf.at[which, z, 0:PLANE - 1, half], w_plane.at[k])
        here = wf.at[which, z, :, half]
        for o in range(1, depth):
            remote(here, here, w_send.at[1], w_z.at[k, z], {"row": (z + o) % depth * PLANE + q}).start()
        weights_to_mate(which, k, z)

    def weights_from_z(which, k):
        for o in range(1, depth):
            zz = (z + o) % depth
            arrive(wf.at[which, zz, :, half], w_z.at[k, zz])
            weights_to_mate(which, k, zz)

    def weights_from_mate(which, k):
        arrive(wf.at[which, :, :, 1 - half], w_mate.at[k])

    w_copy.wait()
    weights_along_z(KV, 0)

    arrive(rets.at[0:PLANE - 1], ret_recv)
    remote(x_ref, xt.at[q], x_send, x_near, {"row": second_row}).start()
    rets[q] = ret_out[q]
    ret = jnp.concatenate([rets[t, 0:hp] for t in range(PLANE)], axis=0)
    tri = (iota((count, count), 0) >= iota((count, count), 1)).astype(F32)
    contract_last = (((1,), (1,)), ((), ()))
    running_c = lax.dot_general(tri, ret, contract_last, precision=HIGH, preferred_element_type=F32)
    running_r = lax.dot_general(ret, tri, contract_last, precision=HIGH, preferred_element_type=F32)
    eye = (iota((count, count), 0) == iota((count, count), 1)).astype(F32)
    ret_c = lax.dot_general(eye, ret, contract_last, precision=HIGH, preferred_element_type=F32)
    before_c = running_c - ret_c
    total_r = running_c[count - 1:count, :]
    rows_t[0] = running_c
    rows_t[1] = before_c
    rows_r[0] = running_r
    rows_r[1] = running_r - ret
    chosen = (iota((heads, width), 0) == iota((heads, width), 1) // hd).astype(F32)
    for k, table in enumerate((jnp.exp(total_r - running_c), jnp.exp(before_c))):
        spread_t[k] = jnp.dot(table, chosen, precision=HIGH, preferred_element_type=F32)
    log_t[...] = jnp.dot(jnp.broadcast_to(total_r, (8, heads)), chosen, precision=HIGH, preferred_element_type=F32)

    def log_of(vp):
        return log_t[:, vp * lanes:(vp + 1) * lanes]

    for j in range(gp):
        plane_log[j] = sum(log_of(t * gp + j) for t in range(PLANE))
    for o in range(1, depth):
        remote(plane_log, plane_logs.at[z], log_send, log_recv, {"row": (z + o) % depth * PLANE + q}).start()
    for j in range(gp):
        for t in range(PLANE):
            vp = t * gp + j
            zero = jnp.zeros((8, lanes), F32)
            decays_t[0, vp] = jnp.exp(log_of(vp))
            decays_t[1, vp] = jnp.exp(sum((log_of(s * gp + j) for s in range(t)), zero))
            decays_t[2, vp] = jnp.exp(sum((log_of(s * gp + j) for s in range(t + 1, PLANE)), zero))

    def picked(table, h):
        return jnp.sum(jnp.where(iota(table.shape, 1) == h, table, 0.0), axis=1, keepdims=True)

    def picked_row(table, h):
        return jnp.sum(jnp.where(iota(table.shape, 0) == h, table, 0.0), axis=0, keepdims=True)

    earlier = iota((count, count), 0) > iota((count, count), 1)
    diagonal = iota((count, count), 0) == iota((count, count), 1)

    def pair_decays(h, carry):
        rc, bc = picked(rows_t[0], h), picked(rows_t[1], h)
        rr, br = picked_row(rows_r[0], h), picked_row(rows_r[1], h)
        exponent = jnp.where(earlier, bc - rr, br - rc)
        decay[h] = jnp.where(diagonal, 0.0, jnp.exp(exponent))
        return carry

    def some_decays(part):
        lax.fori_loop(part * heads // 4, (part + 1) * heads // 4, pair_decays, 0)

    def forward(k):
        part = slice(k * piece, (k + 1) * piece)
        here = xt.at[q1, part]
        arrive(here, x_piece.at[k])
        remote(here, here, x_send, x_far, {"row": second_row}).start()

    def sides_out(t):
        for c in side_copies(t, xt.at[t]):
            c.start()

    def edges_in():
        @pl.when(z > 0)
        def _():
            arrive(top_rows.at[0], edge_recv.at[0, 0])

        @pl.when(z < depth - 1)
        def _():
            arrive(bottom_rows.at[PLANE - 1], edge_recv.at[1, PLANE - 1])

        @pl.when(q12 < PLANE - 1)
        def _():
            arrive(top_rows.at[0], edge_recv.at[0, (q12 + 1) % PLANE])

        @pl.when(q12 > 0)
        def _():
            arrive(bottom_rows.at[0], edge_recv.at[1, (q12 + PLANE - 1) % PLANE])

    place_in_row = iota((count, quarter), 0) % tile_cols
    last = tile_cols - 1

    def far_sides_out():
        for c in side_copies(q, x_ref):
            c.wait_recv()
        token, line = iota((tile_rows, count), 1), iota((tile_rows, count), 0) * tile_cols
        for k in range(2):
            pick = (token == line + (last if k == 0 else 0)).astype(BF16)
            side_out[k] = jnp.dot(pick, side[q, k], preferred_element_type=F32).astype(BF16)
        remote(side_out, side_far, far_send, far_recv, {"row": base + q12}).start()

    def mix(t, kind):
        x0 = xt[t, :, 0:quarter].astype(F32)
        x1 = xt[t, :, quarter:2 * quarter].astype(F32)
        if kind == "far":
            arrive(side_far, far_recv)
            token, line = iota((count, tile_rows), 0), iota((count, tile_rows), 1) * tile_cols
            side0, side1 = [
                jnp.dot((token == line + (0 if k == 0 else last)).astype(BF16), side_far[k],
                        preferred_element_type=F32)
                for k in range(2)
            ]
        else:
            if kind == "near":
                for c in side_copies(t, xt.at[t]):
                    c.wait_recv()
            side0 = pltpu.roll(side[t, 0].astype(F32), count - last, 0)
            side1 = pltpu.roll(side[t, 1].astype(F32), last, 0)
        side0 = jnp.where(col > 0, side0, 0.0)
        side1 = jnp.where(col < cols - 1, side1, 0.0)
        up_t, down_t = (t + PLANE - 1) % PLANE, (t + 1) % PLANE
        up_sent, down_sent = (t == 0) | (up_t == q12), (t == PLANE - 1) | (down_t == q12)
        up_t, down_t = jnp.where(up_sent, t, up_t), jnp.where(down_sent, t, down_t)
        above = xt[up_t, count - tile_cols:count, 2 * quarter:3 * quarter].astype(F32)
        below = xt[down_t, 0:tile_cols, 3 * quarter:].astype(F32)
        top = jnp.where(base + t > 0, jnp.where(up_sent, top_rows[t].astype(F32), above), 0.0)
        bottom = jnp.where(base + t < rows - 1, jnp.where(down_sent, bottom_rows[t].astype(F32), below), 0.0)
        shifted = [
            jnp.where(place_in_row == 0, side0, pltpu.roll(x0, 1, 0)),
            jnp.where(place_in_row == last, side1, pltpu.roll(x1, count - 1, 0)),
            jnp.concatenate([top, xt[t, 0:count - tile_cols, 2 * quarter:3 * quarter].astype(F32)], axis=0),
            jnp.concatenate([xt[t, tile_cols:count, 3 * quarter:].astype(F32), bottom], axis=0),
        ]
        for part in range(4):
            span = slice(part * quarter, (part + 1) * quarter)
            xs = xt[t, :, span].astype(F32)
            for p in range(3):
                c = ratio_ref[p:p + 1, span]
                mx[t, p, :, span] = (xs * c + shifted[part] * (1.0 - c)).astype(BF16)

    def project(p, t):
        proj[p, :, my_cols(t)] = jnp.dot(
            mx[t, p], wf[p].reshape(width, gw), preferred_element_type=F32).astype(BF16)

    low = iota((count, lanes), 1) < hd
    low_u = iota((hd, lanes), 1) < hd
    same_head = (iota((2 * lanes, lanes), 0) % lanes // hd == iota((2 * lanes, lanes), 1) // hd).astype(BF16)

    def halves(value):
        return jnp.dot(jnp.concatenate(two_terms(value), axis=1), same_head, preferred_element_type=F32)

    def span_of(i):
        return pl.ds(pl.multiple_of(i * lanes, lanes), lanes)

    def local_states(t):
        def one(j, carry):
            vp = t * gp + j
            span = span_of(vp)
            k = proj[1, :, span].astype(F32)
            v = proj[2, :, span]
            kd = jnp.concatenate([k * spread_t[0, :, span], k * spread_t[1, :, span]], axis=1).astype(BF16)
            m = lax.dot_general(kd, v, (((0,), (0,)), ((), ())), preferred_element_type=F32)
            sums[0, vp] = jnp.where(low_u, m[0:hd], m[hd:2 * hd])
            sums[1, vp] = jnp.where(low_u, m[2 * hd:3 * hd], m[3 * hd:])
            return carry

        lax.fori_loop(0, gp, one, 0, unroll=True)

    def keys_values(t):
        project(1, t)
        project(2, t)
        local_states(t)

    def planes_out():
        for j in range(gp):
            for d, order in ((0, range(PLANE)), (1, range(PLANE - 1, -1, -1))):
                state = jnp.zeros((hd, lanes), F32)
                for t in order:
                    vp = t * gp + j
                    before[d, vp] = state
                    state = decays_t[0, vp][0:1, :] * state + sums[d, vp]
                plane_sum[d, j] = state.astype(BF16)
        for o in range(1, depth):
            zz = (z + o) % depth
            remote(
                plane_sum.at[(zz < z).astype(jnp.int32)], plane_sums.at[z], sum_send, sum_recv,
                {"row": zz * PLANE + q}).start()

    def planes_in():
        arrive(plane_logs.at[0:depth - 1], log_recv)
        arrive(plane_sums.at[0:depth - 1], sum_recv)
        for j in range(gp):
            def one(i, carry):
                fwd, bwd = carry
                back = depth - 1 - i
                fwd = jnp.where(
                    i < z, jnp.exp(plane_logs[i, j][0:1, :]) * fwd + plane_sums[i, j].astype(F32), fwd)
                bwd = jnp.where(
                    back > z, jnp.exp(plane_logs[back, j][0:1, :]) * bwd + plane_sums[back, j].astype(F32), bwd)
                return fwd, bwd

            start = jnp.zeros((hd, lanes), F32)
            reached = lax.fori_loop(0, depth, one, (start, start), unroll=True if depth <= 4 else 1)
            for t in range(PLANE):
                vp = t * gp + j
                for d in range(2):
                    entering[d, vp] = before[d, vp] + decays_t[1 + d, vp][0:1, :] * reached[d]

    def channels(j):
        return pl.ds(pl.multiple_of(q * gw + j * lanes, lanes), lanes)

    def local_mix(t):
        def one(j, carry):
            vp = t * gp + j
            span = span_of(vp)
            r, k, v = proj[0, :, span], proj[1, :, span], proj[2, :, span]
            outs = []
            for s in range(2):
                rs = jnp.where(low if s == 0 else jnp.logical_not(low), r.astype(F32), 0.0).astype(BF16)
                scores = lax.dot_general(rs, k, contract_last, preferred_element_type=F32)
                weight = (scores * decay[2 * vp + s]).astype(BF16)
                outs.append(jnp.dot(weight, v, preferred_element_type=F32))
            own_term = halves(r.astype(F32) * credit_ref[:, channels(j)] * k.astype(F32)) * v.astype(F32)
            block[vp] = jnp.where(low, outs[0], outs[1]) + own_term
            return carry

        lax.fori_loop(0, gp, one, 0)

    def finish(t, dst, send=None):
        def one(j, carry):
            vp = t * gp + j
            span = span_of(vp)
            r = proj[0, :, span]
            fwd, bwd = [
                jnp.concatenate(
                    [jnp.where(low_u, entering[d, vp], 0.0), jnp.where(low_u, 0.0, entering[d, vp])], axis=0
                ).astype(BF16)
                for d in range(2)
            ]
            wkv = (
                block[vp]
                + spread_t[1, :, span] * jnp.dot(r, fwd, preferred_element_type=F32)
                + spread_t[0, :, span] * jnp.dot(r, bwd, preferred_element_type=F32)
            )
            centred = wkv - halves(wkv) * (1.0 / hd)
            variance = halves(centred * centred) * (1.0 / hd)
            normed = centred * lax.rsqrt(variance + 1e-05) * gain_ref[:, channels(j)]
            dst[t, j] = normed.astype(BF16)
            if send is not None:
                send(t, j)
            return carry

        lax.fori_loop(0, gp, one, 0, unroll=True)

    def finish_and_send(t):
        finish(t, sent, lambda t, j: remote(
            sent.at[t, j], landed.at[q, j], out_send, out_recv.at[q], {"row": base + t}).start())

    group = (
        (iota((count, count), 0) // (2 * tile_cols) == iota((count, count), 1) // (2 * tile_cols))
        & (iota((count, count), 0) % tile_cols // 2 == iota((count, count), 1) % tile_cols // 2)
    ).astype(BF16)

    def over_group(values):
        terms = []
        for value in values:
            terms.extend(two_terms(jnp.broadcast_to(jnp.sum(value, axis=1, keepdims=True), (count, lanes))))
        both = jnp.dot(group, jnp.concatenate(terms, axis=1), preferred_element_type=F32) * (1.0 / (4 * width))
        return [
            both[:, 2 * k * lanes:(2 * k + 1) * lanes] + both[:, (2 * k + 1) * lanes:(2 * k + 2) * lanes]
            for k in range(len(values))
        ]

    none = jnp.zeros((count, lanes), F32)

    def mean_of_x():
        total = none
        for i in range(vp_count):
            total = total + xt[q, :, i * lanes:(i + 1) * lanes].astype(F32)
        shift_t[...] = over_group([total])[0]

    def add_up(t, carry):
        def one(j, carry):
            first, second = carry
            i = t * gp + j
            made = xt[q, :, span_of(i)].astype(F32) - shift_t[...] + landed[t, j].astype(F32)
            block[i] = made
            return first + made, second + made * made

        return lax.fori_loop(0, gp, one, carry, unroll=True)

    for c in small[1:]:
        c.wait()

    far_sides_out()
    some_decays(0)
    x_copy.wait()
    mean_of_x()
    edges_in()
    some_decays(1)
    forward(0)
    forward(1)
    some_decays(2)
    forward(2)
    some_decays(3)
    forward(3)
    sides_out(q1)
    arrive(xt.at[q2], x_near)
    sides_out(q2)
    weights_from_z(KV, 0)
    weights_along_z(R, 1)
    mix(q, "own")
    mix(q1, "near")
    mix(q2, "near")
    weights_from_mate(KV, 0)
    keys_values(q)
    keys_values(q1)
    keys_values(q2)
    arrive(xt.at[q12], x_far)
    mix(q12, "far")
    keys_values(q12)
    planes_out()
    weights_from_z(R, 1)
    weights_from_mate(R, 1)
    project(0, q1)
    local_mix(q1)
    project(0, q2)
    local_mix(q2)
    planes_in()
    finish_and_send(q1)
    finish_and_send(q2)
    project(0, q12)
    local_mix(q12)
    finish_and_send(q12)
    project(0, q)
    local_mix(q)
    finish(q, landed)
    carry = add_up(q, (none, none))
    for t in (q1, q2, q12):
        arrive(landed.at[t], out_recv.at[t])
        carry = add_up(t, carry)

    mean, square = over_group(carry)
    stats[0] = mean
    stats[1] = lax.rsqrt(jnp.maximum(square - mean * mean, 0.0) + 1e-05)
    half_cols = tile_cols // 2
    outs = []
    for a in range(tile_rows // 2):
        def emit(i, carry):
            for part in range(4):
                span = pl.ds(pl.multiple_of(part * width + i * lanes, lanes), lanes)
                take = pl.ds((2 * a + part % 2) * tile_cols + part // 2, half_cols, stride=2)
                value = (block[i, take, :] - stats[0, take, :]) * stats[1, take, :]
                out_ref[a, :, span] = (value * scale_ref[:, span] + offset_ref[:, span]).astype(BF16)
            return carry

        lax.fori_loop(0, vp_count, emit, 0, unroll=4)

    left_by(xt.at[0:3], x_send)
    left_by(wf.at[:, z, 0:PLANE - 1, half], w_send.at[0])
    left_by(wf.at[:, 0:depth - 1, :, half], w_send.at[1])
    left_by(wf.at[:, :, :, half], w_send.at[2])
    left_by(rets.at[0:PLANE - 1], ret_send)
    left_by(plane_logs.at[0:depth - 1], log_send)
    left_by(plane_sums.at[0:depth - 1], sum_send)
    left_by(sent.at[0:PLANE - 1], out_send)
    edges(lambda c: c.wait_send())
    for t in (q, q1, q2):
        for c in side_copies(t, xt.at[t]):
            c.wait_send()
    left_by(side_out, far_send)
    for c in outs:
        c.wait()


def body(x, ratios, w, retention, credit, gain, scale, offset):
    tile_rows, tile_cols, width = x.shape
    heads = retention.shape[0]
    count = tile_rows * tile_cols
    hd = width // heads
    rows, cols = lax.axis_size("row"), lax.axis_size("col")
    depth = rows // PLANE
    pairs = heads // 2
    lanes = 2 * hd
    gw = width // PLANE
    gp = gw // lanes
    dma = pltpu.SemaphoreType.DMA
    anywhere = pl.BlockSpec(memory_space=pl.ANY)
    return pl.pallas_call(
        functools.partial(kernel, rows, cols, tile_rows, tile_cols, heads),
        out_shape=jax.ShapeDtypeStruct((tile_rows // 2, tile_cols // 2, 4 * width), BF16),
        in_specs=[anywhere] * 8,
        out_specs=pl.BlockSpec(memory_space=pltpu.VMEM),
        scratch_shapes=[
            pltpu.VMEM((3, width), F32),
            pltpu.VMEM((heads, tile_rows, tile_cols), F32),
            pltpu.VMEM((1, width), F32),
            pltpu.VMEM((1, width), F32),
            pltpu.VMEM((1, 4 * width), F32),
            pltpu.VMEM((1, 4 * width), F32),
            pltpu.VMEM((count, lanes), F32),
            pltpu.VMEM((PLANE, count, width), BF16),
            pltpu.VMEM((3, depth, PLANE, 2, w.shape[1] // 2, gw), BF16),
            pltpu.VMEM((PLANE, 3, count, width), BF16),
            pltpu.VMEM((3, count, width), BF16),
            pltpu.VMEM((heads, count, count), F32),
            pltpu.VMEM((PLANE, 2, count, width // 4), BF16),
            pltpu.VMEM((2, tile_rows, width // 4), BF16),
            pltpu.VMEM((2, tile_rows, width // 4), BF16),
            pltpu.VMEM((PLANE, tile_cols, width // 4), BF16),
            pltpu.VMEM((PLANE, tile_cols, width // 4), BF16),
            pltpu.VMEM((PLANE, 8, count), F32),
            pltpu.VMEM((PLANE, 8, count), F32),
            pltpu.VMEM((2, count, heads), F32),
            pltpu.VMEM((2, heads, count), F32),
            pltpu.VMEM((2, count, width), F32),
            pltpu.VMEM((8, width), F32),
            pltpu.VMEM((gp, 8, lanes), F32),
            pltpu.VMEM((depth, gp, 8, lanes), F32),
            pltpu.VMEM((2, pairs, hd, lanes), F32),
            pltpu.VMEM((2, pairs, hd, lanes), F32),
            pltpu.VMEM((3, pairs, 8, lanes), F32),
            pltpu.VMEM((2, gp, hd, lanes), BF16),
            pltpu.VMEM((depth, gp, hd, lanes), BF16),
            pltpu.VMEM((2, pairs, hd, lanes), F32),
            pltpu.VMEM((pairs, count, lanes), F32),
            pltpu.VMEM((PLANE, gp, count, lanes), BF16),
            pltpu.VMEM((PLANE, gp, count, lanes), BF16),
            pltpu.VMEM((2, count, lanes), F32),
            dma((6,)),
            dma, dma, dma((PIECES,)), dma, dma,
            dma, dma((3,)), dma((2,)), dma((2, depth)), dma((2,)),
            dma((PLANE, 2)), dma((PLANE, 2)), dma, dma,
            dma((2, PLANE)), dma((2, PLANE)),
            dma, dma, dma, dma, dma, dma, dma, dma((PLANE,)),
        ],
        compiler_params=pltpu.CompilerParams(
            collective_id=0, has_side_effects=True, vmem_limit_bytes=40 * 1024 * 1024),
    )(*[
        pltpu.with_memory_space_constraint(value, pltpu.MemorySpace.HBM)
        for value in (
            x.reshape(count, width), ratios, w, retention,
            credit.reshape(1, width), gain.reshape(1, width),
            scale.reshape(1, 4 * width), offset.reshape(1, 4 * width))
    ])


def solution(mesh):
    return jax.shard_map(
        body,
        mesh=mesh,
        in_specs=(
            P("row", "col", None),
            P(),
            P(None, "row", None),
            P(None, "row", "col"),
            P(),
            P(),
            P(),
            P(),
        ),
        out_specs=P("row", "col", None),
        check_vma=False,
    )
```

```python
import functools

import jax
import jax.numpy as jnp
from jax import lax
from jax.experimental import pallas as pl
from jax.experimental.pallas import tpu as pltpu
from jax.sharding import PartitionSpec as P

MESH = pl.DeviceIdType.MESH
F32 = jnp.float32
BF16 = jnp.bfloat16
HIGH = lax.Precision.HIGHEST
PLANE = 4
PIECES = 4
KV, R = slice(1, 3), slice(0, 1)


def iota(shape, dim):
    return lax.broadcasted_iota(jnp.int32, shape, dim)


def two_terms(value):
    first = value.astype(BF16)
    return first, (value - first.astype(F32)).astype(BF16)


def kernel(
    rows, cols, tile_rows, tile_cols, heads,
    x_ref, ratio_hbm, w_hbm, ret_hbm, credit_hbm, gain_hbm, scale_hbm, offset_hbm,
    out_ref,
    ratio_ref, ret_ref, credit_ref, gain_ref, scale_ref, offset_ref, w_ref, shift_t,
    xt, wf, mx, proj, decay, side, side_out, side_far, top_rows, bottom_rows, ret_out, rets, rows_t, rows_r, spread_t, log_t, plane_log, plane_logs,
    sums, before, decays_t, plane_sum, plane_sums, entering, block, sent, landed, stats,
    small_in, x_own, x_send, x_piece, x_near, x_far, w_own, w_send, w_plane, w_z, w_mate, side_send, side_recv, far_send, far_recv,
    edge_send, edge_recv, ret_send, ret_recv, log_send, log_recv, sum_send, sum_recv, out_send, out_recv,
):
    count, width = xt.shape[1:]
    hd = width // heads
    lanes = 2 * hd
    quarter = width // 4
    gw = width // PLANE
    gp = gw // lanes
    hp = heads // PLANE
    vp_count = PLANE * gp
    hs = w_ref.shape[1] // 2
    piece = count // PIECES
    row, col = lax.axis_index("row"), lax.axis_index("col")
    depth = rows // PLANE
    z, q = row // PLANE, row % PLANE
    bx, by = q % 2, q // 2
    half = col % 2
    mate = col + 1 - 2 * half
    q1 = (1 - half) * (q + 1 - 2 * bx) + half * (q + 2 - 4 * by)
    q2 = half * (q + 1 - 2 * bx) + (1 - half) * (q + 2 - 4 * by)
    q12 = PLANE - 1 - q
    base = z * PLANE
    first_row, second_row = base + q1, base + q2
    right, left = (col + 1) % cols, (col + cols - 1) % cols
    down_slot, up_slot = (q + 1) % PLANE, (q + PLANE - 1) % PLANE

    barrier = pltpu.get_barrier_semaphore()

    def greet(target):
        pl.semaphore_signal(barrier, inc=1, device_id=target, device_id_type=MESH)

    for o in range(1, depth):
        greet({"row": (z + o) % depth * PLANE + q})
    for o in range(1, PLANE):
        greet({"row": base + (q + o) % PLANE})
    for other in (right, left, mate):
        greet({"col": other})

    @pl.when(z > 0)
    def _():
        greet({"row": (base + rows - 1) % rows})

    @pl.when(z < depth - 1)
    def _():
        greet({"row": (base + PLANE) % rows})

    def local(src, dst, sem):
        return pltpu.make_async_copy(src, dst, sem)

    def remote(src, dst, send, recv, target):
        return pltpu.make_async_remote_copy(
            src, dst, send, recv, device_id=target, device_id_type=MESH)

    def arrive(ref, recv):
        remote(ref, ref, x_send, recv, {"col": mate}).wait_recv()

    def left_by(ref, send):
        remote(ref, ref, send, x_near, {"col": mate}).wait_send()

    my_rows = pl.ds(pl.multiple_of(half * hs, hs), hs)

    def my_cols(qq):
        return pl.ds(pl.multiple_of(qq * gw, gw), gw)

    small = [
        local(src, dst, small_in.at[k])
        for k, (src, dst) in enumerate((
            (ret_hbm, ret_ref), (ratio_hbm, ratio_ref), (credit_hbm, credit_ref), (gain_hbm, gain_ref),
            (scale_hbm, scale_ref), (offset_hbm, offset_ref), (w_hbm, w_ref)))
    ]
    for c in small:
        c.start()
    x_copy = local(x_ref, xt.at[q], x_own)
    w_copy = local(w_ref.at[:, my_rows, my_cols(q)], wf.at[:, z, q, half], w_own)
    x_copy.start()
    top_source = x_ref.at[count - tile_cols:count, 2 * quarter:3 * quarter]
    bottom_source = x_ref.at[0:tile_cols, 3 * quarter:]
    small[0].wait()
    own_ret = jnp.concatenate([ret_ref[:, r, :] for r in range(tile_rows)], axis=1)
    for qq in range(PLANE):
        ret_out[qq, 0:hp] = own_ret[qq * hp:(qq + 1) * hp]

    expected = (
        depth + PLANE + 1
        + PLANE * ((q == PLANE - 1) & (z < depth - 1)).astype(jnp.int32)
        + PLANE * ((q == 0) & (z > 0)).astype(jnp.int32)
    )
    pl.semaphore_wait(barrier, expected)

    x_copy.wait()
    small[6].wait()
    w_copy.start()

    def weights_to_plane(which, k):
        for o in range(1, PLANE):
            qq = (q + o) % PLANE
            remote(
                w_ref.at[which, my_rows, my_cols(qq)], wf.at[which, z, q, half], w_send.at[0], w_plane.at[k],
                {"row": base + qq}).start()

    def side_copies(t, source):
        return [
            remote(source.at[:, 0:quarter], side.at[t, 0], side_send.at[t, 0], side_recv.at[t, 0], {"col": right}),
            remote(source.at[:, quarter:2 * quarter], side.at[t, 1], side_send.at[t, 1], side_recv.at[t, 1],
                   {"col": left}),
        ]

    def edges(act):
        @pl.when(q < PLANE - 1)
        def _():
            act(remote(top_source, top_rows.at[down_slot], edge_send.at[0, 0], edge_recv.at[0, down_slot],
                       {"row": base + q12}))

        @pl.when(q > 0)
        def _():
            act(remote(bottom_source, bottom_rows.at[up_slot], edge_send.at[1, 0], edge_recv.at[1, up_slot],
                       {"row": base + q12}))

        for qq in range(PLANE):
            @pl.when((q == PLANE - 1) & (z < depth - 1))
            def _():
                act(remote(top_source, top_rows.at[down_slot], edge_send.at[0, qq], edge_recv.at[0, down_slot],
                           {"row": (base + PLANE + qq) % rows}))

            @pl.when((q == 0) & (z > 0))
            def _():
                act(remote(bottom_source, bottom_rows.at[up_slot], edge_send.at[1, qq], edge_recv.at[1, up_slot],
                           {"row": (base + rows - PLANE + qq) % rows}))

    weights_to_plane(KV, 0)
    for o in range(1, PLANE):
        qq = (q + o) % PLANE
        remote(ret_out.at[qq], rets.at[q], ret_send, ret_recv, {"row": base + qq}).start()
    edges(lambda c: c.start())
    for c in side_copies(q, x_ref):
        c.start()
    for k in range(PIECES):
        part = slice(k * piece, (k + 1) * piece)
        remote(xt.at[q, part], xt.at[q, part], x_send, x_piece.at[k], {"row": first_row}).start()
    weights_to_plane(R, 1)

    def weights_to_mate(which, k, zz):
        here = wf.at[which, zz, :, half]
        remote(here, here, w_send.at[2], w_mate.at[k], {"col": mate}).start()

    def weights_along_z(which, k):
        arrive(wf.at[which, z, 0:PLANE - 1, half], w_plane.at[k])
        here = wf.at[which, z, :, half]
        for o in range(1, depth):
            remote(here, here, w_send.at[1], w_z.at[k, z], {"row": (z + o) % depth * PLANE + q}).start()
        weights_to_mate(which, k, z)

    def weights_from_z(which, k):
        for o in range(1, depth):
            zz = (z + o) % depth
            arrive(wf.at[which, zz, :, half], w_z.at[k, zz])
            weights_to_mate(which, k, zz)

    def weights_from_mate(which, k):
        arrive(wf.at[which, :, :, 1 - half], w_mate.at[k])

    w_copy.wait()
    weights_along_z(KV, 0)

    arrive(rets.at[0:PLANE - 1], ret_recv)
    remote(xt.at[q], xt.at[q], x_send, x_near, {"row": second_row}).start()
    rets[q] = ret_out[q]
    ret = jnp.concatenate([rets[t, 0:hp] for t in range(PLANE)], axis=0)
    tri = (iota((count, count), 0) >= iota((count, count), 1)).astype(F32)
    contract_last = (((1,), (1,)), ((), ()))
    running_c = lax.dot_general(tri, ret, contract_last, precision=HIGH, preferred_element_type=F32)
    running_r = lax.dot_general(ret, tri, contract_last, precision=HIGH, preferred_element_type=F32)
    eye = (iota((count, count), 0) == iota((count, count), 1)).astype(F32)
    ret_c = lax.dot_general(eye, ret, contract_last, precision=HIGH, preferred_element_type=F32)
    before_c = running_c - ret_c
    total_r = running_c[count - 1:count, :]
    rows_t[0] = running_c
    rows_t[1] = before_c
    rows_r[0] = running_r
    rows_r[1] = running_r - ret
    chosen = (iota((heads, width), 0) == iota((heads, width), 1) // hd).astype(F32)
    for k, table in enumerate((jnp.exp(total_r - running_c), jnp.exp(before_c))):
        spread_t[k] = jnp.dot(table, chosen, precision=HIGH, preferred_element_type=F32)
    log_t[...] = jnp.dot(jnp.broadcast_to(total_r, (8, heads)), chosen, precision=HIGH, preferred_element_type=F32)

    def log_of(vp):
        return log_t[:, vp * lanes:(vp + 1) * lanes]

    for j in range(gp):
        plane_log[j] = sum(log_of(t * gp + j) for t in range(PLANE))
    for o in range(1, depth):
        remote(plane_log, plane_logs.at[z], log_send, log_recv, {"row": (z + o) % depth * PLANE + q}).start()
    for j in range(gp):
        for t in range(PLANE):
            vp = t * gp + j
            zero = jnp.zeros((8, lanes), F32)
            decays_t[0, vp] = jnp.exp(log_of(vp))
            decays_t[1, vp] = jnp.exp(sum((log_of(s * gp + j) for s in range(t)), zero))
            decays_t[2, vp] = jnp.exp(sum((log_of(s * gp + j) for s in range(t + 1, PLANE)), zero))

    def picked(table, h):
        return jnp.sum(jnp.where(iota(table.shape, 1) == h, table, 0.0), axis=1, keepdims=True)

    def picked_row(table, h):
        return jnp.sum(jnp.where(iota(table.shape, 0) == h, table, 0.0), axis=0, keepdims=True)

    earlier = iota((count, count), 0) > iota((count, count), 1)
    diagonal = iota((count, count), 0) == iota((count, count), 1)

    def pair_decays(h, carry):
        rc, bc = picked(rows_t[0], h), picked(rows_t[1], h)
        rr, br = picked_row(rows_r[0], h), picked_row(rows_r[1], h)
        exponent = jnp.where(earlier, bc - rr, br - rc)
        decay[h] = jnp.where(diagonal, 0.0, jnp.exp(exponent))
        return carry

    def some_decays(part):
        lax.fori_loop(part * heads // 4, (part + 1) * heads // 4, pair_decays, 0)

    def forward(k):
        part = slice(k * piece, (k + 1) * piece)
        here = xt.at[q1, part]
        arrive(here, x_piece.at[k])
        remote(here, here, x_send, x_far, {"row": second_row}).start()

    def sides_out(t):
        for c in side_copies(t, xt.at[t]):
            c.start()

    def edges_in():
        @pl.when(z > 0)
        def _():
            arrive(top_rows.at[0], edge_recv.at[0, 0])

        @pl.when(z < depth - 1)
        def _():
            arrive(bottom_rows.at[PLANE - 1], edge_recv.at[1, PLANE - 1])

        @pl.when(q12 < PLANE - 1)
        def _():
            arrive(top_rows.at[0], edge_recv.at[0, (q12 + 1) % PLANE])

        @pl.when(q12 > 0)
        def _():
            arrive(bottom_rows.at[0], edge_recv.at[1, (q12 + PLANE - 1) % PLANE])

    place_in_row = iota((count, quarter), 0) % tile_cols
    last = tile_cols - 1

    def far_sides_out():
        for c in side_copies(q, x_ref):
            c.wait_recv()
        token, line = iota((tile_rows, count), 1), iota((tile_rows, count), 0) * tile_cols
        for k in range(2):
            pick = (token == line + (last if k == 0 else 0)).astype(BF16)
            side_out[k] = jnp.dot(pick, side[q, k], preferred_element_type=F32).astype(BF16)
        remote(side_out, side_far, far_send, far_recv, {"row": base + q12}).start()

    def mix(t, kind):
        x0 = xt[t, :, 0:quarter].astype(F32)
        x1 = xt[t, :, quarter:2 * quarter].astype(F32)
        if kind == "far":
            arrive(side_far, far_recv)
            token, line = iota((count, tile_rows), 0), iota((count, tile_rows), 1) * tile_cols
            side0, side1 = [
                jnp.dot((token == line + (0 if k == 0 else last)).astype(BF16), side_far[k],
                        preferred_element_type=F32)
                for k in range(2)
            ]
        else:
            if kind == "near":
                for c in side_copies(t, xt.at[t]):
                    c.wait_recv()
            side0 = pltpu.roll(side[t, 0].astype(F32), count - last, 0)
            side1 = pltpu.roll(side[t, 1].astype(F32), last, 0)
        side0 = jnp.where(col > 0, side0, 0.0)
        side1 = jnp.where(col < cols - 1, side1, 0.0)
        up_t, down_t = (t + PLANE - 1) % PLANE, (t + 1) % PLANE
        up_sent, down_sent = (t == 0) | (up_t == q12), (t == PLANE - 1) | (down_t == q12)
        up_t, down_t = jnp.where(up_sent, t, up_t), jnp.where(down_sent, t, down_t)
        above = xt[up_t, count - tile_cols:count, 2 * quarter:3 * quarter].astype(F32)
        below = xt[down_t, 0:tile_cols, 3 * quarter:].astype(F32)
        top = jnp.where(base + t > 0, jnp.where(up_sent, top_rows[t].astype(F32), above), 0.0)
        bottom = jnp.where(base + t < rows - 1, jnp.where(down_sent, bottom_rows[t].astype(F32), below), 0.0)
        shifted = [
            jnp.where(place_in_row == 0, side0, pltpu.roll(x0, 1, 0)),
            jnp.where(place_in_row == last, side1, pltpu.roll(x1, count - 1, 0)),
            jnp.concatenate([top, xt[t, 0:count - tile_cols, 2 * quarter:3 * quarter].astype(F32)], axis=0),
            jnp.concatenate([xt[t, tile_cols:count, 3 * quarter:].astype(F32), bottom], axis=0),
        ]
        for part in range(4):
            span = slice(part * quarter, (part + 1) * quarter)
            xs = xt[t, :, span].astype(F32)
            for p in range(3):
                c = ratio_ref[p:p + 1, span]
                mx[t, p, :, span] = (xs * c + shifted[part] * (1.0 - c)).astype(BF16)

    def project(p, t):
        proj[p, :, my_cols(t)] = jnp.dot(
            mx[t, p], wf[p].reshape(width, gw), preferred_element_type=F32).astype(BF16)

    low = iota((count, lanes), 1) < hd
    low_u = iota((hd, lanes), 1) < hd
    same_head = (iota((2 * lanes, lanes), 0) % lanes // hd == iota((2 * lanes, lanes), 1) // hd).astype(BF16)

    def halves(value):
        return jnp.dot(jnp.concatenate(two_terms(value), axis=1), same_head, preferred_element_type=F32)

    def span_of(i):
        return pl.ds(pl.multiple_of(i * lanes, lanes), lanes)

    def local_states(t):
        def one(j, carry):
            vp = t * gp + j
            span = span_of(vp)
            k = proj[1, :, span].astype(F32)
            v = proj[2, :, span]
            kd = jnp.concatenate([k * spread_t[0, :, span], k * spread_t[1, :, span]], axis=1).astype(BF16)
            m = lax.dot_general(kd, v, (((0,), (0,)), ((), ())), preferred_element_type=F32)
            sums[0, vp] = jnp.where(low_u, m[0:hd], m[hd:2 * hd])
            sums[1, vp] = jnp.where(low_u, m[2 * hd:3 * hd], m[3 * hd:])
            return carry

        lax.fori_loop(0, gp, one, 0, unroll=True)

    def keys_values(t):
        project(1, t)
        project(2, t)
        local_states(t)

    def planes_out():
        for j in range(gp):
            for d, order in ((0, range(PLANE)), (1, range(PLANE - 1, -1, -1))):
                state = jnp.zeros((hd, lanes), F32)
                for t in order:
                    vp = t * gp + j
                    before[d, vp] = state
                    state = decays_t[0, vp][0:1, :] * state + sums[d, vp]
                plane_sum[d, j] = state.astype(BF16)
        for o in range(1, depth):
            zz = (z + o) % depth
            remote(
                plane_sum.at[(zz < z).astype(jnp.int32)], plane_sums.at[z], sum_send, sum_recv,
                {"row": zz * PLANE + q}).start()

    def planes_in():
        arrive(plane_logs.at[0:depth - 1], log_recv)
        arrive(plane_sums.at[0:depth - 1], sum_recv)
        for j in range(gp):
            def one(i, carry):
                fwd, bwd = carry
                back = depth - 1 - i
                fwd = jnp.where(
                    i < z, jnp.exp(plane_logs[i, j][0:1, :]) * fwd + plane_sums[i, j].astype(F32), fwd)
                bwd = jnp.where(
                    back > z, jnp.exp(plane_logs[back, j][0:1, :]) * bwd + plane_sums[back, j].astype(F32), bwd)
                return fwd, bwd

            start = jnp.zeros((hd, lanes), F32)
            reached = lax.fori_loop(0, depth, one, (start, start), unroll=True if depth <= 4 else 1)
            for t in range(PLANE):
                vp = t * gp + j
                for d in range(2):
                    entering[d, vp] = before[d, vp] + decays_t[1 + d, vp][0:1, :] * reached[d]

    def channels(j):
        return pl.ds(pl.multiple_of(q * gw + j * lanes, lanes), lanes)

    def local_mix(t):
        def one(j, carry):
            vp = t * gp + j
            span = span_of(vp)
            r, k, v = proj[0, :, span], proj[1, :, span], proj[2, :, span]
            outs = []
            for s in range(2):
                rs = jnp.where(low if s == 0 else jnp.logical_not(low), r.astype(F32), 0.0).astype(BF16)
                scores = lax.dot_general(rs, k, contract_last, preferred_element_type=F32)
                weight = (scores * decay[2 * vp + s]).astype(BF16)
                outs.append(jnp.dot(weight, v, preferred_element_type=F32))
            own_term = halves(r.astype(F32) * credit_ref[:, channels(j)] * k.astype(F32)) * v.astype(F32)
            block[vp] = jnp.where(low, outs[0], outs[1]) + own_term
            return carry

        lax.fori_loop(0, gp, one, 0)

    def finish(t, dst, send=None):
        def one(j, carry):
            vp = t * gp + j
            span = span_of(vp)
            r = proj[0, :, span]
            fwd, bwd = [
                jnp.concatenate(
                    [jnp.where(low_u, entering[d, vp], 0.0), jnp.where(low_u, 0.0, entering[d, vp])], axis=0
                ).astype(BF16)
                for d in range(2)
            ]
            wkv = (
                block[vp]
                + spread_t[1, :, span] * jnp.dot(r, fwd, preferred_element_type=F32)
                + spread_t[0, :, span] * jnp.dot(r, bwd, preferred_element_type=F32)
            )
            centred = wkv - halves(wkv) * (1.0 / hd)
            variance = halves(centred * centred) * (1.0 / hd)
            normed = centred * lax.rsqrt(variance + 1e-05) * gain_ref[:, channels(j)]
            dst[t, j] = normed.astype(BF16)
            if send is not None:
                send(t, j)
            return carry

        lax.fori_loop(0, gp, one, 0, unroll=True)

    def finish_and_send(t):
        finish(t, sent, lambda t, j: remote(
            sent.at[t, j], landed.at[q, j], out_send, out_recv.at[q], {"row": base + t}).start())

    group = (
        (iota((count, count), 0) // (2 * tile_cols) == iota((count, count), 1) // (2 * tile_cols))
        & (iota((count, count), 0) % tile_cols // 2 == iota((count, count), 1) % tile_cols // 2)
    ).astype(BF16)

    def over_group(values):
        terms = []
        for value in values:
            terms.extend(two_terms(jnp.broadcast_to(jnp.sum(value, axis=1, keepdims=True), (count, lanes))))
        both = jnp.dot(group, jnp.concatenate(terms, axis=1), preferred_element_type=F32) * (1.0 / (4 * width))
        return [
            both[:, 2 * k * lanes:(2 * k + 1) * lanes] + both[:, (2 * k + 1) * lanes:(2 * k + 2) * lanes]
            for k in range(len(values))
        ]

    none = jnp.zeros((count, lanes), F32)

    def mean_of_x():
        total = none
        for i in range(vp_count):
            total = total + xt[q, :, i * lanes:(i + 1) * lanes].astype(F32)
        shift_t[...] = over_group([total])[0]

    def add_up(t, carry):
        def one(j, carry):
            first, second = carry
            i = t * gp + j
            made = xt[q, :, span_of(i)].astype(F32) - shift_t[...] + landed[t, j].astype(F32)
            block[i] = made
            return first + made, second + made * made

        return lax.fori_loop(0, gp, one, carry, unroll=True)

    for c in small[1:6]:
        c.wait()

    far_sides_out()
    some_decays(0)
    mean_of_x()
    edges_in()
    some_decays(1)
    forward(0)
    forward(1)
    some_decays(2)
    forward(2)
    some_decays(3)
    forward(3)
    sides_out(q1)
    arrive(xt.at[q2], x_near)
    sides_out(q2)
    weights_from_z(KV, 0)
    weights_along_z(R, 1)
    mix(q, "own")
    mix(q1, "near")
    mix(q2, "near")
    weights_from_mate(KV, 0)
    keys_values(q)
    keys_values(q1)
    keys_values(q2)
    arrive(xt.at[q12], x_far)
    mix(q12, "far")
    keys_values(q12)
    planes_out()
    weights_from_z(R, 1)
    weights_from_mate(R, 1)
    project(0, q1)
    local_mix(q1)
    project(0, q2)
    local_mix(q2)
    planes_in()
    finish_and_send(q1)
    finish_and_send(q2)
    project(0, q12)
    local_mix(q12)
    finish_and_send(q12)
    project(0, q)
    local_mix(q)
    finish(q, landed)
    carry = add_up(q, (none, none))
    left_by(xt.at[0:3], x_send)
    left_by(wf.at[:, z, 0:PLANE - 1, half], w_send.at[0])
    left_by(wf.at[:, 0:depth - 1, :, half], w_send.at[1])
    left_by(wf.at[:, :, :, half], w_send.at[2])
    left_by(rets.at[0:PLANE - 1], ret_send)
    left_by(plane_logs.at[0:depth - 1], log_send)
    left_by(plane_sums.at[0:depth - 1], sum_send)
    edges(lambda c: c.wait_send())
    for t in (q, q1, q2):
        for c in side_copies(t, xt.at[t]):
            c.wait_send()
    left_by(side_out, far_send)
    for t in (q1, q2, q12):
        arrive(landed.at[t], out_recv.at[t])
        carry = add_up(t, carry)

    mean, square = over_group(carry)
    stats[0] = mean
    stats[1] = lax.rsqrt(jnp.maximum(square - mean * mean, 0.0) + 1e-05)
    half_cols = tile_cols // 2
    def emit(i, carry):
        for part in range(4):
            span = pl.ds(pl.multiple_of(part * width + i * lanes, lanes), lanes)
            gain, offset = scale_ref[:, span], offset_ref[:, span]
            for a in range(tile_rows // 2):
                take = pl.ds((2 * a + part % 2) * tile_cols + part // 2, half_cols, stride=2)
                value = (block[i, take, :] - stats[0, take, :]) * stats[1, take, :]
                out_ref[a, :, span] = (value * gain + offset).astype(BF16)
        return carry

    lax.fori_loop(0, vp_count, emit, 0)

    left_by(sent.at[0:PLANE - 1], out_send)


def body(x, ratios, w, retention, credit, gain, scale, offset):
    tile_rows, tile_cols, width = x.shape
    heads = retention.shape[0]
    count = tile_rows * tile_cols
    hd = width // heads
    rows, cols = lax.axis_size("row"), lax.axis_size("col")
    depth = rows // PLANE
    pairs = heads // 2
    lanes = 2 * hd
    gw = width // PLANE
    gp = gw // lanes
    dma = pltpu.SemaphoreType.DMA
    anywhere = pl.BlockSpec(memory_space=pl.ANY)
    return pl.pallas_call(
        functools.partial(kernel, rows, cols, tile_rows, tile_cols, heads),
        out_shape=jax.ShapeDtypeStruct((tile_rows // 2, tile_cols // 2, 4 * width), BF16),
        in_specs=[anywhere] * 8,
        out_specs=pl.BlockSpec(memory_space=pltpu.VMEM),
        scratch_shapes=[
            pltpu.VMEM((3, width), F32),
            pltpu.VMEM((heads, tile_rows, tile_cols), F32),
            pltpu.VMEM((1, width), F32),
            pltpu.VMEM((1, width), F32),
            pltpu.VMEM((1, 4 * width), F32),
            pltpu.VMEM((1, 4 * width), F32),
            pltpu.VMEM(w.shape, BF16),
            pltpu.VMEM((count, lanes), F32),
            pltpu.VMEM((PLANE, count, width), BF16),
            pltpu.VMEM((3, depth, PLANE, 2, w.shape[1] // 2, gw), BF16),
            pltpu.VMEM((PLANE, 3, count, width), BF16),
            pltpu.VMEM((3, count, width), BF16),
            pltpu.VMEM((heads, count, count), F32),
            pltpu.VMEM((PLANE, 2, count, width // 4), BF16),
            pltpu.VMEM((2, tile_rows, width // 4), BF16),
            pltpu.VMEM((2, tile_rows, width // 4), BF16),
            pltpu.VMEM((PLANE, tile_cols, width // 4), BF16),
            pltpu.VMEM((PLANE, tile_cols, width // 4), BF16),
            pltpu.VMEM((PLANE, 8, count), F32),
            pltpu.VMEM((PLANE, 8, count), F32),
            pltpu.VMEM((2, count, heads), F32),
            pltpu.VMEM((2, heads, count), F32),
            pltpu.VMEM((2, count, width), F32),
            pltpu.VMEM((8, width), F32),
            pltpu.VMEM((gp, 8, lanes), F32),
            pltpu.VMEM((depth, gp, 8, lanes), F32),
            pltpu.VMEM((2, pairs, hd, lanes), F32),
            pltpu.VMEM((2, pairs, hd, lanes), F32),
            pltpu.VMEM((3, pairs, 8, lanes), F32),
            pltpu.VMEM((2, gp, hd, lanes), BF16),
            pltpu.VMEM((depth, gp, hd, lanes), BF16),
            pltpu.VMEM((2, pairs, hd, lanes), F32),
            pltpu.VMEM((pairs, count, lanes), F32),
            pltpu.VMEM((PLANE, gp, count, lanes), BF16),
            pltpu.VMEM((PLANE, gp, count, lanes), BF16),
            pltpu.VMEM((2, count, lanes), F32),
            dma((7,)),
            dma, dma, dma((PIECES,)), dma, dma,
            dma, dma((3,)), dma((2,)), dma((2, depth)), dma((2,)),
            dma((PLANE, 2)), dma((PLANE, 2)), dma, dma,
            dma((2, PLANE)), dma((2, PLANE)),
            dma, dma, dma, dma, dma, dma, dma, dma((PLANE,)),
        ],
        compiler_params=pltpu.CompilerParams(
            collective_id=0, has_side_effects=True, vmem_limit_bytes=40 * 1024 * 1024),
    )(*[
        pltpu.with_memory_space_constraint(value, pltpu.MemorySpace.HBM)
        for value in (
            x.reshape(count, width), ratios, w, retention,
            credit.reshape(1, width), gain.reshape(1, width),
            scale.reshape(1, 4 * width), offset.reshape(1, 4 * width))
    ])


def solution(mesh):
    return jax.shard_map(
        body,
        mesh=mesh,
        in_specs=(
            P("row", "col", None),
            P(),
            P(None, "row", None),
            P(None, "row", "col"),
            P(),
            P(),
            P(),
            P(),
        ),
        out_specs=P("row", "col", None),
        check_vma=False,
    )
```
